32 devices in a mesh: fsdp: 16 (over z, y, core), tensor: 2 (over x).
Axes of the slice: x: 2, y: 2, z: 4, core: 2. Of those that a mesh axis runs over, the one named last changes fastest.
Arguments:
- tokens: bfloat16 [32, 1024, 1024], P('fsdp', 'tensor'), may hold values from -6 to 6
- cotangent: bfloat16 [32, 1024, 1024], P('fsdp', 'tensor'), may hold values from -8 to 8
- w_qkv: bfloat16 [1024, 3, 1024], P('fsdp', None, 'tensor'), may hold values from -0.1875 to 0.1875
- wo_t: bfloat16 [1024, 1024], P('fsdp', 'tensor'), may hold values from -1.5 to 1.5
- w_up: bfloat16 [1024, 4096], P('fsdp', 'tensor'), may hold values from -0.1875 to 0.1875
- w_down_t: bfloat16 [1024, 4096], P('fsdp', 'tensor'), may hold values from -0.09375 to 0.09375
- norm_gains: bfloat16 [1024, 2], P('fsdp'), may hold values from 0.5 to 1.5
- norm_shifts: bfloat16 [1024, 2], P('fsdp'), may hold values from -1.796875 to 1.796875
- qk_gains: bfloat16 [2, 64], replicated, may hold values from 0.5 to 1.5
Outputs:
- outputs: bfloat16 [32, 1024, 1024], P('fsdp', 'tensor')
- grad_tokens: float32 [32, 1024, 1024], P('fsdp', 'tensor')
- grad_w_qkv: float32 [1024, 3, 1024], P('fsdp', None, 'tensor')
- grad_wo_t: float32 [1024, 1024], P('fsdp', 'tensor')
- grad_w_up: float32 [1024, 4096], P('fsdp', 'tensor')
- grad_w_down_t: float32 [1024, 4096], P('fsdp', 'tensor')
- grad_norm_gains: float32 [1024, 2], P('fsdp')
- grad_norm_shifts: float32 [1024, 2], P('fsdp')
- grad_qk_gains: float32 [2, 64], replicated
The draws below stay inside these ranges and needn't reach their ends.
All inputs are finite; a program needn't handle non-finite values.
Results may differ from the reference program's by a relative error of at most 0.015.
Values may be sent and summed in bfloat16 or wider, within the bound.
A program may use at most 256 MiB of HBM per device.

```python
import jax
import jax.numpy as jnp
from jax import lax

D = 1024
HEADS = 16
HD = 64
FF = 4096
LEN = 1024
IMAGES = 32


def draw_cotangent(key, part):
    place = jnp.arange(IMAGES, dtype=jnp.float32)[:, None, None]
    ramp = 3.0 ** (place / max(IMAGES - 1, 1))
    value = jnp.clip(jax.random.normal(key, (IMAGES, LEN, D), jnp.float32), -4.0, 4.0) * ramp
    return (value / 1.5).astype(jnp.bfloat16)


def levels(rng, extent, shards, smallest, high):
    def one(dim, blocks):
        draws = jax.random.uniform(jax.random.fold_in(jax.random.fold_in(rng, 6), dim), (blocks,), jnp.float32, smallest / len(shards), high / len(shards))
        return jnp.repeat(jnp.exp(draws), extent[dim] // blocks).reshape((-1,) + (1,) * (len(extent) - dim - 1))

    loudness = one(*shards[0])
    for cut in shards[1:]:
        loudness = loudness * one(*cut)
    return loudness


def scatter_about(stream_key, dims, scale, reach, split=(), kind=jnp.bfloat16):
    values = jax.random.normal(stream_key, dims, jnp.float32) * scale
    if len(split) > 0:
        values = levels(stream_key, dims, split, -0.22, 0.18) * values
    return jnp.clip(values, min=-reach, max=reach).astype(kind)


def setup_inputs(seed: int = 0) -> dict:
    seeds = jax.random.split(jax.random.key(seed), 10)
    return {
        "tokens": scatter_about(seeds[0], (IMAGES, LEN, D), 1.0, 6.0, ((0, 16), (1, 2))),
        "cotangent": draw_cotangent(jax.random.fold_in(seeds[9], 71), 0),
        "w_qkv": scatter_about(seeds[2], (D, 3, D), D ** -0.5, 0.1875, ((0, 16), (2, 2))),
        "wo_t": scatter_about(seeds[3], (D, D), (max(D // 64, 4)) ** -0.5, 1.5, ((0, 16), (1, 2))),
        "w_up": scatter_about(seeds[4], (D, FF), D ** -0.5, 0.1875, ((0, 16), (1, 2))),
        "w_down_t": scatter_about(seeds[5], (D, FF), FF ** -0.5, 0.09375, ((0, 16), (1, 2))),
        "norm_gains": jnp.clip(1.0 + 0.1 * jax.random.normal(seeds[6], (D, 2), jnp.float32), 0.5, 1.5).astype(jnp.bfloat16),
        "norm_shifts": scatter_about(seeds[7], (D, 2), 0.3, 1.796875, ((0, 16),)),
        "qk_gains": jnp.clip(1.0 + 0.1 * jax.random.normal(seeds[8], (2, HD), jnp.float32), 0.5, 1.5).astype(jnp.bfloat16),
    }


@jax.custom_vjp
def low(v):
    return lax.optimization_barrier(v.astype(jnp.bfloat16)).astype(jnp.float32)

@jax.custom_vjp
def low_back(v):
    return v

def low_keep(v):
    return (low(v), None)

def low_pass(kept, grad):
    return (grad,)

def back_keep(v):
    return (v, None)

def back_low(kept, grad):
    return (low(grad),)
low.defvjp(low_keep, low_pass)
low_back.defvjp(back_keep, back_low)
EPSILON = 1e-06
HIGHEST = lax.Precision.HIGHEST

def normalize(value):
    center = value - lax.optimization_barrier(jnp.mean(value, -1, keepdims=True))
    return center * lax.rsqrt(lax.optimization_barrier(jnp.mean(center * center, -1, keepdims=True)) + EPSILON)

def block_forward(inputs, w_qkv, wo_t, w_up, w_down_t, norm_gains, norm_shifts, qk_gains):
    first = low(normalize(inputs) * norm_gains[:, 0] + norm_shifts[:, 0])
    joined = jnp.dot(first, w_qkv.reshape(D, 3 * D), precision=HIGHEST).reshape(LEN, 3, HEADS, HD)
    query = low_back(joined[:, 0])
    keys = low_back(joined[:, 1])
    values = low(low_back(joined[:, 2]))
    query_n = low(normalize(query) * qk_gains[0] * HD ** (-0.5))
    keys_n = low(normalize(keys) * qk_gains[1])
    scores = low_back(jnp.einsum('qhd,khd->hqk', query_n, keys_n, precision=HIGHEST))
    largest = lax.optimization_barrier(jnp.max(scores, -1, keepdims=True))
    exponent = jnp.exp(scores - largest)
    probs = low(exponent / lax.optimization_barrier(jnp.sum(exponent, -1, keepdims=True)))
    mixed = low(low_back(jnp.einsum('hqk,khd->qhd', probs, values, precision=HIGHEST))).reshape(LEN, D)
    branch = low_back(jnp.dot(mixed, wo_t.T, precision=HIGHEST))
    middle = inputs + branch
    second = low(normalize(middle) * norm_gains[:, 1] + norm_shifts[:, 1])
    hidden = low_back(jnp.dot(second, w_up, precision=HIGHEST))
    active = low(jax.nn.gelu(hidden, approximate=False))
    return middle + jnp.dot(active, w_down_t.T, precision=HIGHEST)

def reference(tokens, cotangent, w_qkv, wo_t, w_up, w_down_t, norm_gains, norm_shifts, qk_gains):
    params = (w_qkv.astype(jnp.float32), wo_t.astype(jnp.float32), w_up.astype(jnp.float32), w_down_t.astype(jnp.float32), norm_gains.astype(jnp.float32), norm_shifts.astype(jnp.float32), qk_gains.astype(jnp.float32))

    def one_image(totals, item):
        image, grad_out = item
        result, pull = jax.vjp(block_forward, image, *params)
        grads = pull(grad_out)
        totals = tuple((total + part for total, part in zip(totals, grads[1:])))
        return (totals, (result.astype(jnp.bfloat16), grads[0]))
    start_sums = tuple((jnp.zeros(param.shape, jnp.float32) for param in params))
    totals, (outputs, grad_tokens) = lax.scan(one_image, start_sums, (tokens.astype(jnp.float32), cotangent.astype(jnp.float32)))
    return (outputs, grad_tokens, totals[0], totals[1], totals[2], totals[3], totals[4], totals[5], totals[6])
```

```python
import jax
import jax.numpy as jnp
from jax import lax
from jax.sharding import PartitionSpec as P

HD = 64


EPSILON = 1e-06


def norm_stats(value):
    center = value - jnp.mean(value, -1, keepdims=True)
    factor = lax.rsqrt(jnp.mean(center * center, -1, keepdims=True) + EPSILON)
    return (center * factor, factor)


def norm_back(grad_hat, normed, factor):
    return factor * (
        grad_hat
        - jnp.mean(grad_hat, -1, keepdims=True)
        - normed * jnp.mean(grad_hat * normed, -1, keepdims=True)
    )


def contract_rows(left, right):
    return lax.dot_general(
        left, right, (((0,), (0,)), ((), ())), preferred_element_type=jnp.float32
    )


def contract_cols(left, right):
    return lax.dot_general(
        left, right, (((1,), (1,)), ((), ())), preferred_element_type=jnp.float32
    )


def per_device(tokens, cotangent, w_qkv, wo_t, w_up, w_down_t, norm_gains, norm_shifts, qk_gains):
    local_rows = tokens.shape[1]
    width = tokens.shape[2]
    head_cols = w_qkv.shape[2]
    local_heads = head_cols // HD
    hidden_cols = w_up.shape[1]
    tensor_count = lax.axis_size("tensor")
    full_len = local_rows * tensor_count
    block = min(512, full_len)
    blocks = full_len // block
    gain_query = qk_gains[0].astype(jnp.float32)
    gain_keys = qk_gains[1].astype(jnp.float32)
    scale_query = HD ** (-0.5)

    def fetch():
        return (
            lax.all_gather(w_qkv, "fsdp", axis=0, tiled=True),
            lax.all_gather(wo_t, "fsdp", axis=0, tiled=True),
            lax.all_gather(w_up, "fsdp", axis=0, tiled=True),
            lax.all_gather(w_down_t, "fsdp", axis=0, tiled=True),
            lax.all_gather(norm_gains, "fsdp", axis=0, tiled=True),
            lax.all_gather(norm_shifts, "fsdp", axis=0, tiled=True),
        )

    def forward(weights, inputs):
        whole_qkv, whole_out, whole_up, whole_down, gains, shifts = weights
        gains = gains.astype(jnp.float32)
        shifts = shifts.astype(jnp.float32)
        flat_qkv = whole_qkv.reshape(width, 3 * head_cols)
        residual = inputs.astype(jnp.float32)
        first_hat, first_factor = norm_stats(residual)
        first = (first_hat * gains[:, 0] + shifts[:, 0]).astype(jnp.bfloat16)
        piece = lax.all_gather(first, "tensor", axis=0, tiled=True)
        first_full = piece
        joined = jnp.dot(piece, flat_qkv, preferred_element_type=jnp.float32)
        joined = joined.reshape(full_len, 3, local_heads, HD)
        query_hat, query_factor = norm_stats(joined[:, 0])
        keys_hat, keys_factor = norm_stats(joined[:, 1])
        query_n = (query_hat * gain_query * scale_query).astype(jnp.bfloat16)
        keys_n = (keys_hat * gain_keys).astype(jnp.bfloat16)
        values = joined[:, 2].astype(jnp.bfloat16)

        def attend(query_block):
            scores = jnp.einsum(
                "qhd,khd->hqk", query_block, keys_n, preferred_element_type=jnp.float32
            )
            largest = jnp.max(scores, -1, keepdims=True)
            exponent = jnp.exp(scores - largest)
            total_sum = jnp.sum(exponent, -1, keepdims=True)
            probs_low = (exponent / total_sum).astype(jnp.bfloat16)
            mixed_block = jnp.einsum(
                "hqk,khd->qhd", probs_low, values, preferred_element_type=jnp.float32
            )
            return (mixed_block.astype(jnp.bfloat16), (largest + jnp.log(total_sum))[..., 0])

        mixed, log_total = lax.map(attend, query_n.reshape(blocks, block, local_heads, HD))
        mixed = mixed.reshape(full_len, head_cols)
        middle = residual + lax.psum_scatter(
            contract_cols(mixed, whole_out), "tensor", scatter_dimension=0, tiled=True
        )
        second_hat, second_factor = norm_stats(middle)
        second = (second_hat * gains[:, 1] + shifts[:, 1]).astype(jnp.bfloat16)
        piece = lax.all_gather(second, "tensor", axis=0, tiled=True)
        hidden = jnp.dot(piece, whole_up, preferred_element_type=jnp.float32)
        active = jax.nn.gelu(hidden, approximate=False).astype(jnp.bfloat16)
        result = (
            middle
            + lax.psum_scatter(
                contract_cols(active, whole_down).astype(jnp.bfloat16),
                "tensor",
                scatter_dimension=0,
                tiled=True,
            ).astype(jnp.float32)
        ).astype(jnp.bfloat16)
        kept = (
            first_hat,
            first_factor,
            first_full,
            query_hat,
            query_factor,
            keys_hat,
            keys_factor,
            query_n,
            keys_n,
            values,
            mixed,
            log_total,
            second_hat,
            second_factor,
            piece,
            hidden,
            active,
        )
        return (kept, result)

    def backward(weights, kept, grad_out):
        whole_qkv, whole_out, whole_up, whole_down, gains, shifts = weights
        gains = gains.astype(jnp.float32)
        flat_qkv = whole_qkv.reshape(width, 3 * head_cols)
        (
            first_hat,
            first_factor,
            first_full,
            query_hat,
            query_factor,
            keys_hat,
            keys_factor,
            query_n,
            keys_n,
            values,
            mixed_keep,
            log_total,
            second_hat,
            second_factor,
            second_full,
            hidden,
            active,
        ) = kept
        piece = lax.all_gather(grad_out, "tensor", axis=0, tiled=True)
        grad_full = piece
        grad_active = jnp.dot(piece, whole_down, preferred_element_type=jnp.float32)
        grad_down = contract_rows(grad_full, active)
        unused_value, gelu_pull = jax.vjp(
            lambda value: jax.nn.gelu(value, approximate=False), hidden
        )
        grad_hidden = gelu_pull(grad_active)[0].astype(jnp.bfloat16)
        grad_up = contract_rows(second_full, grad_hidden)
        grad_second = lax.psum_scatter(
            contract_cols(grad_hidden, whole_up), "tensor", scatter_dimension=0, tiled=True
        )
        grad_middle = grad_out.astype(jnp.float32) + norm_back(
            grad_second * gains[:, 1], second_hat, second_factor
        )
        grad_branch = grad_middle.astype(jnp.bfloat16)
        piece = lax.all_gather(grad_branch, "tensor", axis=0, tiled=True)
        grad_mixed = jnp.dot(piece, whole_out, preferred_element_type=jnp.float32)
        grad_out_w = contract_rows(piece, mixed_keep)
        grad_mixed = grad_mixed.astype(jnp.bfloat16)
        grad_mixed = grad_mixed.reshape(blocks, block, local_heads, HD)

        def attend_back(carry, item):
            grad_keys_sum, grad_values_sum = carry
            query_block, grad_block, log_block = item
            scores = jnp.einsum(
                "qhd,khd->hqk", query_block, keys_n, preferred_element_type=jnp.float32
            )
            probs = jnp.exp(scores - log_block[..., None])
            grad_probs = jnp.einsum(
                "qhd,khd->hqk", grad_block, values, preferred_element_type=jnp.float32
            )
            delta = jnp.sum(probs * grad_probs, -1, keepdims=True)
            grad_scores = (probs * (grad_probs - delta)).astype(jnp.bfloat16)
            grad_query_block = jnp.einsum(
                "hqk,khd->qhd", grad_scores, keys_n, preferred_element_type=jnp.float32
            )
            grad_keys_sum = grad_keys_sum + jnp.einsum(
                "hqk,qhd->khd", grad_scores, query_block, preferred_element_type=jnp.float32
            )
            grad_values_sum = grad_values_sum + jnp.einsum(
                "hqk,qhd->khd",
                probs.astype(jnp.bfloat16),
                grad_block,
                preferred_element_type=jnp.float32,
            )
            return ((grad_keys_sum, grad_values_sum), grad_query_block)

        empty_heads = jnp.zeros((full_len, local_heads, HD), jnp.float32)
        (grad_keys_n, grad_values), grad_query_n = lax.scan(
            attend_back,
            (empty_heads, empty_heads),
            (query_n.reshape(blocks, block, local_heads, HD), grad_mixed, log_total),
        )
        grad_query_n = grad_query_n.reshape(full_len, local_heads, HD)
        grad_query = norm_back(grad_query_n * gain_query * scale_query, query_hat, query_factor)
        grad_keys = norm_back(grad_keys_n * gain_keys, keys_hat, keys_factor)
        qk_grad = jnp.stack(
            [
                jnp.sum(grad_query_n * query_hat * scale_query, (0, 1)),
                jnp.sum(grad_keys_n * keys_hat, (0, 1)),
            ]
        )
        grad_joined = jnp.stack([grad_query, grad_keys, grad_values], 1).astype(jnp.bfloat16)
        grad_joined = grad_joined.reshape(full_len, 3 * head_cols)
        grad_qkv = contract_rows(first_full, grad_joined).reshape(width, 3, head_cols)
        grad_first = lax.psum_scatter(
            contract_cols(grad_joined, flat_qkv).astype(jnp.bfloat16),
            "tensor",
            scatter_dimension=0,
            tiled=True,
        ).astype(jnp.float32)
        grad_input = grad_middle + norm_back(grad_first * gains[:, 0], first_hat, first_factor)
        gain_grad = jnp.stack(
            [jnp.sum(grad_first * first_hat, 0), jnp.sum(grad_second * second_hat, 0)], 1
        )
        shift_grad = jnp.stack([jnp.sum(grad_first, 0), jnp.sum(grad_second, 0)], 1)
        return (
            (grad_qkv, grad_out_w, grad_up, grad_down, gain_grad, shift_grad, qk_grad),
            grad_input,
        )

    def micro_step(totals, item):
        inputs, grad_out = item
        forward_weights = fetch()
        kept, result = forward(forward_weights, inputs)
        backward_weights = fetch()
        grads, grad_input = backward(backward_weights, kept, grad_out)
        totals = tuple((total + part for total, part in zip(totals, grads)))
        return (totals, (result, grad_input))

    out_cols_count = wo_t.shape[1]
    start_sums = (
        jnp.zeros((width, 3, head_cols), jnp.float32),
        jnp.zeros((width, out_cols_count), jnp.float32),
        jnp.zeros((width, hidden_cols), jnp.float32),
        jnp.zeros((width, hidden_cols), jnp.float32),
        jnp.zeros((width, 2), jnp.float32),
        jnp.zeros((width, 2), jnp.float32),
        jnp.zeros((2, HD), jnp.float32),
    )
    totals, (outputs, grad_tokens) = lax.scan(micro_step, start_sums, (tokens, cotangent))
    out_total = totals[1]
    grad_qkv, grad_out_w, grad_up, grad_down = (
        lax.psum_scatter(
            totals[0].astype(jnp.bfloat16), "fsdp", scatter_dimension=0, tiled=True
        ).astype(jnp.float32),
        lax.psum_scatter(
            out_total.astype(jnp.bfloat16), "fsdp", scatter_dimension=0, tiled=True
        ).astype(jnp.float32),
        lax.psum_scatter(
            totals[2].astype(jnp.bfloat16), "fsdp", scatter_dimension=0, tiled=True
        ).astype(jnp.float32),
        lax.psum_scatter(
            totals[3].astype(jnp.bfloat16), "fsdp", scatter_dimension=0, tiled=True
        ).astype(jnp.float32),
    )
    gain_total, shift_total, qk_total = lax.psum(
        (totals[4], totals[5], totals[6]), ("fsdp", "tensor")
    )
    own_rows = width // lax.axis_size("fsdp")
    offset = lax.axis_index("fsdp") * own_rows
    gain_part = lax.dynamic_slice_in_dim(gain_total, offset, own_rows, 0)
    shift_part = lax.dynamic_slice_in_dim(shift_total, offset, own_rows, 0)
    return (
        outputs,
        grad_tokens,
        grad_qkv,
        grad_out_w,
        grad_up,
        grad_down,
        gain_part,
        shift_part,
        qk_total,
    )


def whole_images(tokens, cotangent, w_qkv, wo_t, w_up, w_down_t, norm_gains, norm_shifts, qk_gains):
    tensor_count = lax.axis_size("tensor")
    local_rows = tokens.shape[1]
    width = tokens.shape[2]
    full_len = local_rows * tensor_count
    own_rows = w_qkv.shape[0]
    both = ("tensor", "fsdp")
    scale_query = HD ** (-0.5)
    gain_query = qk_gains[0].astype(jnp.float32)
    gain_keys = qk_gains[1].astype(jnp.float32)

    def swap(value):
        return lax.all_to_all(value, "tensor", split_axis=0, concat_axis=1, tiled=True)

    def swap_back(value):
        return lax.all_to_all(value, "tensor", split_axis=1, concat_axis=0, tiled=True)

    def gather(shard):
        return lax.all_gather(shard, both).reshape((tensor_count, width) + shard.shape[1:])

    def scatter(grad):
        flat = grad.astype(jnp.bfloat16).reshape((tensor_count * width,) + grad.shape[2:])
        return lax.psum_scatter(flat, both, scatter_dimension=0, tiled=True).astype(jnp.float32)

    image = swap(tokens)[0]
    grad_out = swap(cotangent)[0]
    gains = lax.all_gather(norm_gains, "fsdp", axis=0, tiled=True).astype(jnp.float32)
    shifts = lax.all_gather(norm_shifts, "fsdp", axis=0, tiled=True).astype(jnp.float32)
    qkv = gather(w_qkv)
    out_w = gather(wo_t)
    up = gather(w_up)
    down = gather(w_down_t)
    head_cols = qkv.shape[3]
    heads = head_cols // HD

    residual = image.astype(jnp.float32)
    first_hat, first_factor = norm_stats(residual)
    first = (first_hat * gains[:, 0] + shifts[:, 0]).astype(jnp.bfloat16)
    joined = jnp.einsum("ld,tdpc->tplc", first, qkv, preferred_element_type=jnp.float32)
    joined = joined.reshape(tensor_count, 3, full_len, heads, HD)
    query_hat, query_factor = norm_stats(joined[:, 0])
    keys_hat, keys_factor = norm_stats(joined[:, 1])
    query_n = (query_hat * gain_query * scale_query).astype(jnp.bfloat16)
    keys_n = (keys_hat * gain_keys).astype(jnp.bfloat16)
    values = joined[:, 2].astype(jnp.bfloat16)

    def attend(item):
        query_one, keys_one, values_one = item
        scores = jnp.einsum("qhd,khd->hqk", query_one, keys_one, preferred_element_type=jnp.float32)
        largest = jnp.max(scores, -1, keepdims=True)
        exponent = jnp.exp(scores - largest)
        total_sum = jnp.sum(exponent, -1, keepdims=True)
        probs_low = (exponent / total_sum).astype(jnp.bfloat16)
        mixed_one = jnp.einsum("hqk,khd->qhd", probs_low, values_one, preferred_element_type=jnp.float32)
        return mixed_one.astype(jnp.bfloat16), largest + jnp.log(total_sum)

    mixed, log_total = lax.map(attend, (query_n, keys_n, values))
    mixed = mixed.reshape(tensor_count, full_len, head_cols)
    middle = residual + jnp.einsum("tlc,tdc->ld", mixed, out_w, preferred_element_type=jnp.float32)
    second_hat, second_factor = norm_stats(middle)
    second = (second_hat * gains[:, 1] + shifts[:, 1]).astype(jnp.bfloat16)
    hidden = jnp.einsum("ld,tdf->tlf", second, up, preferred_element_type=jnp.float32)
    active, gelu_pull = jax.vjp(lambda value: jax.nn.gelu(value, approximate=False), hidden)
    active = active.astype(jnp.bfloat16)
    result = (
        middle + jnp.einsum("tlf,tdf->ld", active, down, preferred_element_type=jnp.float32)
    ).astype(jnp.bfloat16)

    grad_active = jnp.einsum("ld,tdf->tlf", grad_out, down, preferred_element_type=jnp.float32)
    grad_down = jnp.einsum("ld,tlf->tdf", grad_out, active, preferred_element_type=jnp.float32)
    grad_down = scatter(grad_down)
    grad_hidden = gelu_pull(grad_active)[0].astype(jnp.bfloat16)
    grad_up = jnp.einsum("ld,tlf->tdf", second, grad_hidden, preferred_element_type=jnp.float32)
    grad_up = scatter(grad_up)
    grad_second = jnp.einsum("tlf,tdf->ld", grad_hidden, up, preferred_element_type=jnp.float32)
    grad_middle = grad_out.astype(jnp.float32) + norm_back(
        grad_second * gains[:, 1], second_hat, second_factor
    )
    grad_branch = grad_middle.astype(jnp.bfloat16)
    grad_out_w = jnp.einsum("ld,tlc->tdc", grad_branch, mixed, preferred_element_type=jnp.float32)
    grad_out_w = scatter(grad_out_w)
    grad_mixed = jnp.einsum("ld,tdc->tlc", grad_branch, out_w, preferred_element_type=jnp.float32)
    grad_mixed = grad_mixed.astype(jnp.bfloat16).reshape(tensor_count, full_len, heads, HD)

    def attend_back(item):
        query_one, keys_one, values_one, grad_one, log_one = item
        scores = jnp.einsum("qhd,khd->hqk", query_one, keys_one, preferred_element_type=jnp.float32)
        probs = jnp.exp(scores - log_one)
        grad_probs = jnp.einsum("qhd,khd->hqk", grad_one, values_one, preferred_element_type=jnp.float32)
        delta = jnp.sum(probs * grad_probs, -1, keepdims=True)
        grad_scores = (probs * (grad_probs - delta)).astype(jnp.bfloat16)
        return (
            jnp.einsum("hqk,khd->qhd", grad_scores, keys_one, preferred_element_type=jnp.float32),
            jnp.einsum("hqk,qhd->khd", grad_scores, query_one, preferred_element_type=jnp.float32),
            jnp.einsum(
                "hqk,qhd->khd", probs.astype(jnp.bfloat16), grad_one, preferred_element_type=jnp.float32
            ),
        )

    grad_query_n, grad_keys_n, grad_values = lax.map(
        attend_back, (query_n, keys_n, values, grad_mixed, log_total)
    )
    grad_query = norm_back(grad_query_n * gain_query * scale_query, query_hat, query_factor)
    grad_keys = norm_back(grad_keys_n * gain_keys, keys_hat, keys_factor)
    qk_grad = jnp.stack(
        [
            jnp.sum(grad_query_n * query_hat * scale_query, (0, 1, 2)),
            jnp.sum(grad_keys_n * keys_hat, (0, 1, 2)),
        ]
    )
    grad_joined = jnp.stack([grad_query, grad_keys, grad_values], 1).astype(jnp.bfloat16)
    grad_joined = grad_joined.reshape(tensor_count, 3, full_len, head_cols)
    grad_qkv = jnp.einsum("ld,tplc->tdpc", first, grad_joined, preferred_element_type=jnp.float32)
    grad_qkv = scatter(grad_qkv)
    grad_first = jnp.einsum("tplc,tdpc->ld", grad_joined, qkv, preferred_element_type=jnp.float32)
    grad_input = grad_middle + norm_back(grad_first * gains[:, 0], first_hat, first_factor)
    gain_grad = jnp.stack(
        [jnp.sum(grad_first * first_hat, 0), jnp.sum(grad_second * second_hat, 0)], 1
    )
    shift_grad = jnp.stack([jnp.sum(grad_first, 0), jnp.sum(grad_second, 0)], 1)
    gain_total, shift_total, qk_total = lax.psum((gain_grad, shift_grad, qk_grad), ("fsdp", "tensor"))
    offset = lax.axis_index("fsdp") * own_rows
    return (
        swap_back(result[None]),
        swap_back(grad_input[None].astype(jnp.bfloat16)).astype(jnp.float32),
        grad_qkv,
        grad_out_w,
        grad_up,
        grad_down,
        lax.dynamic_slice_in_dim(gain_total, offset, own_rows, 0),
        lax.dynamic_slice_in_dim(shift_total, offset, own_rows, 0),
        qk_total,
    )


def layer(tokens, *rest):
    if tokens.shape[0] == lax.axis_size("tensor"):
        return whole_images(tokens, *rest)
    return per_device(tokens, *rest)


def solution(mesh):
    in_specs = (
        P("fsdp", "tensor", None),
        P("fsdp", "tensor", None),
        P("fsdp", None, "tensor"),
        P("fsdp", "tensor"),
        P("fsdp", "tensor"),
        P("fsdp", "tensor"),
        P("fsdp", None),
        P("fsdp", None),
        P(),
    )
    out_specs = (
        P("fsdp", "tensor", None),
        P("fsdp", "tensor", None),
        P("fsdp", None, "tensor"),
        P("fsdp", "tensor"),
        P("fsdp", "tensor"),
        P("fsdp", "tensor"),
        P("fsdp", None),
        P("fsdp", None),
        P(),
    )
    return jax.shard_map(
        layer, mesh=mesh, in_specs=in_specs, out_specs=out_specs, check_vma=False
    )
```

```python
import functools

import jax
import jax.numpy as jnp
from jax import lax
from jax.experimental import pallas as pl
from jax.experimental.pallas import tpu as pltpu
from jax.sharding import PartitionSpec as P

HD = 64


EPSILON = 1e-06


def norm_stats(value):
    center = value - jnp.mean(value, -1, keepdims=True)
    factor = lax.rsqrt(jnp.mean(center * center, -1, keepdims=True) + EPSILON)
    return (center * factor, factor)


def norm_back(grad_hat, normed, factor):
    return factor * (
        grad_hat
        - jnp.mean(grad_hat, -1, keepdims=True)
        - normed * jnp.mean(grad_hat * normed, -1, keepdims=True)
    )


def contract_rows(left, right):
    return lax.dot_general(
        left, right, (((0,), (0,)), ((), ())), preferred_element_type=jnp.float32
    )


def contract_cols(left, right):
    return lax.dot_general(
        left, right, (((1,), (1,)), ((), ())), preferred_element_type=jnp.float32
    )


def per_device(tokens, cotangent, w_qkv, wo_t, w_up, w_down_t, norm_gains, norm_shifts, qk_gains):
    local_rows = tokens.shape[1]
    width = tokens.shape[2]
    head_cols = w_qkv.shape[2]
    local_heads = head_cols // HD
    hidden_cols = w_up.shape[1]
    tensor_count = lax.axis_size("tensor")
    full_len = local_rows * tensor_count
    block = min(512, full_len)
    blocks = full_len // block
    gain_query = qk_gains[0].astype(jnp.float32)
    gain_keys = qk_gains[1].astype(jnp.float32)
    scale_query = HD ** (-0.5)

    def fetch():
        return (
            lax.all_gather(w_qkv, "fsdp", axis=0, tiled=True),
            lax.all_gather(wo_t, "fsdp", axis=0, tiled=True),
            lax.all_gather(w_up, "fsdp", axis=0, tiled=True),
            lax.all_gather(w_down_t, "fsdp", axis=0, tiled=True),
            lax.all_gather(norm_gains, "fsdp", axis=0, tiled=True),
            lax.all_gather(norm_shifts, "fsdp", axis=0, tiled=True),
        )

    def forward(weights, inputs):
        whole_qkv, whole_out, whole_up, whole_down, gains, shifts = weights
        gains = gains.astype(jnp.float32)
        shifts = shifts.astype(jnp.float32)
        flat_qkv = whole_qkv.reshape(width, 3 * head_cols)
        residual = inputs.astype(jnp.float32)
        first_hat, first_factor = norm_stats(residual)
        first = (first_hat * gains[:, 0] + shifts[:, 0]).astype(jnp.bfloat16)
        piece = lax.all_gather(first, "tensor", axis=0, tiled=True)
        first_full = piece
        joined = jnp.dot(piece, flat_qkv, preferred_element_type=jnp.float32)
        joined = joined.reshape(full_len, 3, local_heads, HD)
        query_hat, query_factor = norm_stats(joined[:, 0])
        keys_hat, keys_factor = norm_stats(joined[:, 1])
        query_n = (query_hat * gain_query * scale_query).astype(jnp.bfloat16)
        keys_n = (keys_hat * gain_keys).astype(jnp.bfloat16)
        values = joined[:, 2].astype(jnp.bfloat16)

        def attend(query_block):
            scores = jnp.einsum(
                "qhd,khd->hqk", query_block, keys_n, preferred_element_type=jnp.float32
            )
            largest = jnp.max(scores, -1, keepdims=True)
            exponent = jnp.exp(scores - largest)
            total_sum = jnp.sum(exponent, -1, keepdims=True)
            probs_low = (exponent / total_sum).astype(jnp.bfloat16)
            mixed_block = jnp.einsum(
                "hqk,khd->qhd", probs_low, values, preferred_element_type=jnp.float32
            )
            return (mixed_block.astype(jnp.bfloat16), (largest + jnp.log(total_sum))[..., 0])

        mixed, log_total = lax.map(attend, query_n.reshape(blocks, block, local_heads, HD))
        mixed = mixed.reshape(full_len, head_cols)
        middle = residual + lax.psum_scatter(
            contract_cols(mixed, whole_out), "tensor", scatter_dimension=0, tiled=True
        )
        second_hat, second_factor = norm_stats(middle)
        second = (second_hat * gains[:, 1] + shifts[:, 1]).astype(jnp.bfloat16)
        piece = lax.all_gather(second, "tensor", axis=0, tiled=True)
        hidden = jnp.dot(piece, whole_up, preferred_element_type=jnp.float32)
        active = jax.nn.gelu(hidden, approximate=False).astype(jnp.bfloat16)
        result = (
            middle
            + lax.psum_scatter(
                contract_cols(active, whole_down).astype(jnp.bfloat16),
                "tensor",
                scatter_dimension=0,
                tiled=True,
            ).astype(jnp.float32)
        ).astype(jnp.bfloat16)
        kept = (
            first_hat,
            first_factor,
            first_full,
            query_hat,
            query_factor,
            keys_hat,
            keys_factor,
            query_n,
            keys_n,
            values,
            mixed,
            log_total,
            second_hat,
            second_factor,
            piece,
            hidden,
            active,
        )
        return (kept, result)

    def backward(weights, kept, grad_out):
        whole_qkv, whole_out, whole_up, whole_down, gains, shifts = weights
        gains = gains.astype(jnp.float32)
        flat_qkv = whole_qkv.reshape(width, 3 * head_cols)
        (
            first_hat,
            first_factor,
            first_full,
            query_hat,
            query_factor,
            keys_hat,
            keys_factor,
            query_n,
            keys_n,
            values,
            mixed_keep,
            log_total,
            second_hat,
            second_factor,
            second_full,
            hidden,
            active,
        ) = kept
        piece = lax.all_gather(grad_out, "tensor", axis=0, tiled=True)
        grad_full = piece
        grad_active = jnp.dot(piece, whole_down, preferred_element_type=jnp.float32)
        grad_down = contract_rows(grad_full, active)
        unused_value, gelu_pull = jax.vjp(
            lambda value: jax.nn.gelu(value, approximate=False), hidden
        )
        grad_hidden = gelu_pull(grad_active)[0].astype(jnp.bfloat16)
        grad_up = contract_rows(second_full, grad_hidden)
        grad_second = lax.psum_scatter(
            contract_cols(grad_hidden, whole_up), "tensor", scatter_dimension=0, tiled=True
        )
        grad_middle = grad_out.astype(jnp.float32) + norm_back(
            grad_second * gains[:, 1], second_hat, second_factor
        )
        grad_branch = grad_middle.astype(jnp.bfloat16)
        piece = lax.all_gather(grad_branch, "tensor", axis=0, tiled=True)
        grad_mixed = jnp.dot(piece, whole_out, preferred_element_type=jnp.float32)
        grad_out_w = contract_rows(piece, mixed_keep)
        grad_mixed = grad_mixed.astype(jnp.bfloat16)
        grad_mixed = grad_mixed.reshape(blocks, block, local_heads, HD)

        def attend_back(carry, item):
            grad_keys_sum, grad_values_sum = carry
            query_block, grad_block, log_block = item
            scores = jnp.einsum(
                "qhd,khd->hqk", query_block, keys_n, preferred_element_type=jnp.float32
            )
            probs = jnp.exp(scores - log_block[..., None])
            grad_probs = jnp.einsum(
                "qhd,khd->hqk", grad_block, values, preferred_element_type=jnp.float32
            )
            delta = jnp.sum(probs * grad_probs, -1, keepdims=True)
            grad_scores = (probs * (grad_probs - delta)).astype(jnp.bfloat16)
            grad_query_block = jnp.einsum(
                "hqk,khd->qhd", grad_scores, keys_n, preferred_element_type=jnp.float32
            )
            grad_keys_sum = grad_keys_sum + jnp.einsum(
                "hqk,qhd->khd", grad_scores, query_block, preferred_element_type=jnp.float32
            )
            grad_values_sum = grad_values_sum + jnp.einsum(
                "hqk,qhd->khd",
                probs.astype(jnp.bfloat16),
                grad_block,
                preferred_element_type=jnp.float32,
            )
            return ((grad_keys_sum, grad_values_sum), grad_query_block)

        empty_heads = jnp.zeros((full_len, local_heads, HD), jnp.float32)
        (grad_keys_n, grad_values), grad_query_n = lax.scan(
            attend_back,
            (empty_heads, empty_heads),
            (query_n.reshape(blocks, block, local_heads, HD), grad_mixed, log_total),
        )
        grad_query_n = grad_query_n.reshape(full_len, local_heads, HD)
        grad_query = norm_back(grad_query_n * gain_query * scale_query, query_hat, query_factor)
        grad_keys = norm_back(grad_keys_n * gain_keys, keys_hat, keys_factor)
        qk_grad = jnp.stack(
            [
                jnp.sum(grad_query_n * query_hat * scale_query, (0, 1)),
                jnp.sum(grad_keys_n * keys_hat, (0, 1)),
            ]
        )
        grad_joined = jnp.stack([grad_query, grad_keys, grad_values], 1).astype(jnp.bfloat16)
        grad_joined = grad_joined.reshape(full_len, 3 * head_cols)
        grad_qkv = contract_rows(first_full, grad_joined).reshape(width, 3, head_cols)
        grad_first = lax.psum_scatter(
            contract_cols(grad_joined, flat_qkv).astype(jnp.bfloat16),
            "tensor",
            scatter_dimension=0,
            tiled=True,
        ).astype(jnp.float32)
        grad_input = grad_middle + norm_back(grad_first * gains[:, 0], first_hat, first_factor)
        gain_grad = jnp.stack(
            [jnp.sum(grad_first * first_hat, 0), jnp.sum(grad_second * second_hat, 0)], 1
        )
        shift_grad = jnp.stack([jnp.sum(grad_first, 0), jnp.sum(grad_second, 0)], 1)
        return (
            (grad_qkv, grad_out_w, grad_up, grad_down, gain_grad, shift_grad, qk_grad),
            grad_input,
        )

    def micro_step(totals, item):
        inputs, grad_out = item
        forward_weights = fetch()
        kept, result = forward(forward_weights, inputs)
        backward_weights = fetch()
        grads, grad_input = backward(backward_weights, kept, grad_out)
        totals = tuple((total + part for total, part in zip(totals, grads)))
        return (totals, (result, grad_input))

    out_cols_count = wo_t.shape[1]
    start_sums = (
        jnp.zeros((width, 3, head_cols), jnp.float32),
        jnp.zeros((width, out_cols_count), jnp.float32),
        jnp.zeros((width, hidden_cols), jnp.float32),
        jnp.zeros((width, hidden_cols), jnp.float32),
        jnp.zeros((width, 2), jnp.float32),
        jnp.zeros((width, 2), jnp.float32),
        jnp.zeros((2, HD), jnp.float32),
    )
    totals, (outputs, grad_tokens) = lax.scan(micro_step, start_sums, (tokens, cotangent))
    out_total = totals[1]
    grad_qkv, grad_out_w, grad_up, grad_down = (
        lax.psum_scatter(
            totals[0].astype(jnp.bfloat16), "fsdp", scatter_dimension=0, tiled=True
        ).astype(jnp.float32),
        lax.psum_scatter(
            out_total.astype(jnp.bfloat16), "fsdp", scatter_dimension=0, tiled=True
        ).astype(jnp.float32),
        lax.psum_scatter(
            totals[2].astype(jnp.bfloat16), "fsdp", scatter_dimension=0, tiled=True
        ).astype(jnp.float32),
        lax.psum_scatter(
            totals[3].astype(jnp.bfloat16), "fsdp", scatter_dimension=0, tiled=True
        ).astype(jnp.float32),
    )
    gain_total, shift_total, qk_total = lax.psum(
        (totals[4], totals[5], totals[6]), ("fsdp", "tensor")
    )
    own_rows = width // lax.axis_size("fsdp")
    offset = lax.axis_index("fsdp") * own_rows
    gain_part = lax.dynamic_slice_in_dim(gain_total, offset, own_rows, 0)
    shift_part = lax.dynamic_slice_in_dim(shift_total, offset, own_rows, 0)
    return (
        outputs,
        grad_tokens,
        grad_qkv,
        grad_out_w,
        grad_up,
        grad_down,
        gain_part,
        shift_part,
        qk_total,
    )


PAIR = 2 * HD
F32, BF16 = jnp.float32, jnp.bfloat16
LIMIT = 60 << 20


def nn(a, b):
    return lax.dot_general(a, b, (((1,), (0,)), ((), ())), preferred_element_type=F32)


def nt(a, b):
    return lax.dot_general(a, b, (((1,), (1,)), ((), ())), preferred_element_type=F32)


def stats(value):
    center = value - jnp.mean(value, -1, keepdims=True)
    factor = lax.rsqrt(jnp.mean(center * center, -1, keepdims=True) + EPSILON)
    return center * factor, factor


def back(grad_hat, normed, factor):
    return factor * (
        grad_hat
        - jnp.mean(grad_hat, -1, keepdims=True)
        - normed * jnp.mean(grad_hat * normed, -1, keepdims=True)
    )


def head_mean_matrix(width):
    row = lax.broadcasted_iota(jnp.int32, (width, width), 0) // HD
    col = lax.broadcasted_iota(jnp.int32, (width, width), 1) // HD
    return jnp.where(row == col, 1.0 / HD, 0.0).astype(BF16)


def head_mean(value, matrix):
    high = value.astype(BF16)
    low = (value - high.astype(F32)).astype(BF16)
    return nn(high, matrix) + nn(low, matrix)


def head_stats(value, matrix):
    center = value - head_mean(value, matrix)
    factor = lax.rsqrt(head_mean(center * center, matrix) + EPSILON)
    return center * factor, factor


def head_back(grad_hat, normed, factor, matrix):
    return factor * (
        grad_hat - head_mean(grad_hat, matrix) - normed * head_mean(grad_hat * normed, matrix)
    )


QKV_TILE = 256


def project_body(per_part, image, norms, gains, w, first, qn, kn, v, q_raw, k_raw, held):
    step = pl.program_id(0)

    @pl.when(step == 0)
    def _():
        rows = image.shape[0] // 4

        def norm(i, _):
            at = pl.ds(i * rows, rows)
            hat, _f = stats(image[at].astype(F32))
            value = (hat * norms[0:1] + norms[2:3]).astype(BF16)
            held[at] = value
            first[at] = value
            return 0
        lax.fori_loop(0, 4, norm, 0)

    joined = nn(held[...], w[0])
    part = step // per_part
    matrix = head_mean_matrix(QKV_TILE)

    @pl.when(part == 0)
    def _():
        hat, _f = head_stats(joined, matrix)
        qn[...] = (hat * gains[0:1] * (HD ** -0.5)).astype(BF16)
        q_raw[...] = joined.astype(BF16)

    @pl.when(part == 1)
    def _():
        hat, _f = head_stats(joined, matrix)
        kn[...] = (hat * gains[1:2]).astype(BF16)
        k_raw[...] = joined.astype(BF16)

    @pl.when(part == 2)
    def _():
        v[...] = joined.astype(BF16)


def project(image, norms, gains, w, cols):
    length, width = image.shape
    half = cols // 3
    per_half = half // QKV_TILE
    per_part = 2 * per_half

    def w_map(s):
        part, rest = s // per_part, s % per_part
        return rest // per_half, 0, part * per_half + rest % per_half

    def out_map(part):
        return lambda s: (0, jnp.clip(s - part * per_part, 0, per_part - 1))

    block = lambda part: pl.BlockSpec((length, QKV_TILE), out_map(part))
    full = lambda a: pl.BlockSpec(a.shape, lambda s: (0,) * a.ndim)
    heads = jax.ShapeDtypeStruct((length, 2 * half), BF16)
    return pl.pallas_call(
        functools.partial(project_body, per_part),
        grid=(3 * per_part,),
        in_specs=[full(image), full(norms), full(gains), pl.BlockSpec((1, width, QKV_TILE), w_map)],
        out_specs=[pl.BlockSpec((length, width), lambda s: (0, 0)), block(0), block(1), block(2), block(0), block(1)],
        out_shape=[jax.ShapeDtypeStruct((length, width), BF16)] + [heads] * 5,
        scratch_shapes=[pltpu.VMEM((length, width), BF16)],
        compiler_params=pltpu.CompilerParams(vmem_limit_bytes=LIMIT),
        name="project",
    )(image, norms, gains, w)


Q_TILE = 256


def attend_body(qn, kn, v, mixed, inverse):
    length = qn.shape[0]
    lane = lax.broadcasted_iota(jnp.int32, (1, PAIR), 1) < HD
    keys = kn[...]
    ones = jnp.ones((length, PAIR), BF16)
    values = jnp.concatenate([v[...], ones], axis=1)
    zero = jnp.zeros((), BF16)
    for i in range(length // Q_TILE):
        at = slice(i * Q_TILE, (i + 1) * Q_TILE)
        query = qn[at]
        got = []
        for mask in (lane, ~lane):
            scores = nt(jnp.where(mask, query, zero), keys)
            got.append(nn(jnp.exp(scores).astype(BF16), values))
        inv = 1.0 / jnp.where(lane, got[0][:, PAIR:], got[1][:, PAIR:])
        mixed[at] = (jnp.where(lane, got[0][:, :PAIR], got[1][:, :PAIR]) * inv).astype(BF16)
        inverse[at] = inv


def attend(qn, kn, v):
    length, width = qn.shape
    block = pl.BlockSpec((length, PAIR), lambda h: (0, h))
    return pl.pallas_call(
        attend_body,
        grid=(width // PAIR,),
        in_specs=[block] * 3,
        out_specs=[block] * 2,
        out_shape=[jax.ShapeDtypeStruct((length, width), BF16), jax.ShapeDtypeStruct((length, width), F32)],
        compiler_params=pltpu.CompilerParams(vmem_limit_bytes=LIMIT),
        name="attend",
    )(qn, kn, v)


def attend_back_body(gains, qn, kn, v, q_raw, k_raw, mixed, grad_mixed, inverse, grad_q, grad_k, grad_v, grad_gains):
    length = qn.shape[0]
    first = lax.broadcasted_iota(jnp.int32, (1, PAIR), 1) < HD
    lanes = lax.broadcasted_iota(jnp.int32, (1, PAIR), 1)
    zero = jnp.zeros((), BF16)
    go = grad_mixed[...].astype(F32)
    inv = inverse[...]
    product = go * mixed[...].astype(F32) * inv
    go_inv = (go * inv).astype(BF16)
    query, keys, values = qn[...], kn[...], v[...]
    heads = []
    for h, mask in ((0, first), (1, ~first)):
        delta = -jnp.sum(jnp.where(mask, product, 0.0), -1, keepdims=True)
        high = delta.astype(BF16)
        low = (delta - high.astype(F32)).astype(BF16)
        spare = (1 - h) * HD
        grad_aug = jnp.where(mask, go_inv, jnp.where(lanes == spare, high, jnp.where(lanes == spare + 1, low, zero)))
        values_aug = jnp.where(mask, values, jnp.where((lanes == spare) | (lanes == spare + 1), jnp.ones((), BF16), zero))
        heads.append((jnp.where(mask, query, zero), jnp.where(mask, keys, zero), jnp.where(mask, go_inv, zero), grad_aug, values_aug))
    dq = []
    dk = jnp.zeros((length, PAIR), F32)
    dv = jnp.zeros((length, PAIR), F32)
    for i in range(length // Q_TILE):
        at = slice(i * Q_TILE, (i + 1) * Q_TILE)
        part = jnp.zeros((Q_TILE, PAIR), F32)
        for qm, km, gm, ga, va in heads:
            exponent = jnp.exp(nt(km, qm[at]))
            grad_scores = (exponent * nt(va, ga[at])).astype(BF16)
            dv = dv + nn(exponent.astype(BF16), gm[at])
            dk = dk + nn(grad_scores, qm[at])
            part = part + lax.dot_general(grad_scores, km, (((0,), (0,)), ((), ())), preferred_element_type=F32)
        dq.append(part)
    dq = jnp.concatenate(dq, axis=0)
    grad_v[...] = dv.astype(BF16)
    matrix = head_mean_matrix(PAIR)
    hat, factor = head_stats(q_raw[...].astype(F32), matrix)
    scale = HD ** -0.5
    sum_q = jnp.sum(dq * hat, 0, keepdims=True) * scale
    grad_q[...] = head_back(dq * gains[0:1] * scale, hat, factor, matrix).astype(BF16)
    hat, factor = head_stats(k_raw[...].astype(F32), matrix)
    sum_k = jnp.sum(dk * hat, 0, keepdims=True)
    grad_k[...] = head_back(dk * gains[1:2], hat, factor, matrix).astype(BF16)

    @pl.when(pl.program_id(0) == 0)
    def _():
        grad_gains[...] = jnp.zeros_like(grad_gains)
    grad_gains[...] += jnp.concatenate([sum_q, sum_k], axis=0)


def attend_back(gains, qn, kn, v, q_raw, k_raw, mixed, grad_mixed, inverse):
    length, width = qn.shape
    block = pl.BlockSpec((length, PAIR), lambda h: (0, h))
    same = pl.BlockSpec((2, PAIR), lambda h: (0, 0))
    heads = jax.ShapeDtypeStruct((length, width), BF16)
    return pl.pallas_call(
        attend_back_body,
        grid=(width // PAIR,),
        in_specs=[same] + [block] * 8,
        out_specs=[block] * 3 + [same],
        out_shape=[heads] * 3 + [jax.ShapeDtypeStruct((2, PAIR), F32)],
        compiler_params=pltpu.CompilerParams(vmem_limit_bytes=LIMIT),
        name="attend_back",
    )(gains, qn, kn, v, q_raw, k_raw, mixed, grad_mixed, inverse)


ROWS = 256


def branch_body(image, norms, mixed, w, middle, second):
    half = w.shape[2]
    value = image[...].astype(F32) + nt(mixed[:, :half], w[0]) + nt(mixed[:, half:], w[1])
    middle[...] = value
    hat, _f = stats(value)
    second[...] = (hat * norms[1:2] + norms[3:4]).astype(BF16)


def branch(image, norms, mixed, w):
    length, width = image.shape
    row = pl.BlockSpec((ROWS, width), lambda i: (i, 0))
    full = lambda a: pl.BlockSpec(a.shape, lambda s: (0,) * a.ndim)
    return pl.pallas_call(
        branch_body,
        grid=(length // ROWS,),
        in_specs=[row, full(norms), row, full(w)],
        out_specs=[row, row],
        out_shape=[jax.ShapeDtypeStruct((length, width), F32), jax.ShapeDtypeStruct((length, width), BF16)],
        compiler_params=pltpu.CompilerParams(vmem_limit_bytes=LIMIT),
        name="branch",
    )(image, norms, mixed, w)


FF_TILE = 512


def gelu_parts(v):
    bell = jnp.exp(v * v * -0.5)
    t = 1.0 / (1.0 + (0.3275911 * 0.7071067811865476) * jnp.abs(v))
    poly = t * (0.127414796 + t * (-0.142248368 + t * (0.7107068705 + t * (-0.7265760135 + t * 0.5307027145))))
    tail = poly * bell
    return jnp.where(v >= 0, 1.0 - tail, tail), bell * 0.3989422804014327


def feed_body(second, cot, middle, up, down, result, grad_second, grad_up, grad_down, acc, second_t, cot_t, active, grad_hidden):
    step = pl.program_id(0)
    length = second.shape[0]

    @pl.when(step == 0)
    def _():
        second_t[...] = second[...].T
        cot_t[...] = cot[...].T
        acc[...] = middle[...]
        grad_second[...] = jnp.zeros_like(grad_second)

    w_up, w_down = up[0], down[0]
    for i in range(length // ROWS):
        at = slice(i * ROWS, (i + 1) * ROWS)
        hidden = nn(second[at], w_up)
        grad_active = nn(cot[at], w_down)
        cumulative, density = gelu_parts(hidden)
        a = (hidden * cumulative).astype(BF16)
        g = (grad_active * (cumulative + hidden * density)).astype(BF16)
        active[at] = a
        grad_hidden[at] = g
        acc[at] += nt(a, w_down)
        grad_second[at] += nt(g, w_up)
    grad_up[0] = nn(second_t[...], grad_hidden[...]).astype(BF16)
    grad_down[0] = nn(cot_t[...], active[...]).astype(BF16)

    @pl.when(step == pl.num_programs(0) - 1)
    def _():
        result[...] = acc[...].astype(BF16)


def feed(second, cot, middle, up, down):
    length, width = second.shape
    per_half = up.shape[2] // FF_TILE
    full = lambda a: pl.BlockSpec(a.shape, lambda s: (0,) * a.ndim, pipeline_mode=pl.Buffered(1))
    tile = pl.BlockSpec((1, width, FF_TILE), lambda s: (s // per_half, 0, s % per_half))
    out = lambda: pl.BlockSpec((length, width), lambda s: (0, 0), pipeline_mode=pl.Buffered(1))
    return pl.pallas_call(
        feed_body,
        grid=(2 * per_half,),
        in_specs=[full(second), full(cot), full(middle), tile, tile],
        out_specs=[out(), out(), tile, tile],
        out_shape=[
            jax.ShapeDtypeStruct((length, width), BF16),
            jax.ShapeDtypeStruct((length, width), F32),
            jax.ShapeDtypeStruct(up.shape, BF16),
            jax.ShapeDtypeStruct(down.shape, BF16),
        ],
        scratch_shapes=[
            pltpu.VMEM((length, width), F32),
            pltpu.VMEM((width, length), BF16),
            pltpu.VMEM((width, length), BF16),
            pltpu.VMEM((length, FF_TILE), BF16),
            pltpu.VMEM((length, FF_TILE), BF16),
        ],
        compiler_params=pltpu.CompilerParams(vmem_limit_bytes=LIMIT),
        name="feed",
    )(second, cot, middle, up, down)


def branch_back_body(norms, cot, grad_second, middle, mixed, w, grad_middle, grad_mixed, grad_w, sums, acc):
    step = pl.program_id(0)
    half = w.shape[2]

    @pl.when(step == 0)
    def _():
        sums[...] = jnp.zeros_like(sums)
        acc[...] = jnp.zeros_like(acc)
    hat, factor = stats(middle[...])
    gs = grad_second[...]
    gm = cot[...].astype(F32) + back(gs * norms[1:2], hat, factor)
    grad_middle[...] = gm
    branch_grad = gm.astype(BF16)
    branch_t = branch_grad.T
    for t in range(2):
        at = slice(t * half, (t + 1) * half)
        grad_mixed[:, at] = nn(branch_grad, w[t]).astype(BF16)
        acc[t] += nn(branch_t, mixed[:, at])
    sums[0:1] += jnp.sum(gs * hat, 0, keepdims=True)
    sums[1:2] += jnp.sum(gs, 0, keepdims=True)

    @pl.when(step == pl.num_programs(0) - 1)
    def _():
        grad_w[...] = acc[...].astype(BF16)


def branch_back(norms, cot, grad_second, middle, mixed, w):
    length, width = middle.shape
    row = pl.BlockSpec((ROWS, width), lambda i: (i, 0))
    full = lambda shape: pl.BlockSpec(shape, lambda s: (0,) * len(shape))
    return pl.pallas_call(
        branch_back_body,
        grid=(length // ROWS,),
        in_specs=[full(norms.shape), row, row, row, row, full(w.shape)],
        out_specs=[row, row, full(w.shape), full((2, width))],
        out_shape=[
            jax.ShapeDtypeStruct((length, width), F32),
            jax.ShapeDtypeStruct((length, width), BF16),
            jax.ShapeDtypeStruct(w.shape, BF16),
            jax.ShapeDtypeStruct((2, width), F32),
        ],
        scratch_shapes=[pltpu.VMEM(w.shape, F32)],
        compiler_params=pltpu.CompilerParams(vmem_limit_bytes=LIMIT),
        name="branch_back",
    )(norms, cot, grad_second, middle, mixed, w)


def project_back_body(norms, image, first, grad_middle, gq, gk, gv, w, grad_w, grad_image, sums, acc, first_t):
    step = pl.program_id(0)
    length = image.shape[0]
    half = w.shape[2] // 3

    @pl.when(step == 0)
    def _():
        first_t[...] = first[...].T
        acc[...] = jnp.zeros_like(acc)
    for part, g in enumerate((gq, gk, gv)):
        at = slice(part * half, (part + 1) * half)
        grad_w[0, :, at] = nn(first_t[...], g[...]).astype(BF16)
        acc[...] += nt(g[...], w[0, :, at])

    @pl.when(step == 1)
    def _():
        sum_hat = jnp.zeros((1, image.shape[1]), F32)
        sum_all = jnp.zeros((1, image.shape[1]), F32)
        for i in range(length // ROWS):
            at = slice(i * ROWS, (i + 1) * ROWS)
            hat, factor = stats(image[at].astype(F32))
            gf = acc[at]
            grad_image[at] = (grad_middle[at] + back(gf * norms[0:1], hat, factor)).astype(BF16)
            sum_hat = sum_hat + jnp.sum(gf * hat, 0, keepdims=True)
            sum_all = sum_all + jnp.sum(gf, 0, keepdims=True)
        sums[0:1] = sum_hat
        sums[1:2] = sum_all


def project_back(norms, image, first, grad_middle, gq, gk, gv, w, cols):
    length, width = image.shape
    half = cols // 3
    full = lambda shape: pl.BlockSpec(shape, lambda s: (0,) * len(shape), pipeline_mode=pl.Buffered(1))
    strip = pl.BlockSpec((length, half), lambda s: (0, s))
    weight = pl.BlockSpec((1, width, 3 * half), lambda s: (s, 0, 0))
    return pl.pallas_call(
        project_back_body,
        grid=(2,),
        in_specs=[full(norms.shape), full(image.shape), full(first.shape), full(grad_middle.shape), strip, strip, strip, weight],
        out_specs=[weight, full(image.shape), full((2, width))],
        out_shape=[
            jax.ShapeDtypeStruct((2, width, cols), BF16),
            jax.ShapeDtypeStruct((length, width), BF16),
            jax.ShapeDtypeStruct((2, width), F32),
        ],
        scratch_shapes=[pltpu.VMEM((length, width), F32), pltpu.VMEM((width, length), BF16)],
        compiler_params=pltpu.CompilerParams(vmem_limit_bytes=LIMIT),
        name="project_back",
    )(norms, image, first, grad_middle, gq, gk, gv, w)


MESH = pl.DeviceIdType.MESH


class Place:
    def __init__(self, zs):
        f = lax.axis_index("fsdp")
        self.zs = zs
        self.x = lax.axis_index("tensor")
        self.c = lax.rem(f, 2)
        self.y = lax.rem(lax.div(f, 2), 2)
        self.z = lax.div(f, 4)

    def dev(self, z=None, y=None, c=None, x=None):
        z = self.z if z is None else z
        y = self.y if y is None else y
        c = self.c if c is None else c
        x = self.x if x is None else x
        return {"fsdp": (z * 2 + y) * 2 + c, "tensor": x}

    def peers(self):
        out = [self.dev(z=lax.rem(self.z + k, self.zs)) for k in range(1, self.zs)]
        return out + [self.dev(y=1 - self.y), self.dev(c=1 - self.c), self.dev(x=1 - self.x)]


def meet(place):
    barrier = pltpu.get_barrier_semaphore()
    peers = place.peers()
    for peer in peers:
        pl.semaphore_signal(barrier, inc=1, device_id=peer, device_id_type=MESH)
    pl.semaphore_wait(barrier, len(peers))


def remote(src, dst, send, recv, peer):
    return pltpu.make_async_remote_copy(
        src_ref=src, dst_ref=dst, send_sem=send, recv_sem=recv, device_id=peer, device_id_type=MESH
    )


class Gather:
    def __init__(self, place, shard, whole, cols, order, send, recv):
        p = self.p = place
        self.shard = shard.at[:, cols]
        self.whole = whole
        self.cols = cols
        self.order = order
        self.send, self.recv = send, recv
        self.used = 0
        self.stages = [self.stage(i) for i in range(3)]
        self.cores = [self.core_parts(i) for i in range(3)]
        self.own = pltpu.make_async_copy(self.shard, self.at({}), self.send.at[self.used])

    def at(self, index):
        p = self.p
        own = {"x": p.x, "y": p.y, "z": p.z}
        x, y, z = (index.get(d, own[d]) for d in "xyz")
        return self.whole.at[x, z, y, p.c, :, self.cols]

    def copy(self, src, dst, peer):
        n = self.used
        self.used += 1
        return remote(src, dst, self.send.at[n], self.recv.at[n], peer)

    def others(self, d):
        p = self.p
        if d == "z":
            return [lax.rem(p.z + k, p.zs) for k in range(1, p.zs)]
        return [1 - getattr(p, d)]

    def stage(self, i):
        d = self.order[i]
        held = self.at({e: slice(None) for e in self.order[:i]})
        src = self.shard if i == 0 else held
        return [self.copy(src, held, self.p.dev(**{d: to})) for to in self.others(d)]

    def core_parts(self, i):
        done = {e: slice(None) for e in self.order[:i]}
        d = self.order[i]
        peer = self.p.dev(c=1 - self.p.c)
        if i == 0:
            refs = [self.at({d: slice(None)})]
        else:
            refs = [self.at({**done, d: to}) for to in self.others(d)]
        return [self.copy(ref, ref, peer) for ref in refs]

    def tick0(self):
        self.own.start()
        for copy in self.stages[0]:
            copy.start()

    def tick(self, i):
        if i == 1:
            self.own.wait()
        for copy in self.stages[i - 1]:
            copy.wait()
        if i < 3:
            for copy in self.stages[i]:
                copy.start()
        for copy in self.cores[i - 1]:
            copy.start()

    def tick1(self):
        self.tick(1)

    def tick2(self):
        self.tick(2)

    def tick3(self):
        self.tick(3)

    def tick4(self):
        for part in self.cores:
            for copy in part:
                copy.wait()


def sems_for(zs):
    return 2 * zs + 8


class Swap:
    def __init__(self, place, value, image, sems):
        p = self.p = place
        half = value.shape[1]
        rows = pl.ds(pl.multiple_of(p.x * half, half), half)
        self.copy = remote(value.at[1 - p.x], image.at[rows], sems.at[0], sems.at[1], p.dev(x=1 - p.x))
        self.mine = pltpu.make_async_copy(value.at[p.x], image.at[rows], sems.at[2])

    def start(self):
        self.copy.start()
        self.mine.start()

    def wait(self):
        self.copy.wait()
        self.mine.wait()


def gather_kernel(zs, groups, n_w, n_swap, *refs):
    shards = refs[:n_w]
    values = refs[n_w:n_w + n_swap]
    wholes = refs[n_w + n_swap:2 * n_w + n_swap]
    images = refs[2 * n_w + n_swap:2 * n_w + 2 * n_swap]
    send, recv, swap_sem = refs[2 * n_w + 2 * n_swap:]
    p = Place(zs)
    meet(p)
    swaps = [Swap(p, values[i], images[i], swap_sem.at[i]) for i in range(n_swap)]
    gs = [Gather(p, shards[w], wholes[w], pl.ds(lo, n), order, send.at[i], recv.at[i])
          for i, (w, lo, n, order) in enumerate(groups)]
    if swaps:
        swaps[0].start()
    n = len(gs)
    for t in range(n + 4):
        for k, tick in ((0, "tick0"), (1, "tick1"), (2, "tick2"), (3, "tick3"), (4, "tick4")):
            if 0 <= t - k < n:
                getattr(gs[t - k], tick)()
        if t == 1:
            for s in swaps[1:]:
                s.start()
    for s in swaps:
        s.wait()


def gather_all(shards, values, groups, zs, collective_id):
    n_w, n_s = len(shards), len(values)
    out = [jax.ShapeDtypeStruct((2, zs, 2, 2) + s.shape, s.dtype) for s in shards]
    out += [jax.ShapeDtypeStruct((v.shape[0] * v.shape[1], v.shape[2]), v.dtype) for v in values]
    got = pl.pallas_call(
        functools.partial(gather_kernel, zs, groups, n_w, n_s),
        out_shape=out,
        in_specs=[pl.BlockSpec(memory_space=pl.ANY)] * (n_w + n_s),
        out_specs=[pl.BlockSpec(memory_space=pl.ANY)] * (n_w + n_s),
        scratch_shapes=[
            pltpu.SemaphoreType.DMA((len(groups), sems_for(zs))),
            pltpu.SemaphoreType.DMA((len(groups), sems_for(zs))),
            pltpu.SemaphoreType.DMA((max(n_s, 1), 3)),
        ],
        compiler_params=pltpu.CompilerParams(collective_id=collective_id, has_side_effects=True),
        name="gather_weights",
    )(*shards, *values)
    return got[:n_w], got[n_w:]


class Scatter:
    def __init__(self, place, grad, cols, order, a, b, b1, b2, b3, send, recv):
        self.p = place
        self.grad, self.cols, self.order = grad, cols, order
        self.a, self.b, self.b1, self.b2, self.b3 = a, b, b1, b2, b3
        self.send, self.recv = send, recv

    def load(self):
        p = self.p
        return pltpu.make_async_copy(self.grad.at[:, :, :, p.c, :, self.cols], self.a, self.send.at[p.zs + 2])

    def core(self):
        p = self.p
        return remote(self.grad.at[:, :, :, 1 - p.c, :, self.cols], self.b, self.send.at[0], self.recv.at[0], p.dev(c=1 - p.c))

    def first(self):
        p = self.p
        if self.order == "x":
            return remote(self.a.at[1 - p.x], self.b1, self.send.at[1], self.recv.at[1], p.dev(x=1 - p.x))
        return remote(self.a.at[:, :, 1 - p.y], self.b1, self.send.at[1], self.recv.at[1], p.dev(y=1 - p.y))

    def second(self):
        p = self.p
        if self.order == "x":
            return remote(self.a.at[p.x, :, 1 - p.y], self.b2, self.send.at[2], self.recv.at[2], p.dev(y=1 - p.y))
        return remote(self.a.at[1 - p.x, :, p.y], self.b2, self.send.at[2], self.recv.at[2], p.dev(x=1 - p.x))

    def z_copies(self):
        p = self.p
        out = []
        for k in range(1, p.zs):
            to = lax.rem(p.z + k, p.zs)
            out.append(remote(self.a.at[p.x, to, p.y], self.b3.at[k - 1], self.send.at[2 + k], self.recv.at[2 + k], p.dev(z=to)))
        return out


def add_loop(count, body):
    lax.fori_loop(0, count, lambda i, _: (body(i), 0)[1], 0)


class SwapBack:
    def __init__(self, place, value, out, sems):
        p = place
        half = out.shape[1]
        to = pl.ds(pl.multiple_of((1 - p.x) * half, half), half)
        rows = pl.ds(pl.multiple_of(p.x * half, half), half)
        self.copy = remote(value.at[to], out.at[p.x], sems.at[0], sems.at[1], p.dev(x=1 - p.x))
        self.mine = pltpu.make_async_copy(value.at[rows], out.at[p.x], sems.at[2])

    def start(self):
        self.copy.start()
        self.mine.start()

    def wait(self):
        self.copy.wait()
        self.mine.wait()


class Sum:
    def __init__(self, place, value, total, got, send, recv):
        self.p, self.value, self.total, self.got, self.send, self.recv = place, value, total, got, send, recv

    def copies(self, i):
        p = self.p
        if i < 3:
            peers = [(p.dev(c=1 - p.c), p.dev(x=1 - p.x), p.dev(y=1 - p.y))[i]]
        else:
            peers = [p.dev(z=lax.rem(p.z + k, p.zs)) for k in range(1, p.zs)]
        return [remote(self.total, self.got.at[i + k], self.send.at[i + k], self.recv.at[i + k], peer)
                for k, peer in enumerate(peers)]

    def start(self, i):
        for copy in self.copies(i):
            copy.start()

    def finish(self, i):
        copies = self.copies(i)
        for copy in copies:
            copy.wait()
        total = self.total[...]
        for k in range(len(copies)):
            total = total + self.got[i + k]
        self.total[...] = total


def scatter_kernel(zs, groups, n_w, n_s, *refs):
    grads = refs[:n_w]
    values = refs[n_w:n_w + n_s]
    small = refs[n_w + n_s]
    outs = refs[n_w + n_s + 1:2 * n_w + n_s + 1]
    backs = refs[2 * n_w + n_s + 1:2 * n_w + 2 * n_s + 1]
    total = refs[2 * n_w + 2 * n_s + 1]
    rest = refs[2 * n_w + 2 * n_s + 2:]
    n = len(groups)
    bufs = [rest[5 * i:5 * i + 5] for i in range(n)]
    send, recv, swap_sem, got, sum_send, sum_recv = rest[5 * n:]
    p = Place(zs)
    meet(p)
    gs = [Scatter(p, grads[w], pl.ds(lo, m), order, *bufs[i], send.at[i], recv.at[i])
          for i, (w, lo, m, order) in enumerate(groups)]
    swaps = [SwapBack(p, values[i], backs[i], swap_sem.at[i]) for i in range(n_s)]
    total[...] = small[...]
    sums = Sum(p, small, total, got, sum_send, sum_recv)

    def t0(i):
        gs[i].load().start()
        gs[i].core().start()

    def t1(i):
        g = gs[i]
        g.load().wait()
        g.core().wait()

        def add(j):
            x, z, y = lax.div(j, 2 * zs), lax.rem(lax.div(j, 2), zs), lax.rem(j, 2)
            g.a[x, z, y] = g.a[x, z, y] + g.b[x, z, y]
        add_loop(4 * zs, add)
        g.first().start()

    def t2(i):
        g = gs[i]
        g.first().wait()

        def add(j):
            if g.order == "x":
                z, y = lax.div(j, 2), lax.rem(j, 2)
                g.a[p.x, z, y] = g.a[p.x, z, y] + g.b1[z, y]
            else:
                x, z = lax.div(j, zs), lax.rem(j, zs)
                g.a[x, z, p.y] = g.a[x, z, p.y] + g.b1[x, z]
        add_loop(2 * zs, add)
        g.second().start()

    def t3(i):
        g = gs[i]
        g.second().wait()

        def add(z):
            g.a[p.x, z, p.y] = g.a[p.x, z, p.y] + g.b2[z]
        add_loop(zs, add)
        for copy in g.z_copies():
            copy.start()

    def t4(i):
        g = gs[i]
        w, lo, m, order = groups[i]
        for copy in g.z_copies():
            copy.wait()
        value = g.a[p.x, p.z, p.y].astype(jnp.float32)
        for k in range(zs - 1):
            value = value + g.b3[k].astype(jnp.float32)
        outs[w][:, lo:lo + m] = value

    for t in range(n + 4):
        for k, tick in ((0, t0), (4, t4), (3, t3), (2, t2), (1, t1)):
            if 0 <= t - k < n:
                tick(t - k)
        if t < 4:
            sums.start(t)
        if t < len(swaps):
            swaps[t].start()
        if t < 4:
            sums.finish(t)
    for s in swaps:
        s.wait()


def scatter_all(grads, values, small, groups, zs, collective_id):
    n_w, n_s = len(grads), len(values)
    rows = grads[0].shape[4]
    scratch = []
    for w, lo, m, order in groups:
        first = (zs, 2, rows, m) if order == "x" else (2, zs, rows, m)
        for shape in ((2, zs, 2, rows, m), (2, zs, 2, rows, m), first, (zs, rows, m), (zs - 1, rows, m)):
            scratch.append(pltpu.VMEM(shape, jnp.bfloat16))
    scratch += [pltpu.SemaphoreType.DMA((len(groups), zs + 3)), pltpu.SemaphoreType.DMA((len(groups), zs + 3))]
    scratch += [pltpu.SemaphoreType.DMA((n_s, 3)), pltpu.VMEM((zs + 2,) + small.shape, jnp.float32)]
    scratch += [pltpu.SemaphoreType.DMA((zs + 2,)), pltpu.SemaphoreType.DMA((zs + 2,))]
    vmem = pl.BlockSpec(memory_space=pltpu.VMEM)
    hbm = pl.BlockSpec(memory_space=pl.ANY)
    got = pl.pallas_call(
        functools.partial(scatter_kernel, zs, groups, n_w, n_s),
        out_shape=[jax.ShapeDtypeStruct(g.shape[4:], jnp.float32) for g in grads]
        + [jax.ShapeDtypeStruct((2, v.shape[0] // 2, v.shape[1]), v.dtype) for v in values]
        + [jax.ShapeDtypeStruct(small.shape, jnp.float32)],
        in_specs=[hbm] * (n_w + n_s) + [vmem],
        out_specs=[vmem] * n_w + [hbm] * n_s + [vmem],
        scratch_shapes=scratch,
        compiler_params=pltpu.CompilerParams(collective_id=collective_id, has_side_effects=True, vmem_limit_bytes=60 << 20),
        name="scatter_grads",
    )(*grads, *values, small)
    return got[:n_w], got[n_w:n_w + n_s], got[-1]


GATHERS = ((0, 0, 768, "zyx"), (0, 768, 896, "zxy"), (1, 0, 512, "zyx"), (2, 0, 1024, "zxy"), (2, 1024, 1024, "zyx"),
           (3, 0, 1024, "zxy"), (3, 1024, 1024, "zyx"))
SCATTERS = ((3, 0, 1024, "x"), (3, 1024, 1024, "y"), (2, 0, 1024, "x"), (2, 1024, 1024, "y"), (1, 0, 512, "x"),
            (0, 0, 768, "y"), (0, 768, 768, "x"))


def whole_images(tokens, cotangent, w_qkv, wo_t, w_up, w_down_t, norm_gains, norm_shifts, qk_gains):
    zs = lax.axis_size("fsdp") // 4
    rows = w_qkv.shape[0]
    width = tokens.shape[2]
    cols = 3 * w_qkv.shape[2]
    side = jnp.concatenate([norm_gains, norm_shifts, jnp.zeros((rows, 124), BF16)], axis=1)
    shards = (jnp.concatenate([w_qkv.reshape(rows, cols), side], axis=1), wo_t, w_up, w_down_t)
    wholes, (image, cot) = gather_all(shards, (tokens, cotangent), GATHERS, zs, 0)
    qkv, out_w, up, down = (w.reshape(2, width, w.shape[5]) for w in wholes)
    norms = qkv[0, :, cols:cols + 4].T.astype(F32)
    gains = qk_gains.astype(F32)

    first, qn, kn, v, q_raw, k_raw = project(image, norms, jnp.tile(gains, (1, QKV_TILE // HD)), qkv, cols)
    mixed, inverse = attend(qn, kn, v)
    middle, second = branch(image, norms, mixed, out_w)
    result, grad_second, grad_up, grad_down = feed(second, cot, middle, up, down)
    grad_middle, grad_mixed, grad_out_w, sums_second = branch_back(norms, cot, grad_second, middle, mixed, out_w)
    grad_q, grad_k, grad_v, sums_qk = attend_back(
        jnp.tile(gains, (1, 2)), qn, kn, v, q_raw, k_raw, mixed, grad_mixed, inverse
    )
    grad_qkv, grad_image, sums_first = project_back(norms, image, first, grad_middle, grad_q, grad_k, grad_v, qkv, cols)

    sums_qk = jnp.pad((sums_qk[:, :HD] + sums_qk[:, HD:]).reshape(1, 2 * HD), ((0, 3), (0, width - 2 * HD)))
    small = jnp.concatenate([sums_first, sums_second, sums_qk], axis=0)
    grads = [g.reshape((2, zs, 2, 2, rows, g.shape[2])) for g in (grad_qkv, grad_out_w, grad_up, grad_down)]
    grads, (outputs, grad_tokens), small = scatter_all(grads, (result, grad_image), small, SCATTERS, zs, 1)
    mine = lax.dynamic_slice_in_dim(small, lax.axis_index("fsdp") * rows, rows, 1)
    return (
        outputs,
        grad_tokens.astype(F32),
        grads[0].reshape(w_qkv.shape),
        grads[1],
        grads[2],
        grads[3],
        jnp.stack([mine[0], mine[2]], 1),
        jnp.stack([mine[1], mine[3]], 1),
        small[4, :2 * HD].reshape(2, HD),
    )


def layer(tokens, *rest):
    if tokens.shape[0] == lax.axis_size("tensor") == 2 and lax.axis_size("fsdp") % 4 == 0:
        return whole_images(tokens, *rest)
    return per_device(tokens, *rest)


def solution(mesh):
    in_specs = (
        P("fsdp", "tensor", None),
        P("fsdp", "tensor", None),
        P("fsdp", None, "tensor"),
        P("fsdp", "tensor"),
        P("fsdp", "tensor"),
        P("fsdp", "tensor"),
        P("fsdp", None),
        P("fsdp", None),
        P(),
    )
    out_specs = (
        P("fsdp", "tensor", None),
        P("fsdp", "tensor", None),
        P("fsdp", None, "tensor"),
        P("fsdp", "tensor"),
        P("fsdp", "tensor"),
        P("fsdp", "tensor"),
        P("fsdp", None),
        P("fsdp", None),
        P(),
    )
    return jax.shard_map(
        layer, mesh=mesh, in_specs=in_specs, out_specs=out_specs, check_vma=False
    )
```

```python
import functools

import jax
import jax.numpy as jnp
from jax import lax
from jax.experimental import pallas as pl
from jax.experimental.pallas import tpu as pltpu
from jax.sharding import PartitionSpec as P

HD = 64


EPSILON = 1e-06


def norm_stats(value):
    center = value - jnp.mean(value, -1, keepdims=True)
    factor = lax.rsqrt(jnp.mean(center * center, -1, keepdims=True) + EPSILON)
    return (center * factor, factor)


def norm_back(grad_hat, normed, factor):
    return factor * (
        grad_hat
        - jnp.mean(grad_hat, -1, keepdims=True)
        - normed * jnp.mean(grad_hat * normed, -1, keepdims=True)
    )


def contract_rows(left, right):
    return lax.dot_general(
        left, right, (((0,), (0,)), ((), ())), preferred_element_type=jnp.float32
    )


def contract_cols(left, right):
    return lax.dot_general(
        left, right, (((1,), (1,)), ((), ())), preferred_element_type=jnp.float32
    )


def per_device(tokens, cotangent, w_qkv, wo_t, w_up, w_down_t, norm_gains, norm_shifts, qk_gains):
    local_rows = tokens.shape[1]
    width = tokens.shape[2]
    head_cols = w_qkv.shape[2]
    local_heads = head_cols // HD
    hidden_cols = w_up.shape[1]
    tensor_count = lax.axis_size("tensor")
    full_len = local_rows * tensor_count
    block = min(512, full_len)
    blocks = full_len // block
    gain_query = qk_gains[0].astype(jnp.float32)
    gain_keys = qk_gains[1].astype(jnp.float32)
    scale_query = HD ** (-0.5)

    def fetch():
        return (
            lax.all_gather(w_qkv, "fsdp", axis=0, tiled=True),
            lax.all_gather(wo_t, "fsdp", axis=0, tiled=True),
            lax.all_gather(w_up, "fsdp", axis=0, tiled=True),
            lax.all_gather(w_down_t, "fsdp", axis=0, tiled=True),
            lax.all_gather(norm_gains, "fsdp", axis=0, tiled=True),
            lax.all_gather(norm_shifts, "fsdp", axis=0, tiled=True),
        )

    def forward(weights, inputs):
        whole_qkv, whole_out, whole_up, whole_down, gains, shifts = weights
        gains = gains.astype(jnp.float32)
        shifts = shifts.astype(jnp.float32)
        flat_qkv = whole_qkv.reshape(width, 3 * head_cols)
        residual = inputs.astype(jnp.float32)
        first_hat, first_factor = norm_stats(residual)
        first = (first_hat * gains[:, 0] + shifts[:, 0]).astype(jnp.bfloat16)
        piece = lax.all_gather(first, "tensor", axis=0, tiled=True)
        first_full = piece
        joined = jnp.dot(piece, flat_qkv, preferred_element_type=jnp.float32)
        joined = joined.reshape(full_len, 3, local_heads, HD)
        query_hat, query_factor = norm_stats(joined[:, 0])
        keys_hat, keys_factor = norm_stats(joined[:, 1])
        query_n = (query_hat * gain_query * scale_query).astype(jnp.bfloat16)
        keys_n = (keys_hat * gain_keys).astype(jnp.bfloat16)
        values = joined[:, 2].astype(jnp.bfloat16)

        def attend(query_block):
            scores = jnp.einsum(
                "qhd,khd->hqk", query_block, keys_n, preferred_element_type=jnp.float32
            )
            largest = jnp.max(scores, -1, keepdims=True)
            exponent = jnp.exp(scores - largest)
            total_sum = jnp.sum(exponent, -1, keepdims=True)
            probs_low = (exponent / total_sum).astype(jnp.bfloat16)
            mixed_block = jnp.einsum(
                "hqk,khd->qhd", probs_low, values, preferred_element_type=jnp.float32
            )
            return (mixed_block.astype(jnp.bfloat16), (largest + jnp.log(total_sum))[..., 0])

        mixed, log_total = lax.map(attend, query_n.reshape(blocks, block, local_heads, HD))
        mixed = mixed.reshape(full_len, head_cols)
        middle = residual + lax.psum_scatter(
            contract_cols(mixed, whole_out), "tensor", scatter_dimension=0, tiled=True
        )
        second_hat, second_factor = norm_stats(middle)
        second = (second_hat * gains[:, 1] + shifts[:, 1]).astype(jnp.bfloat16)
        piece = lax.all_gather(second, "tensor", axis=0, tiled=True)
        hidden = jnp.dot(piece, whole_up, preferred_element_type=jnp.float32)
        active = jax.nn.gelu(hidden, approximate=False).astype(jnp.bfloat16)
        result = (
            middle
            + lax.psum_scatter(
                contract_cols(active, whole_down).astype(jnp.bfloat16),
                "tensor",
                scatter_dimension=0,
                tiled=True,
            ).astype(jnp.float32)
        ).astype(jnp.bfloat16)
        kept = (
            first_hat,
            first_factor,
            first_full,
            query_hat,
            query_factor,
            keys_hat,
            keys_factor,
            query_n,
            keys_n,
            values,
            mixed,
            log_total,
            second_hat,
            second_factor,
            piece,
            hidden,
            active,
        )
        return (kept, result)

    def backward(weights, kept, grad_out):
        whole_qkv, whole_out, whole_up, whole_down, gains, shifts = weights
        gains = gains.astype(jnp.float32)
        flat_qkv = whole_qkv.reshape(width, 3 * head_cols)
        (
            first_hat,
            first_factor,
            first_full,
            query_hat,
            query_factor,
            keys_hat,
            keys_factor,
            query_n,
            keys_n,
            values,
            mixed_keep,
            log_total,
            second_hat,
            second_factor,
            second_full,
            hidden,
            active,
        ) = kept
        piece = lax.all_gather(grad_out, "tensor", axis=0, tiled=True)
        grad_full = piece
        grad_active = jnp.dot(piece, whole_down, preferred_element_type=jnp.float32)
        grad_down = contract_rows(grad_full, active)
        unused_value, gelu_pull = jax.vjp(
            lambda value: jax.nn.gelu(value, approximate=False), hidden
        )
        grad_hidden = gelu_pull(grad_active)[0].astype(jnp.bfloat16)
        grad_up = contract_rows(second_full, grad_hidden)
        grad_second = lax.psum_scatter(
            contract_cols(grad_hidden, whole_up), "tensor", scatter_dimension=0, tiled=True
        )
        grad_middle = grad_out.astype(jnp.float32) + norm_back(
            grad_second * gains[:, 1], second_hat, second_factor
        )
        grad_branch = grad_middle.astype(jnp.bfloat16)
        piece = lax.all_gather(grad_branch, "tensor", axis=0, tiled=True)
        grad_mixed = jnp.dot(piece, whole_out, preferred_element_type=jnp.float32)
        grad_out_w = contract_rows(piece, mixed_keep)
        grad_mixed = grad_mixed.astype(jnp.bfloat16)
        grad_mixed = grad_mixed.reshape(blocks, block, local_heads, HD)

        def attend_back(carry, item):
            grad_keys_sum, grad_values_sum = carry
            query_block, grad_block, log_block = item
            scores = jnp.einsum(
                "qhd,khd->hqk", query_block, keys_n, preferred_element_type=jnp.float32
            )
            probs = jnp.exp(scores - log_block[..., None])
            grad_probs = jnp.einsum(
                "qhd,khd->hqk", grad_block, values, preferred_element_type=jnp.float32
            )
            delta = jnp.sum(probs * grad_probs, -1, keepdims=True)
            grad_scores = (probs * (grad_probs - delta)).astype(jnp.bfloat16)
            grad_query_block = jnp.einsum(
                "hqk,khd->qhd", grad_scores, keys_n, preferred_element_type=jnp.float32
            )
            grad_keys_sum = grad_keys_sum + jnp.einsum(
                "hqk,qhd->khd", grad_scores, query_block, preferred_element_type=jnp.float32
            )
            grad_values_sum = grad_values_sum + jnp.einsum(
                "hqk,qhd->khd",
                probs.astype(jnp.bfloat16),
                grad_block,
                preferred_element_type=jnp.float32,
            )
            return ((grad_keys_sum, grad_values_sum), grad_query_block)

        empty_heads = jnp.zeros((full_len, local_heads, HD), jnp.float32)
        (grad_keys_n, grad_values), grad_query_n = lax.scan(
            attend_back,
            (empty_heads, empty_heads),
            (query_n.reshape(blocks, block, local_heads, HD), grad_mixed, log_total),
        )
        grad_query_n = grad_query_n.reshape(full_len, local_heads, HD)
        grad_query = norm_back(grad_query_n * gain_query * scale_query, query_hat, query_factor)
        grad_keys = norm_back(grad_keys_n * gain_keys, keys_hat, keys_factor)
        qk_grad = jnp.stack(
            [
                jnp.sum(grad_query_n * query_hat * scale_query, (0, 1)),
                jnp.sum(grad_keys_n * keys_hat, (0, 1)),
            ]
        )
        grad_joined = jnp.stack([grad_query, grad_keys, grad_values], 1).astype(jnp.bfloat16)
        grad_joined = grad_joined.reshape(full_len, 3 * head_cols)
        grad_qkv = contract_rows(first_full, grad_joined).reshape(width, 3, head_cols)
        grad_first = lax.psum_scatter(
            contract_cols(grad_joined, flat_qkv).astype(jnp.bfloat16),
            "tensor",
            scatter_dimension=0,
            tiled=True,
        ).astype(jnp.float32)
        grad_input = grad_middle + norm_back(grad_first * gains[:, 0], first_hat, first_factor)
        gain_grad = jnp.stack(
            [jnp.sum(grad_first * first_hat, 0), jnp.sum(grad_second * second_hat, 0)], 1
        )
        shift_grad = jnp.stack([jnp.sum(grad_first, 0), jnp.sum(grad_second, 0)], 1)
        return (
            (grad_qkv, grad_out_w, grad_up, grad_down, gain_grad, shift_grad, qk_grad),
            grad_input,
        )

    def micro_step(totals, item):
        inputs, grad_out = item
        forward_weights = fetch()
        kept, result = forward(forward_weights, inputs)
        backward_weights = fetch()
        grads, grad_input = backward(backward_weights, kept, grad_out)
        totals = tuple((total + part for total, part in zip(totals, grads)))
        return (totals, (result, grad_input))

    out_cols_count = wo_t.shape[1]
    start_sums = (
        jnp.zeros((width, 3, head_cols), jnp.float32),
        jnp.zeros((width, out_cols_count), jnp.float32),
        jnp.zeros((width, hidden_cols), jnp.float32),
        jnp.zeros((width, hidden_cols), jnp.float32),
        jnp.zeros((width, 2), jnp.float32),
        jnp.zeros((width, 2), jnp.float32),
        jnp.zeros((2, HD), jnp.float32),
    )
    totals, (outputs, grad_tokens) = lax.scan(micro_step, start_sums, (tokens, cotangent))
    out_total = totals[1]
    grad_qkv, grad_out_w, grad_up, grad_down = (
        lax.psum_scatter(
            totals[0].astype(jnp.bfloat16), "fsdp", scatter_dimension=0, tiled=True
        ).astype(jnp.float32),
        lax.psum_scatter(
            out_total.astype(jnp.bfloat16), "fsdp", scatter_dimension=0, tiled=True
        ).astype(jnp.float32),
        lax.psum_scatter(
            totals[2].astype(jnp.bfloat16), "fsdp", scatter_dimension=0, tiled=True
        ).astype(jnp.float32),
        lax.psum_scatter(
            totals[3].astype(jnp.bfloat16), "fsdp", scatter_dimension=0, tiled=True
        ).astype(jnp.float32),
    )
    gain_total, shift_total, qk_total = lax.psum(
        (totals[4], totals[5], totals[6]), ("fsdp", "tensor")
    )
    own_rows = width // lax.axis_size("fsdp")
    offset = lax.axis_index("fsdp") * own_rows
    gain_part = lax.dynamic_slice_in_dim(gain_total, offset, own_rows, 0)
    shift_part = lax.dynamic_slice_in_dim(shift_total, offset, own_rows, 0)
    return (
        outputs,
        grad_tokens,
        grad_qkv,
        grad_out_w,
        grad_up,
        grad_down,
        gain_part,
        shift_part,
        qk_total,
    )


PAIR = 2 * HD
F32, BF16 = jnp.float32, jnp.bfloat16
LIMIT = 60 << 20


def nn(a, b):
    return lax.dot_general(a, b, (((1,), (0,)), ((), ())), preferred_element_type=F32)


def nt(a, b):
    return lax.dot_general(a, b, (((1,), (1,)), ((), ())), preferred_element_type=F32)


def stats(value):
    center = value - jnp.mean(value, -1, keepdims=True)
    factor = lax.rsqrt(jnp.mean(center * center, -1, keepdims=True) + EPSILON)
    return center * factor, factor


def back(grad_hat, normed, factor):
    return factor * (
        grad_hat
        - jnp.mean(grad_hat, -1, keepdims=True)
        - normed * jnp.mean(grad_hat * normed, -1, keepdims=True)
    )


def head_mean_matrix(width):
    row = lax.broadcasted_iota(jnp.int32, (width, width), 0) // HD
    col = lax.broadcasted_iota(jnp.int32, (width, width), 1) // HD
    return jnp.where(row == col, 1.0 / HD, 0.0).astype(BF16)


def head_mean(value, matrix):
    high = value.astype(BF16)
    low = (value - high.astype(F32)).astype(BF16)
    return nn(high, matrix) + nn(low, matrix)


def head_stats(value, matrix):
    center = value - head_mean(value, matrix)
    factor = lax.rsqrt(head_mean(center * center, matrix) + EPSILON)
    return center * factor, factor


def head_back(grad_hat, normed, factor, matrix):
    return factor * (
        grad_hat - head_mean(grad_hat, matrix) - normed * head_mean(grad_hat * normed, matrix)
    )


MESH = pl.DeviceIdType.MESH
ALL = slice(None)


class Place:
    def __init__(self, zs):
        f = lax.axis_index("fsdp")
        self.zs = zs
        self.x = lax.axis_index("tensor")
        self.c = lax.rem(f, 2)
        self.y = lax.rem(lax.div(f, 2), 2)
        self.z = lax.div(f, 4)

    def dev(self, z=None, y=None, c=None, x=None):
        z = self.z if z is None else z
        y = self.y if y is None else y
        c = self.c if c is None else c
        x = self.x if x is None else x
        return {"fsdp": (z * 2 + y) * 2 + c, "tensor": x}

    def along_z(self):
        return [lax.rem(self.z + k, self.zs) for k in range(1, self.zs)]

    def peers(self):
        out = [self.dev(z=z) for z in self.along_z()]
        return out + [self.dev(y=1 - self.y), self.dev(c=1 - self.c), self.dev(x=1 - self.x)]


def meet(place):
    barrier = pltpu.get_barrier_semaphore()
    peers = place.peers()
    for peer in peers:
        pl.semaphore_signal(barrier, inc=1, device_id=peer, device_id_type=MESH)
    pl.semaphore_wait(barrier, len(peers))


def remote(src, dst, send, recv, peer):
    return pltpu.make_async_remote_copy(
        src_ref=src, dst_ref=dst, send_sem=send, recv_sem=recv, device_id=peer, device_id_type=MESH
    )


def start(*copies):
    for copy in copies:
        copy.start()


def wait(*copies):
    for copy in copies:
        copy.wait()


class Gather:
    def __init__(self, place, shard, whole, lo, size, order, send, recv):
        p = self.p = place
        cols = self.cols = pl.ds(lo, size)
        self.shard = None if shard is None else shard.at[:, cols]
        self.whole = whole
        self.order = order
        self.send, self.recv = send, recv
        if shard is not None:
            self.own = pltpu.make_async_copy(self.shard, self.at({}), self.send.at[2 * p.zs + 7])

    def at(self, index):
        p = self.p
        own = {"x": p.x, "y": p.y, "z": p.z}
        x, y, z = (index.get(d, own[d]) for d in "xyz")
        return self.whole.at[x, z, y, p.c, :, self.cols]

    def others(self, d):
        return self.p.along_z() if d == "z" else [1 - getattr(self.p, d)]

    def copies(self, base, i, pairs):
        base += sum(len(self.others(d)) for d in self.order[:i])
        return [remote(src, dst, self.send.at[base + k], self.recv.at[base + k], peer) for k, (src, dst, peer) in enumerate(pairs)]

    def stage(self, i):
        d = self.order[i]
        held = self.at({e: ALL for e in self.order[:i]})
        src = self.shard if i == 0 else held
        return self.copies(0, i, [(src, held, self.p.dev(**{d: to})) for to in self.others(d)])

    def core_parts(self, i):
        done = {e: ALL for e in self.order[:i]}
        d = self.order[i]
        if i == 0:
            refs = [self.at({d: ALL})]
        else:
            refs = [self.at({**done, d: to}) for to in self.others(d)]
        peer = self.p.dev(c=1 - self.p.c)
        return self.copies(self.p.zs + 1, i, [(ref, ref, peer) for ref in refs])

    def begin(self):
        start(self.own, *self.stage(0))

    def begun(self):
        wait(self.own, *self.stage(0))

    def go(self, i):
        if i < 3:
            start(*self.stage(i))
        start(*self.core_parts(i - 1))

    def came(self, i):
        wait(*self.stage(i))

    def rest(self, *parts):
        for i in parts:
            wait(*self.core_parts(i))


def gather_sems(zs):
    return 2 * zs + 8


class Swap:
    def __init__(self, place, value, image, sems):
        p = place
        half = value.shape[1]
        rows = pl.ds(pl.multiple_of(p.x * half, half), half)
        self.copy = remote(value.at[1 - p.x], image.at[rows], sems.at[0], sems.at[1], p.dev(x=1 - p.x))
        self.mine = pltpu.make_async_copy(value.at[p.x], image.at[rows], sems.at[2])


class SwapBack:
    def __init__(self, place, value, out, sems):
        p = place
        half = out.shape[1]
        to = pl.ds(pl.multiple_of((1 - p.x) * half, half), half)
        rows = pl.ds(pl.multiple_of(p.x * half, half), half)
        self.copy = remote(value.at[to], out.at[p.x], sems.at[0], sems.at[1], p.dev(x=1 - p.x))
        self.mine = pltpu.make_async_copy(value.at[rows], out.at[p.x], sems.at[2])


class Sum:
    def __init__(self, place, total, got, send, recv):
        self.p, self.total, self.got, self.send, self.recv = place, total, got, send, recv

    def copies(self, i):
        p = self.p
        if i < 3:
            peers = [(p.dev(c=1 - p.c), p.dev(x=1 - p.x), p.dev(y=1 - p.y))[i]]
        else:
            peers = [p.dev(z=z) for z in p.along_z()]
        return [remote(self.total, self.got.at[i + k], self.send.at[i + k], self.recv.at[i + k], peer)
                for k, peer in enumerate(peers)]

    def go(self, i):
        start(*self.copies(i))

    def add(self, i):
        copies = self.copies(i)
        wait(*copies)
        total = self.total[...]
        for k in range(len(copies)):
            total = total + self.got[i + k]
        self.total[...] = total


def add_slabs(count, pair):
    def body(i, _):
        into, from_ = pair(i)
        into[...] = into[...] + from_[...]
        return 0
    lax.fori_loop(0, count, body, 0)


class Scatter:
    def __init__(self, place, order, held, away, b, b1, b2, b3, send, recv):
        self.p, self.order, self.held, self.away = place, order, held, away
        self.b, self.b1, self.b2, self.b3 = b, b1, b2, b3
        self.send, self.recv = send, recv

    def copy(self, n, src, dst, peer):
        return remote(src, dst, self.send.at[n], self.recv.at[n], peer)

    def core(self):
        return self.copy(0, self.away, self.b, self.p.dev(c=1 - self.p.c))

    def core_add(self):
        zs = self.p.zs
        wait(self.core())

        def pair(j):
            x, z, y = lax.div(j, 2 * zs), lax.rem(lax.div(j, 2), zs), lax.rem(j, 2)
            return self.held(x, z, y), self.b.at[x, z, y]
        add_slabs(4 * zs, pair)

    def first(self):
        p = self.p
        if self.order == "x":
            return self.copy(1, self.held(1 - p.x, ALL, ALL), self.b1, p.dev(x=1 - p.x))
        return self.copy(1, self.held(ALL, ALL, 1 - p.y), self.b1, p.dev(y=1 - p.y))

    def first_add(self):
        p, zs = self.p, self.p.zs
        wait(self.first())

        def pair(j):
            if self.order == "x":
                z, y = lax.div(j, 2), lax.rem(j, 2)
                return self.held(p.x, z, y), self.b1.at[z, y]
            x, z = lax.div(j, zs), lax.rem(j, zs)
            return self.held(x, z, p.y), self.b1.at[x, z]
        add_slabs(2 * zs, pair)

    def state(self):
        p = self.p
        return self.held(p.x, ALL, ALL) if self.order == "x" else self.held(ALL, ALL, p.y)

    def second(self):
        p = self.p
        if self.order == "x":
            return self.copy(2, self.held(p.x, ALL, 1 - p.y), self.b2, p.dev(y=1 - p.y))
        return self.copy(2, self.held(1 - p.x, ALL, p.y), self.b2, p.dev(x=1 - p.x))

    def second_add(self):
        p = self.p
        wait(self.second())
        add_slabs(p.zs, lambda z: (self.held(p.x, z, p.y), self.b2.at[z]))

    def last(self):
        p = self.p
        return [self.copy(3 + k, self.held(p.x, to, p.y), self.b3.at[k], p.dev(z=to)) for k, to in enumerate(p.along_z())]

    def finish(self, out):
        p = self.p
        wait(*self.last())
        value = self.held(p.x, p.z, p.y)[...].astype(F32)
        for k in range(p.zs - 1):
            value = value + self.b3[k].astype(F32)
        out[...] = value


def scatter_sems(zs):
    return zs + 2


def landing(zs, rows, m, order, stages="0123"):
    shapes = [(2, zs, 2, rows, m), (zs, 2, rows, m) if order == "x" else (2, zs, rows, m), (zs, rows, m), (zs - 1, rows, m)]
    return [pltpu.VMEM(shapes[int(i)], BF16) for i in stages]


def state_shape(zs, rows, m, order):
    return (zs, 2, rows, m) if order == "x" else (2, zs, rows, m)


def on(step, hooks):
    for at, hook in hooks.items():
        pl.when(step == at)(hook)


HBM = pl.BlockSpec(memory_space=pl.ANY)
WHOLE_VMEM = pl.BlockSpec(memory_space=pltpu.VMEM)
DMA = pltpu.SemaphoreType.DMA


def params(collective_id):
    return pltpu.CompilerParams(collective_id=collective_id, has_side_effects=True, vmem_limit_bytes=LIMIT)


Q_GROUPS = ((0, 384, "zyx"), (384, 384, "zxy"), (768, 512, "zxy"), (1280, 384, "zxy"))
FF_GROUP = 512


def opening_body(zs, q, o, u, d, tokens, whole_q, whole_o, whole_u, whole_d, image, send, recv, swap_sem):
    p = Place(zs)
    meet(p)
    swap = Swap(p, tokens, image, swap_sem)
    a, b, c, e = (Gather(p, q, whole_q, lo, n, order, send.at[i], recv.at[i]) for i, (lo, n, order) in enumerate(Q_GROUPS))
    others = [(o, whole_o, 0), (u, whole_u, 0), (d, whole_d, 0), (u, whole_u, 1), (d, whole_d, 1)]
    later = [Gather(p, s, w, j * FF_GROUP, FF_GROUP, "zxy", send.at[4 + i], recv.at[4 + i]) for i, (s, w, j) in enumerate(others)]
    start(swap.copy, swap.mine)
    a.begin()
    b.begin()
    a.begun()
    a.go(1)
    c.begin()
    b.begun()
    b.go(1)
    e.begin()
    a.came(1)
    a.go(2)
    b.came(1)
    b.go(2)
    c.begun()
    c.go(1)
    for g in later[:3]:
        g.begin()
    e.begun()
    e.go(1)
    for g in later[3:]:
        g.begin()
    c.came(1)
    c.go(2)
    e.came(1)
    e.go(2)
    for g in (a, b, c, e):
        g.came(2)
        g.go(3)
    for g in later:
        g.begun()
    wait(swap.copy, swap.mine)
    for g in (a, b, c, e):
        g.rest(0, 1, 2)


def opening(q, o, u, d, tokens, zs):
    whole = lambda s: jax.ShapeDtypeStruct((2, zs, 2, 2) + s.shape, s.dtype)
    return pl.pallas_call(
        functools.partial(opening_body, zs),
        out_shape=[whole(q), whole(o), whole(u), whole(d), jax.ShapeDtypeStruct((2 * tokens.shape[1], tokens.shape[2]), BF16)],
        in_specs=[HBM] * 5,
        out_specs=[HBM] * 5,
        scratch_shapes=[DMA((9, gather_sems(zs))), DMA((9, gather_sems(zs))), DMA((3,))],
        compiler_params=params(0),
        name="opening",
    )(q, o, u, d, tokens)


QKV_TILE = 256
Q_TILE = 256
ROWS = 256


def full(shape):
    return pl.BlockSpec(shape, lambda s: (0,) * len(shape), pipeline_mode=pl.Buffered(1))


def clipped(shape, axis, first, count):
    def at(s):
        i = jnp.clip(s - first, 0, count - 1)
        return (i, 0) if axis == 0 else (0, i)
    return pl.BlockSpec(shape, at)


def project_step(step, per_part, joined, gains, kept, blocks):
    part = lax.div(step, per_part)
    tile = lax.rem(step, per_part)
    matrix = head_mean_matrix(QKV_TILE)
    cols = pl.ds(pl.multiple_of(tile * QKV_TILE, QKV_TILE), QKV_TILE)
    qn_s, kn_s, v_s = kept
    qn, kn, v, q_raw, k_raw = blocks

    @pl.when(part == 0)
    def _():
        hat, _f = head_stats(joined, matrix)
        value = (hat * gains[0:1] * (HD ** -0.5)).astype(BF16)
        qn[...] = value
        qn_s[:, cols] = value
        q_raw[...] = joined.astype(BF16)

    @pl.when(part == 1)
    def _():
        hat, _f = head_stats(joined, matrix)
        value = (hat * gains[1:2]).astype(BF16)
        kn[...] = value
        kn_s[:, cols] = value
        k_raw[...] = joined.astype(BF16)

    @pl.when(part == 2)
    def _():
        value = joined.astype(BF16)
        v[...] = value
        v_s[:, cols] = value


def attend_step(query_all, keys, values, mixed_s, cols, mixed, inverse):
    length = keys.shape[0]
    lane = lax.broadcasted_iota(jnp.int32, (1, PAIR), 1) < HD
    values = jnp.concatenate([values, jnp.ones((length, PAIR), BF16)], axis=1)
    zero = jnp.zeros((), BF16)
    for i in range(length // Q_TILE):
        at = slice(i * Q_TILE, (i + 1) * Q_TILE)
        query = query_all[at]
        got = []
        for mask in (lane, ~lane):
            scores = nt(jnp.where(mask, query, zero), keys)
            got.append(nn(jnp.exp(scores).astype(BF16), values))
        inv = 1.0 / jnp.where(lane, got[0][:, PAIR:], got[1][:, PAIR:])
        value = (jnp.where(lane, got[0][:, :PAIR], got[1][:, :PAIR]) * inv).astype(BF16)
        mixed[at] = value
        mixed_s[at, cols] = value
        inverse[at] = inv


def attention_body(
    zs, per_part, pairs, image, norms, gains, w, cot_in, u, d, _o, _u, _d,
    first, qn, kn, v, q_raw, k_raw, mixed, inverse, middle, second, cot, whole_o, whole_u, whole_d,
    held, qn_s, kn_s, v_s, mixed_s, out_w, send, recv, swap_sem,
):
    step = pl.program_id(0)
    p = Place(zs)
    length = image.shape[0]
    head0, row0 = 3 * per_part, 3 * per_part + pairs
    n = FF_GROUP
    swap = Swap(p, cot_in, cot, swap_sem)
    o = Gather(p, None, whole_o, 0, whole_o.shape[5], "zxy", send.at[0], recv.at[0])
    u0 = Gather(p, None, whole_u, 0, n, "zxy", send.at[1], recv.at[1])
    d0 = Gather(p, None, whole_d, 0, n, "zyx", send.at[2], recv.at[2])
    u1 = Gather(p, None, whole_u, n, n, "zxy", send.at[3], recv.at[3])
    d1 = Gather(p, None, whole_d, n, n, "zxy", send.at[4], recv.at[4])
    nexts = [Gather(p, s, t, j * n, n, "zxy", send.at[5 + i], recv.at[5 + i])
             for i, (s, t, j) in enumerate(((u, whole_u, 2), (d, whole_d, 2), (u, whole_u, 3), (d, whole_d, 3)))]
    load = pltpu.make_async_copy(whole_o, out_w, swap_sem.at[3])

    def h0():
        meet(p)
        o.go(1)
        d0.go(1)
        nexts[0].begin()
        nexts[1].begin()

    def h3():
        o.came(1)
        o.go(2)
        d0.came(1)
        u0.go(1)

    def h6():
        u0.came(1)
        u0.go(2)
        u1.go(1)
        d0.go(2)

    def h9():
        u1.came(1)
        u1.go(2)
        d1.go(1)
        nexts[2].begin()
        nexts[3].begin()

    def h12():
        d1.came(1)
        d1.go(2)
        start(swap.copy, swap.mine)

    def h15():
        o.came(2)
        o.go(3)

    def h18():
        u0.came(2)
        u0.go(3)
        o.rest(0, 1, 2)
        load.start()

    def h19():
        d0.came(2)
        d0.go(3)

    def h20():
        load.wait()

    def h22():
        u1.came(2)
        u1.go(3)

    on(step, {0: h0, 3: h3, 6: h6, 9: h9, 12: h12, 15: h15, 18: h18, 19: h19, 20: h20, 22: h22})

    @pl.when(step == 0)
    def _():
        rows = length // 4

        def norm(i, _):
            at = pl.ds(i * rows, rows)
            hat, _f = stats(image[at].astype(F32))
            value = (hat * norms[0:1] + norms[2:3]).astype(BF16)
            held[at] = value
            first[at] = value
            return 0
        lax.fori_loop(0, 4, norm, 0)

    @pl.when(step < head0)
    def _():
        project_step(step, per_part, nn(held[...], w[0]), gains, (qn_s, kn_s, v_s), (qn, kn, v, q_raw, k_raw))

    @pl.when((step >= head0) & (step < row0))
    def _():
        cols = pl.ds(pl.multiple_of((step - head0) * PAIR, PAIR), PAIR)
        attend_step(qn_s[:, cols], kn_s[:, cols], v_s[:, cols], mixed_s, cols, mixed, inverse)

    @pl.when(step >= row0)
    def _():
        at = pl.ds(pl.multiple_of((step - row0) * ROWS, ROWS), ROWS)
        half = out_w.shape[5]
        w0, w1 = (out_w[t].reshape(-1, half) for t in range(2))
        value = image[at].astype(F32) + nt(mixed_s[at, :half], w0) + nt(mixed_s[at, half:], w1)
        middle[...] = value
        hat, _f = stats(value)
        second[...] = (hat * norms[1:2] + norms[3:4]).astype(BF16)

    @pl.when(step == pl.num_programs(0) - 1)
    def _():
        d1.came(2)
        d1.go(3)
        for g in nexts:
            g.begun()
        wait(swap.copy, swap.mine)
        for g in (u0, d0, u1, d1):
            g.rest(0, 1, 2)


def attention(image, norms, gains, w, cols, cot, u, d, whole_o, whole_u, whole_d, zs):
    length, width = image.shape
    half = cols // 3
    per_half = half // QKV_TILE
    per_part = 2 * per_half
    pairs = 2 * half // PAIR
    head0, row0 = 3 * per_part, 3 * per_part + pairs
    steps = row0 + length // ROWS

    def w_map(s):
        s = jnp.minimum(s, head0 - 1)
        part, rest = s // per_part, s % per_part
        return rest // per_half, 0, part * per_half + rest % per_half

    tiles = lambda part: clipped((length, QKV_TILE), 1, part * per_part, per_part)
    heads = clipped((length, PAIR), 1, head0, pairs)
    rows = clipped((ROWS, width), 0, row0, length // ROWS)
    bf = jax.ShapeDtypeStruct((length, 2 * half), BF16)
    same = lambda a: jax.ShapeDtypeStruct(a.shape, a.dtype)
    store = pltpu.VMEM((length, 2 * half), BF16)
    return pl.pallas_call(
        functools.partial(attention_body, zs, per_part, pairs),
        grid=(steps,),
        in_specs=[full(image.shape), full(norms.shape), full(gains.shape), pl.BlockSpec((1, width, QKV_TILE), w_map)] + [HBM] * 6,
        out_specs=[full((length, width)), tiles(0), tiles(1), tiles(2), tiles(0), tiles(1), heads, heads, rows, rows] + [HBM] * 4,
        out_shape=[same(image), bf, bf, bf, bf, bf, bf, jax.ShapeDtypeStruct((length, 2 * half), F32),
                   jax.ShapeDtypeStruct((length, width), F32), same(image), same(image), same(whole_o), same(whole_u), same(whole_d)],
        scratch_shapes=[pltpu.VMEM((length, width), BF16), store, store, store, store, pltpu.VMEM(whole_o.shape, BF16),
                        DMA((9, gather_sems(zs))), DMA((9, gather_sems(zs))), DMA((4,))],
        input_output_aliases={7: 11, 8: 12, 9: 13},
        compiler_params=params(1),
        name="attention",
    )(image, norms, gains, w, cot, u, d, whole_o, whole_u, whole_d)


def gelu_parts(v):
    bell = jnp.exp(v * v * -0.5)
    t = 1.0 / (1.0 + (0.3275911 * 0.7071067811865476) * jnp.abs(v))
    poly = t * (0.127414796 + t * (-0.142248368 + t * (0.7107068705 + t * (-0.7265760135 + t * 0.5307027145))))
    tail = poly * bell
    return jnp.where(v >= 0, 1.0 - tail, tail), bell * 0.3989422804014327


FEED_ORDERS = ("y", "x")


def feed_body(
    zs, second, cot, middle, _u, _d,
    result, grad_second, grad_u, grad_d, state_u, state_d, whole_u, whole_d,
    acc, second_t, cot_t, active, grad_hidden, tiles, g, tile_sem, misc_sem, send, recv, *landings,
):
    step = pl.program_id(0)
    p = Place(zs)
    length = second.shape[0]
    n = FF_GROUP
    u2 = Gather(p, None, whole_u, 2 * n, n, "zxy", send.at[0], recv.at[0])
    d2 = Gather(p, None, whole_d, 2 * n, n, "zyx", send.at[1], recv.at[1])
    u3 = Gather(p, None, whole_u, 3 * n, n, "zxy", send.at[2], recv.at[2])
    d3 = Gather(p, None, whole_d, 3 * n, n, "zyx", send.at[3], recv.at[3])
    groups = []
    for j in range(2):
        for k in range(2):
            i = 2 * j + k
            held = lambda x, z, y, j=j, k=k: g.at[k, j, x, z, y, p.c]
            groups.append(Scatter(p, FEED_ORDERS[k], held, g.at[k, j, :, :, :, 1 - p.c], *landings[2 * i:2 * i + 2], None, None,
                                  send.at[4 + i], recv.at[4 + i]))
    su0, sd0, su1, sd1 = groups
    init = pltpu.make_async_copy(middle, acc, misc_sem.at[0])
    states = [pltpu.make_async_copy(s.state(), (state_u, state_d)[k].at[j], misc_sem.at[1 + 2 * j + k])
              for j in range(2) for k, s in ((0, groups[2 * j]), (1, groups[2 * j + 1]))]
    outs = [pltpu.make_async_copy(g.at[k, j], (grad_u, grad_d)[k].at[j - 2], misc_sem.at[5 + 2 * (j - 2) + k])
            for j in (2, 3) for k in range(2)]

    def loads(s):
        j, t = (s // 2, s % 2) if isinstance(s, int) else (lax.div(s, 2), lax.rem(s, 2))
        slot = t
        cols = pl.ds(j * n if isinstance(s, int) else pl.multiple_of(j * n, n), n)
        return [pltpu.make_async_copy(w.at[t, :, :, :, :, cols], tiles.at[k, slot], tile_sem.at[k, slot])
                for k, w in ((0, whole_u), (1, whole_d))]

    @pl.when(step == 0)
    def _():
        meet(p)
        start(*loads(0))
        start(*loads(1))
        init.start()
        for w in (u2, d2, u3, d3):
            w.go(1)
        second_t[...] = second[...].T
        cot_t[...] = cot[...].T
        grad_second[...] = jnp.zeros_like(grad_second)

    def h1():
        start(*loads(2))
        for w in (u2, d2):
            w.came(1)
            w.go(2)

    def h2():
        start(*loads(3))
        start(su0.core(), sd0.core())
        for w in (u3, d3):
            w.came(1)
            w.go(2)

    def h3():
        su0.core_add()
        sd0.core_add()
        start(su0.first(), sd0.first())
        for w in (u2, d2):
            w.came(2)
            w.go(3)

    def h4():
        for w in (u2, d2):
            w.rest(0, 1, 2)
        start(*loads(4))
        start(*loads(5))
        start(su1.core(), sd1.core())
        for w in (u3, d3):
            w.came(2)
            w.go(3)

    def h5():
        for w in (u3, d3):
            w.rest(0, 1, 2)
        start(*loads(6))
        su1.core_add()
        sd1.core_add()
        start(su1.first(), sd1.first())

    def h6():
        start(*loads(7))
        su0.first_add()
        sd0.first_add()
        start(*states[:2])
        start(*outs[:2])

    on(step, {1: h1, 2: h2, 3: h3, 4: h4, 5: h5, 6: h6})
    wait(*loads(step))

    @pl.when(step == 0)
    def _():
        init.wait()
    slot = lax.rem(step, 2)
    w_up = tiles[0, slot].reshape(-1, n)
    w_down = tiles[1, slot].reshape(-1, n)
    for i in range(length // ROWS):
        at = slice(i * ROWS, (i + 1) * ROWS)
        hidden = nn(second[at], w_up)
        grad_active = nn(cot[at], w_down)
        cumulative, density = gelu_parts(hidden)
        a = (hidden * cumulative).astype(BF16)
        b = (grad_active * (cumulative + hidden * density)).astype(BF16)
        active[at] = a
        grad_hidden[at] = b
        acc[at] += nt(a, w_down)
        grad_second[at] += nt(b, w_up)
    j, t = lax.div(step, 2), lax.rem(step, 2)
    shape = g.shape[3:]
    g[0, j, t] = nn(second_t[...], grad_hidden[...]).astype(BF16).reshape(shape)
    g[1, j, t] = nn(cot_t[...], active[...]).astype(BF16).reshape(shape)

    @pl.when(step == pl.num_programs(0) - 1)
    def _():
        start(*outs[2:])
        result[...] = acc[...].astype(BF16)
        su1.first_add()
        sd1.first_add()
        start(*states[2:])
        wait(*states)
        wait(*outs)


def feed(second, cot, middle, whole_u, whole_d, zs):
    length, width = second.shape
    rows, n = whole_u.shape[4], FF_GROUP
    same = lambda a: jax.ShapeDtypeStruct(a.shape, a.dtype)
    tile = (2, zs, 2, 2, rows, n)
    grads = jax.ShapeDtypeStruct((2,) + tile, BF16)
    square = pltpu.VMEM((length, width), BF16)
    strip = pltpu.VMEM((length, n), BF16)
    scratch = [pltpu.VMEM((length, width), F32), square, square, strip, strip, pltpu.VMEM((2, 2) + tile[1:], BF16),
               pltpu.VMEM((2, 4) + tile, BF16), DMA((2, 2)), DMA((9,)), DMA((8, gather_sems(zs))), DMA((8, gather_sems(zs)))]
    for i in range(4):
        scratch += landing(zs, rows, n, FEED_ORDERS[i % 2], "01")
    return pl.pallas_call(
        functools.partial(feed_body, zs),
        grid=(8,),
        in_specs=[full(second.shape), full(cot.shape), HBM, HBM, HBM],
        out_specs=[full(second.shape), full(second.shape)] + [HBM] * 6,
        out_shape=[same(second), jax.ShapeDtypeStruct((length, width), F32), grads, grads]
        + [jax.ShapeDtypeStruct((2,) + state_shape(zs, rows, n, o), BF16) for o in FEED_ORDERS]
        + [same(whole_u), same(whole_d)],
        scratch_shapes=scratch,
        input_output_aliases={3: 6, 4: 7},
        compiler_params=params(2),
        name="feed",
    )(second, cot, middle, whole_u, whole_d)


LATE_ORDERS = ("x", "y", "y", "y")


def attend_back_step(gains, go, inv, query, keys, values, q_raw, k_raw, mixed, grad_q, grad_k, grad_v, grad_gains):
    length = query.shape[0]
    lanes = lax.broadcasted_iota(jnp.int32, (1, PAIR), 1)
    first = lanes < HD
    zero = jnp.zeros((), BF16)
    go = go.astype(F32)
    product = go * mixed.astype(F32) * inv
    go_inv = (go * inv).astype(BF16)
    heads = []
    for h, mask in ((0, first), (1, ~first)):
        delta = -jnp.sum(jnp.where(mask, product, 0.0), -1, keepdims=True)
        high = delta.astype(BF16)
        low = (delta - high.astype(F32)).astype(BF16)
        spare = (1 - h) * HD
        grad_aug = jnp.where(mask, go_inv, jnp.where(lanes == spare, high, jnp.where(lanes == spare + 1, low, zero)))
        values_aug = jnp.where(mask, values, jnp.where((lanes == spare) | (lanes == spare + 1), jnp.ones((), BF16), zero))
        heads.append((jnp.where(mask, query, zero), jnp.where(mask, keys, zero), jnp.where(mask, go_inv, zero), grad_aug, values_aug))
    dq = []
    dk = jnp.zeros((length, PAIR), F32)
    dv = jnp.zeros((length, PAIR), F32)
    for i in range(length // Q_TILE):
        at = slice(i * Q_TILE, (i + 1) * Q_TILE)
        part = jnp.zeros((Q_TILE, PAIR), F32)
        for qm, km, gm, ga, va in heads:
            exponent = jnp.exp(nt(km, qm[at]))
            grad_scores = (exponent * nt(va, ga[at])).astype(BF16)
            dv = dv + nn(exponent.astype(BF16), gm[at])
            dk = dk + nn(grad_scores, qm[at])
            part = part + lax.dot_general(grad_scores, km, (((0,), (0,)), ((), ())), preferred_element_type=F32)
        dq.append(part)
    dq = jnp.concatenate(dq, axis=0)
    grad_v[...] = dv.astype(BF16)
    matrix = head_mean_matrix(PAIR)
    hat, factor = head_stats(q_raw.astype(F32), matrix)
    scale = HD ** -0.5
    sum_q = jnp.sum(dq * hat, 0, keepdims=True) * scale
    grad_q[...] = head_back(dq * gains[0:1] * scale, hat, factor, matrix).astype(BF16)
    hat, factor = head_stats(k_raw.astype(F32), matrix)
    sum_k = jnp.sum(dk * hat, 0, keepdims=True)
    grad_k[...] = head_back(dk * gains[1:2], hat, factor, matrix).astype(BF16)
    grad_gains[...] += jnp.concatenate([sum_q, sum_k], axis=0)


def backward_body(
    zs, rows_steps, norms, gains, cot, grad_second, middle, mixed_rows, w, qn, kn, v, q_raw, k_raw, mixed, inverse,
    grads_u, grads_d, state_u, state_d, result,
    grad_middle, grad_q, grad_k, grad_v, grad_gains, sums, shard_u, shard_d, shard_o, outputs,
    grad_mixed, acc, g_o, own_early, own_late, load_sem, swap_sem, send, recv, *landings,
):
    step = pl.program_id(0)
    p = Place(zs)
    n = FF_GROUP
    half = w.shape[2]
    at = iter(landings)
    take = lambda count: [next(at) for _ in range(count)]
    early, late, loads = [], [], []
    for i in range(4):
        j, k = divmod(i, 2)
        order = FEED_ORDERS[k]
        state = (state_u, state_d)[k].at[j]
        if order == "x":
            far, near = state.at[:, 1 - p.y], state.at[:, p.y]
        else:
            far, near = state.at[1 - p.x], state.at[p.x]
        b2, b3 = take(2)
        s = Scatter(p, order, lambda x, z, y, i=i: own_early.at[i, z], None, None, None, b2, b3, send.at[i], recv.at[i])
        s.second = lambda s=s, far=far, order=order: s.copy(2, far, s.b2, p.dev(y=1 - p.y) if order == "x" else p.dev(x=1 - p.x))
        early.append(s)
        loads.append(pltpu.make_async_copy(near, own_early.at[i], load_sem.at[i]))
    for i in range(4):
        j, k = divmod(i, 2)
        grad = (grads_u, grads_d)[k].at[j]
        s = Scatter(p, LATE_ORDERS[i], lambda x, z, y, i=i: own_late.at[i, x, z, y], grad.at[:, :, :, 1 - p.c],
                    *take(4), send.at[4 + i], recv.at[4 + i])
        late.append(s)
        loads.append(pltpu.make_async_copy(grad.at[:, :, :, p.c], own_late.at[i], load_sem.at[4 + i]))
    so = Scatter(p, "y", lambda x, z, y: g_o.at[x, z, y, p.c], g_o.at[:, :, :, 1 - p.c], *take(4), send.at[8], recv.at[8])
    swap = SwapBack(p, result, outputs, swap_sem)

    def out(k, j):
        return (shard_u, shard_d)[k].at[:, pl.ds(j * n, n)]

    def h0():
        meet(p)
        start(*loads)
        start(*[s.second() for s in early])
        start(*[s.core() for s in late[:2]])

    def h2():
        wait(*loads)
        for s in late[:2]:
            s.core_add()
            s.first().start()
        start(*[s.core() for s in late[2:]])

    def h4():
        so.core().start()
        for s in early:
            s.second_add()
            start(*s.last())
        for s in late[2:]:
            s.core_add()
            s.first().start()

    def h5():
        so.core_add()
        so.first().start()

    def h6():
        for s in late[:2]:
            s.first_add()
            s.second().start()
        start(swap.copy, swap.mine)

    def h9():
        for s in late[2:]:
            s.first_add()
            s.second().start()
        for s in late[:2]:
            s.second_add()
            start(*s.last())

    def h10():
        so.first_add()
        so.second().start()
        for i, s in enumerate(early):
            s.finish(out(i % 2, i // 2))

    def h11():
        for s in late[2:]:
            s.second_add()
            start(*s.last())

    on(step, {0: h0, 2: h2, 4: h4, 5: h5, 6: h6, 9: h9, 10: h10, 11: h11})

    @pl.when(step == 0)
    def _():
        sums[...] = jnp.zeros_like(sums)
        acc[...] = jnp.zeros_like(acc)
        grad_gains[...] = jnp.zeros_like(grad_gains)

    @pl.when(step < rows_steps)
    def _():
        hat, factor = stats(middle[...])
        gs = grad_second[...]
        gm = cot[...].astype(F32) + back(gs * norms[1:2], hat, factor)
        grad_middle[...] = gm
        branch_grad = gm.astype(BF16)
        branch_t = branch_grad.T
        here = pl.ds(pl.multiple_of(step * ROWS, ROWS), ROWS)
        for t in range(2):
            cols = slice(t * half, (t + 1) * half)
            grad_mixed[here, cols] = nn(branch_grad, w[t]).astype(BF16)
            acc[t] += nn(branch_t, mixed_rows[:, cols])
        sums[0:1] += jnp.sum(gs * hat, 0, keepdims=True)
        sums[1:2] += jnp.sum(gs, 0, keepdims=True)

    @pl.when(step == rows_steps - 1)
    def _():
        g_o[...] = acc[...].astype(BF16).reshape(g_o.shape)

    @pl.when(step >= rows_steps)
    def _():
        cols = pl.ds(pl.multiple_of((step - rows_steps) * PAIR, PAIR), PAIR)
        attend_back_step(gains, grad_mixed[:, cols], inverse[...], qn[...], kn[...], v[...], q_raw[...], k_raw[...], mixed[...],
                         grad_q, grad_k, grad_v, grad_gains)

    @pl.when(step == pl.num_programs(0) - 1)
    def _():
        so.second_add()
        start(*so.last())
        for i, s in enumerate(late):
            s.finish(out(i % 2, 2 + i // 2))
        so.finish(shard_o)
        wait(swap.copy, swap.mine)


def backward(norms, gains, cot, grad_second, middle, mixed, w, kept, inverse, grads_u, grads_d, state_u, state_d, result, zs):
    length, width = middle.shape
    half = w.shape[2]
    rows, n = grads_u.shape[5], FF_GROUP
    row_steps, pairs = length // ROWS, 2 * half // PAIR
    row = clipped((ROWS, width), 0, 0, row_steps)
    head = clipped((length, PAIR), 1, row_steps, pairs)
    heads = jax.ShapeDtypeStruct((length, 2 * half), BF16)
    f32 = lambda *shape: jax.ShapeDtypeStruct(shape, F32)
    scratch = [
        pltpu.VMEM((length, 2 * half), BF16), pltpu.VMEM(w.shape, F32), pltpu.VMEM((2, zs, 2, 2, rows, half), BF16),
        pltpu.VMEM((4, zs, rows, n), BF16), pltpu.VMEM((4, 2, zs, 2, rows, n), BF16), DMA((8,)), DMA((3,)),
        DMA((9, scatter_sems(zs))), DMA((9, scatter_sems(zs))),
    ]
    for i in range(4):
        scratch += landing(zs, rows, n, FEED_ORDERS[i % 2], "23")
    for i in range(4):
        scratch += landing(zs, rows, n, LATE_ORDERS[i])
    scratch += landing(zs, rows, half, "y")
    return pl.pallas_call(
        functools.partial(backward_body, zs, row_steps),
        grid=(row_steps + pairs,),
        in_specs=[full(norms.shape), full(gains.shape), row, row, row, row, full(w.shape)] + [head] * 7 + [HBM] * 5,
        out_specs=[row, head, head, head, full((2, PAIR)), full((2, width)), full((rows, 4 * n)), full((rows, 4 * n)),
                   full((rows, half)), HBM],
        out_shape=[f32(length, width), heads, heads, heads, f32(2, PAIR), f32(2, width), f32(rows, 4 * n), f32(rows, 4 * n),
                   f32(rows, half), jax.ShapeDtypeStruct((2, length // 2, width), BF16)],
        scratch_shapes=scratch,
        compiler_params=params(3),
        name="backward",
    )(norms, gains, cot, grad_second, middle, mixed, w, *kept, mixed, inverse, grads_u, grads_d, state_u, state_d, result)


PART_GROUP = 256
CLOSING = ((0, 0, 768, "y"), (1, 0, 384, "y"), (1, 384, 384, "x"))


def closing_body(
    zs, norms, sums_second, sums_qk, image_in, first_in, grad_middle_in, gq_in, gk_in, gv_in, w_in,
    shard_q, total, grad_tokens,
    image, first, grad_middle, grads, w, first_t, acc, grad_image, g, load_sem, swap_sem, got, sum_send, sum_recv, send, recv, *landings,
):
    p = Place(zs)
    meet(p)
    length, width = image.shape
    half = grads.shape[2] // 2
    load_grads = [pltpu.make_async_copy(a, grads.at[i], load_sem.at[i]) for i, a in enumerate((gq_in, gk_in, gv_in))]
    load_first = pltpu.make_async_copy(first_in, first, load_sem.at[3])
    load_w = pltpu.make_async_copy(w_in, w, load_sem.at[4])
    load_image = pltpu.make_async_copy(image_in, image, load_sem.at[5])
    load_middle = pltpu.make_async_copy(grad_middle_in, grad_middle, load_sem.at[6])
    start(load_first, *load_grads, load_w, load_image, load_middle)
    groups = []
    for i, (k, lo, m, order) in enumerate(CLOSING):
        at = pl.ds(lo, m)
        held = lambda x, z, y, k=k, at=at: g.at[k, x, z, y, p.c, :, at]
        groups.append(Scatter(p, order, held, g.at[k, :, :, :, 1 - p.c, :, at], *landings[4 * i:4 * i + 4], send.at[i], recv.at[i]))
    a, b, c = groups
    swap = SwapBack(p, grad_image, grad_tokens, swap_sem)
    small = Sum(p, total, got, sum_send, sum_recv)

    load_first.wait()
    first_t[...] = first[...].T
    wait(*load_grads)

    def weight_grad(k):
        def one(i, _):
            t, part = lax.div(i, 3), lax.rem(i, 3)
            cols = pl.ds(pl.multiple_of(t * half + k * PART_GROUP, PART_GROUP), PART_GROUP)
            value = nn(first_t[...], grads[part, :, cols]).astype(BF16)
            g[k, t, :, :, :, :, pl.ds(pl.multiple_of(part * PART_GROUP, PART_GROUP), PART_GROUP)] = value.reshape(
                g.shape[2:6] + (PART_GROUP,))
            return 0
        lax.fori_loop(0, 6, one, 0)

    weight_grad(0)
    a.core().start()
    weight_grad(1)
    start(b.core(), c.core())
    a.core_add()
    a.first().start()
    b.core_add()
    b.first().start()
    c.core_add()
    c.first().start()
    load_w.wait()
    acc[...] = jnp.zeros_like(acc)

    def to_first(i, _):
        t, part = lax.div(i, 3), lax.rem(i, 3)
        cols = pl.ds(pl.multiple_of(t * half, half), half)
        acc[...] += nt(grads[part, :, cols], w[t, :, pl.ds(pl.multiple_of(part * half, half), half)])
        return 0
    lax.fori_loop(0, 6, to_first, 0)
    wait(load_image, load_middle)

    def norm_back(i, carry):
        at = pl.ds(pl.multiple_of(i * ROWS, ROWS), ROWS)
        hat, factor = stats(image[at].astype(F32))
        gf = acc[at]
        grad_image[at] = (grad_middle[at] + back(gf * norms[0:1], hat, factor)).astype(BF16)
        return carry[0] + jnp.sum(gf * hat, 0, keepdims=True), carry[1] + jnp.sum(gf, 0, keepdims=True)
    zero = jnp.zeros((1, width), F32)
    sum_hat, sum_all = lax.fori_loop(0, length // ROWS, norm_back, (zero, zero))
    start(swap.copy, swap.mine)
    total[...] = jnp.zeros_like(total)
    total[0:1] = sum_hat
    total[1:2] = sum_all
    total[2:4] = sums_second[...]
    total[4:6, 0:PAIR] = sums_qk[...]
    small.go(0)
    a.first_add()
    a.second().start()
    small.add(0)
    small.go(1)
    c.first_add()
    c.second().start()
    small.add(1)
    small.go(2)
    b.first_add()
    b.second().start()
    small.add(2)
    small.go(3)
    a.second_add()
    start(*a.last())
    small.add(3)
    c.second_add()
    start(*c.last())
    b.second_add()
    start(*b.last())
    for s, (k, lo, m, order) in zip(groups, CLOSING):
        s.finish(shard_q.at[k, :, pl.ds(lo, m)])
    wait(swap.copy, swap.mine)


def closing(norms, sums_second, sums_qk, image, first, grad_middle, gq, gk, gv, w, zs):
    length, width = image.shape
    rows = width // (4 * zs)
    wide = 3 * PART_GROUP
    square = pltpu.VMEM((length, width), BF16)
    scratch = [
        square, square, pltpu.VMEM((length, width), F32), pltpu.VMEM((3,) + gq.shape, BF16), pltpu.VMEM(w.shape, BF16), square,
        pltpu.VMEM((length, width), F32), square, pltpu.VMEM((2, 2, zs, 2, 2, rows, wide), BF16), DMA((7,)), DMA((3,)),
        pltpu.VMEM((zs + 2, 8, width), F32), DMA((zs + 2,)), DMA((zs + 2,)),
        DMA((3, scatter_sems(zs))), DMA((3, scatter_sems(zs))),
    ]
    for k, lo, m, order in CLOSING:
        scratch += landing(zs, rows, m, order)
    return pl.pallas_call(
        functools.partial(closing_body, zs),
        in_specs=[WHOLE_VMEM] * 3 + [HBM] * 7,
        out_specs=[WHOLE_VMEM, WHOLE_VMEM, HBM],
        out_shape=[jax.ShapeDtypeStruct((2, rows, wide), F32), jax.ShapeDtypeStruct((8, width), F32),
                   jax.ShapeDtypeStruct((2, length // 2, width), BF16)],
        scratch_shapes=scratch,
        compiler_params=params(4),
        name="closing",
    )(norms, sums_second, sums_qk, image, first, grad_middle, gq, gk, gv, w)


def whole_images(tokens, cotangent, w_qkv, wo_t, w_up, w_down_t, norm_gains, norm_shifts, qk_gains):
    zs = lax.axis_size("fsdp") // 4
    rows = w_qkv.shape[0]
    width = tokens.shape[2]
    half = w_qkv.shape[2]
    cols = 3 * half
    side = jnp.concatenate([norm_gains, norm_shifts, jnp.zeros((rows, 124), BF16)], axis=1)
    shard_q = jnp.concatenate([w_qkv.reshape(rows, cols), side], axis=1)
    whole_q, whole_o, whole_u, whole_d, image = opening(shard_q, wo_t, w_up, w_down_t, tokens, zs)
    qkv = whole_q.reshape(2, width, cols + 128)
    norms = qkv[0, :, cols:cols + 4].T.astype(F32)
    gains = qk_gains.astype(F32)
    first, qn, kn, v, q_raw, k_raw, mixed, inverse, middle, second, cot, whole_o, whole_u, whole_d = attention(
        image, norms, jnp.tile(gains, (1, QKV_TILE // HD)), qkv, cols, cotangent, w_up, w_down_t, whole_o, whole_u, whole_d, zs
    )
    result, grad_second, grads_u, grads_d, state_u, state_d, whole_u, whole_d = feed(second, cot, middle, whole_u, whole_d, zs)
    grad_middle, gq, gk, gv, sums_qk, sums_second, shard_u, shard_d, shard_o, outputs = backward(
        norms, jnp.tile(gains, (1, 2)), cot, grad_second, middle, mixed, whole_o.reshape(2, width, half),
        (qn, kn, v, q_raw, k_raw), inverse, grads_u, grads_d, state_u, state_d, result, zs
    )
    grad_q, small, grad_tokens = closing(norms, sums_second, sums_qk, image, first, grad_middle, gq, gk, gv, qkv, zs)
    grad_q = grad_q.reshape(2, rows, 3, PART_GROUP).transpose(1, 2, 0, 3).reshape(w_qkv.shape)
    mine = lax.dynamic_slice_in_dim(small, lax.axis_index("fsdp") * rows, rows, 1)
    return (
        outputs,
        grad_tokens.astype(F32),
        grad_q,
        shard_o,
        shard_u,
        shard_d,
        jnp.stack([mine[0], mine[2]], 1),
        jnp.stack([mine[1], mine[3]], 1),
        small[4:6, :HD] + small[4:6, HD:2 * HD],
    )


def layer(tokens, *rest):
    if tokens.shape[0] == lax.axis_size("tensor") == 2 and lax.axis_size("fsdp") % 4 == 0:
        return whole_images(tokens, *rest)
    return per_device(tokens, *rest)


def solution(mesh):
    in_specs = (
        P("fsdp", "tensor", None),
        P("fsdp", "tensor", None),
        P("fsdp", None, "tensor"),
        P("fsdp", "tensor"),
        P("fsdp", "tensor"),
        P("fsdp", "tensor"),
        P("fsdp", None),
        P("fsdp", None),
        P(),
    )
    out_specs = (
        P("fsdp", "tensor", None),
        P("fsdp", "tensor", None),
        P("fsdp", None, "tensor"),
        P("fsdp", "tensor"),
        P("fsdp", "tensor"),
        P("fsdp", "tensor"),
        P("fsdp", None),
        P("fsdp", None),
        P(),
    )
    return jax.shard_map(
        layer, mesh=mesh, in_specs=in_specs, out_specs=out_specs, check_vma=False
    )
```

```python
import functools

import jax
import jax.numpy as jnp
from jax import lax
from jax.experimental import pallas as pl
from jax.experimental.pallas import tpu as pltpu
from jax.sharding import PartitionSpec as P

HD = 64


EPSILON = 1e-06


def norm_stats(value):
    center = value - jnp.mean(value, -1, keepdims=True)
    factor = lax.rsqrt(jnp.mean(center * center, -1, keepdims=True) + EPSILON)
    return (center * factor, factor)


def norm_back(grad_hat, normed, factor):
    return factor * (
        grad_hat
        - jnp.mean(grad_hat, -1, keepdims=True)
        - normed * jnp.mean(grad_hat * normed, -1, keepdims=True)
    )


def contract_rows(left, right):
    return lax.dot_general(
        left, right, (((0,), (0,)), ((), ())), preferred_element_type=jnp.float32
    )


def contract_cols(left, right):
    return lax.dot_general(
        left, right, (((1,), (1,)), ((), ())), preferred_element_type=jnp.float32
    )


def per_device(tokens, cotangent, w_qkv, wo_t, w_up, w_down_t, norm_gains, norm_shifts, qk_gains):
    local_rows = tokens.shape[1]
    width = tokens.shape[2]
    head_cols = w_qkv.shape[2]
    local_heads = head_cols // HD
    hidden_cols = w_up.shape[1]
    tensor_count = lax.axis_size("tensor")
    full_len = local_rows * tensor_count
    block = min(512, full_len)
    blocks = full_len // block
    gain_query = qk_gains[0].astype(jnp.float32)
    gain_keys = qk_gains[1].astype(jnp.float32)
    scale_query = HD ** (-0.5)

    def fetch():
        return (
            lax.all_gather(w_qkv, "fsdp", axis=0, tiled=True),
            lax.all_gather(wo_t, "fsdp", axis=0, tiled=True),
            lax.all_gather(w_up, "fsdp", axis=0, tiled=True),
            lax.all_gather(w_down_t, "fsdp", axis=0, tiled=True),
            lax.all_gather(norm_gains, "fsdp", axis=0, tiled=True),
            lax.all_gather(norm_shifts, "fsdp", axis=0, tiled=True),
        )

    def forward(weights, inputs):
        whole_qkv, whole_out, whole_up, whole_down, gains, shifts = weights
        gains = gains.astype(jnp.float32)
        shifts = shifts.astype(jnp.float32)
        flat_qkv = whole_qkv.reshape(width, 3 * head_cols)
        residual = inputs.astype(jnp.float32)
        first_hat, first_factor = norm_stats(residual)
        first = (first_hat * gains[:, 0] + shifts[:, 0]).astype(jnp.bfloat16)
        piece = lax.all_gather(first, "tensor", axis=0, tiled=True)
        first_full = piece
        joined = jnp.dot(piece, flat_qkv, preferred_element_type=jnp.float32)
        joined = joined.reshape(full_len, 3, local_heads, HD)
        query_hat, query_factor = norm_stats(joined[:, 0])
        keys_hat, keys_factor = norm_stats(joined[:, 1])
        query_n = (query_hat * gain_query * scale_query).astype(jnp.bfloat16)
        keys_n = (keys_hat * gain_keys).astype(jnp.bfloat16)
        values = joined[:, 2].astype(jnp.bfloat16)

        def attend(query_block):
            scores = jnp.einsum(
                "qhd,khd->hqk", query_block, keys_n, preferred_element_type=jnp.float32
            )
            largest = jnp.max(scores, -1, keepdims=True)
            exponent = jnp.exp(scores - largest)
            total_sum = jnp.sum(exponent, -1, keepdims=True)
            probs_low = (exponent / total_sum).astype(jnp.bfloat16)
            mixed_block = jnp.einsum(
                "hqk,khd->qhd", probs_low, values, preferred_element_type=jnp.float32
            )
            return (mixed_block.astype(jnp.bfloat16), (largest + jnp.log(total_sum))[..., 0])

        mixed, log_total = lax.map(attend, query_n.reshape(blocks, block, local_heads, HD))
        mixed = mixed.reshape(full_len, head_cols)
        middle = residual + lax.psum_scatter(
            contract_cols(mixed, whole_out), "tensor", scatter_dimension=0, tiled=True
        )
        second_hat, second_factor = norm_stats(middle)
        second = (second_hat * gains[:, 1] + shifts[:, 1]).astype(jnp.bfloat16)
        piece = lax.all_gather(second, "tensor", axis=0, tiled=True)
        hidden = jnp.dot(piece, whole_up, preferred_element_type=jnp.float32)
        active = jax.nn.gelu(hidden, approximate=False).astype(jnp.bfloat16)
        result = (
            middle
            + lax.psum_scatter(
                contract_cols(active, whole_down).astype(jnp.bfloat16),
                "tensor",
                scatter_dimension=0,
                tiled=True,
            ).astype(jnp.float32)
        ).astype(jnp.bfloat16)
        kept = (
            first_hat,
            first_factor,
            first_full,
            query_hat,
            query_factor,
            keys_hat,
            keys_factor,
            query_n,
            keys_n,
            values,
            mixed,
            log_total,
            second_hat,
            second_factor,
            piece,
            hidden,
            active,
        )
        return (kept, result)

    def backward(weights, kept, grad_out):
        whole_qkv, whole_out, whole_up, whole_down, gains, shifts = weights
        gains = gains.astype(jnp.float32)
        flat_qkv = whole_qkv.reshape(width, 3 * head_cols)
        (
            first_hat,
            first_factor,
            first_full,
            query_hat,
            query_factor,
            keys_hat,
            keys_factor,
            query_n,
            keys_n,
            values,
            mixed_keep,
            log_total,
            second_hat,
            second_factor,
            second_full,
            hidden,
            active,
        ) = kept
        piece = lax.all_gather(grad_out, "tensor", axis=0, tiled=True)
        grad_full = piece
        grad_active = jnp.dot(piece, whole_down, preferred_element_type=jnp.float32)
        grad_down = contract_rows(grad_full, active)
        unused_value, gelu_pull = jax.vjp(
            lambda value: jax.nn.gelu(value, approximate=False), hidden
        )
        grad_hidden = gelu_pull(grad_active)[0].astype(jnp.bfloat16)
        grad_up = contract_rows(second_full, grad_hidden)
        grad_second = lax.psum_scatter(
            contract_cols(grad_hidden, whole_up), "tensor", scatter_dimension=0, tiled=True
        )
        grad_middle = grad_out.astype(jnp.float32) + norm_back(
            grad_second * gains[:, 1], second_hat, second_factor
        )
        grad_branch = grad_middle.astype(jnp.bfloat16)
        piece = lax.all_gather(grad_branch, "tensor", axis=0, tiled=True)
        grad_mixed = jnp.dot(piece, whole_out, preferred_element_type=jnp.float32)
        grad_out_w = contract_rows(piece, mixed_keep)
        grad_mixed = grad_mixed.astype(jnp.bfloat16)
        grad_mixed = grad_mixed.reshape(blocks, block, local_heads, HD)

        def attend_back(carry, item):
            grad_keys_sum, grad_values_sum = carry
            query_block, grad_block, log_block = item
            scores = jnp.einsum(
                "qhd,khd->hqk", query_block, keys_n, preferred_element_type=jnp.float32
            )
            probs = jnp.exp(scores - log_block[..., None])
            grad_probs = jnp.einsum(
                "qhd,khd->hqk", grad_block, values, preferred_element_type=jnp.float32
            )
            delta = jnp.sum(probs * grad_probs, -1, keepdims=True)
            grad_scores = (probs * (grad_probs - delta)).astype(jnp.bfloat16)
            grad_query_block = jnp.einsum(
                "hqk,khd->qhd", grad_scores, keys_n, preferred_element_type=jnp.float32
            )
            grad_keys_sum = grad_keys_sum + jnp.einsum(
                "hqk,qhd->khd", grad_scores, query_block, preferred_element_type=jnp.float32
            )
            grad_values_sum = grad_values_sum + jnp.einsum(
                "hqk,qhd->khd",
                probs.astype(jnp.bfloat16),
                grad_block,
                preferred_element_type=jnp.float32,
            )
            return ((grad_keys_sum, grad_values_sum), grad_query_block)

        empty_heads = jnp.zeros((full_len, local_heads, HD), jnp.float32)
        (grad_keys_n, grad_values), grad_query_n = lax.scan(
            attend_back,
            (empty_heads, empty_heads),
            (query_n.reshape(blocks, block, local_heads, HD), grad_mixed, log_total),
        )
        grad_query_n = grad_query_n.reshape(full_len, local_heads, HD)
        grad_query = norm_back(grad_query_n * gain_query * scale_query, query_hat, query_factor)
        grad_keys = norm_back(grad_keys_n * gain_keys, keys_hat, keys_factor)
        qk_grad = jnp.stack(
            [
                jnp.sum(grad_query_n * query_hat * scale_query, (0, 1)),
                jnp.sum(grad_keys_n * keys_hat, (0, 1)),
            ]
        )
        grad_joined = jnp.stack([grad_query, grad_keys, grad_values], 1).astype(jnp.bfloat16)
        grad_joined = grad_joined.reshape(full_len, 3 * head_cols)
        grad_qkv = contract_rows(first_full, grad_joined).reshape(width, 3, head_cols)
        grad_first = lax.psum_scatter(
            contract_cols(grad_joined, flat_qkv).astype(jnp.bfloat16),
            "tensor",
            scatter_dimension=0,
            tiled=True,
        ).astype(jnp.float32)
        grad_input = grad_middle + norm_back(grad_first * gains[:, 0], first_hat, first_factor)
        gain_grad = jnp.stack(
            [jnp.sum(grad_first * first_hat, 0), jnp.sum(grad_second * second_hat, 0)], 1
        )
        shift_grad = jnp.stack([jnp.sum(grad_first, 0), jnp.sum(grad_second, 0)], 1)
        return (
            (grad_qkv, grad_out_w, grad_up, grad_down, gain_grad, shift_grad, qk_grad),
            grad_input,
        )

    def micro_step(totals, item):
        inputs, grad_out = item
        forward_weights = fetch()
        kept, result = forward(forward_weights, inputs)
        backward_weights = fetch()
        grads, grad_input = backward(backward_weights, kept, grad_out)
        totals = tuple((total + part for total, part in zip(totals, grads)))
        return (totals, (result, grad_input))

    out_cols_count = wo_t.shape[1]
    start_sums = (
        jnp.zeros((width, 3, head_cols), jnp.float32),
        jnp.zeros((width, out_cols_count), jnp.float32),
        jnp.zeros((width, hidden_cols), jnp.float32),
        jnp.zeros((width, hidden_cols), jnp.float32),
        jnp.zeros((width, 2), jnp.float32),
        jnp.zeros((width, 2), jnp.float32),
        jnp.zeros((2, HD), jnp.float32),
    )
    totals, (outputs, grad_tokens) = lax.scan(micro_step, start_sums, (tokens, cotangent))
    out_total = totals[1]
    grad_qkv, grad_out_w, grad_up, grad_down = (
        lax.psum_scatter(
            totals[0].astype(jnp.bfloat16), "fsdp", scatter_dimension=0, tiled=True
        ).astype(jnp.float32),
        lax.psum_scatter(
            out_total.astype(jnp.bfloat16), "fsdp", scatter_dimension=0, tiled=True
        ).astype(jnp.float32),
        lax.psum_scatter(
            totals[2].astype(jnp.bfloat16), "fsdp", scatter_dimension=0, tiled=True
        ).astype(jnp.float32),
        lax.psum_scatter(
            totals[3].astype(jnp.bfloat16), "fsdp", scatter_dimension=0, tiled=True
        ).astype(jnp.float32),
    )
    gain_total, shift_total, qk_total = lax.psum(
        (totals[4], totals[5], totals[6]), ("fsdp", "tensor")
    )
    own_rows = width // lax.axis_size("fsdp")
    offset = lax.axis_index("fsdp") * own_rows
    gain_part = lax.dynamic_slice_in_dim(gain_total, offset, own_rows, 0)
    shift_part = lax.dynamic_slice_in_dim(shift_total, offset, own_rows, 0)
    return (
        outputs,
        grad_tokens,
        grad_qkv,
        grad_out_w,
        grad_up,
        grad_down,
        gain_part,
        shift_part,
        qk_total,
    )


PAIR = 2 * HD
F32, BF16 = jnp.float32, jnp.bfloat16
LIMIT = 60 << 20


def nn(a, b):
    return lax.dot_general(a, b, (((1,), (0,)), ((), ())), preferred_element_type=F32)


def nt(a, b):
    return lax.dot_general(a, b, (((1,), (1,)), ((), ())), preferred_element_type=F32)


def stats(value):
    center = value - jnp.mean(value, -1, keepdims=True)
    factor = lax.rsqrt(jnp.mean(center * center, -1, keepdims=True) + EPSILON)
    return center * factor, factor


def back(grad_hat, normed, factor):
    return factor * (
        grad_hat
        - jnp.mean(grad_hat, -1, keepdims=True)
        - normed * jnp.mean(grad_hat * normed, -1, keepdims=True)
    )


def head_mean_matrix(width):
    row = lax.broadcasted_iota(jnp.int32, (width, width), 0) // HD
    col = lax.broadcasted_iota(jnp.int32, (width, width), 1) // HD
    return jnp.where(row == col, 1.0 / HD, 0.0).astype(BF16)


def head_mean(value, matrix):
    high = value.astype(BF16)
    low = (value - high.astype(F32)).astype(BF16)
    return nn(high, matrix) + nn(low, matrix)


def head_stats(value, matrix):
    center = value - head_mean(value, matrix)
    factor = lax.rsqrt(head_mean(center * center, matrix) + EPSILON)
    return center * factor, factor


def head_back(grad_hat, normed, factor, matrix):
    return factor * (
        grad_hat - head_mean(grad_hat, matrix) - normed * head_mean(grad_hat * normed, matrix)
    )


MESH = pl.DeviceIdType.MESH
ALL = slice(None)


class Place:
    def __init__(self, zs):
        f = lax.axis_index("fsdp")
        self.zs = zs
        self.x = lax.axis_index("tensor")
        self.c = lax.rem(f, 2)
        self.y = lax.rem(lax.div(f, 2), 2)
        self.z = lax.div(f, 4)

    def dev(self, z=None, y=None, c=None, x=None):
        z = self.z if z is None else z
        y = self.y if y is None else y
        c = self.c if c is None else c
        x = self.x if x is None else x
        return {"fsdp": (z * 2 + y) * 2 + c, "tensor": x}

    def along_z(self):
        return [lax.rem(self.z + k, self.zs) for k in range(1, self.zs)]

    def peers(self):
        out = [self.dev(z=z) for z in self.along_z()]
        return out + [self.dev(y=1 - self.y), self.dev(c=1 - self.c), self.dev(x=1 - self.x)]


def meet(place):
    barrier = pltpu.get_barrier_semaphore()
    peers = place.peers()
    for peer in peers:
        pl.semaphore_signal(barrier, inc=1, device_id=peer, device_id_type=MESH)
    pl.semaphore_wait(barrier, len(peers))


def remote(src, dst, send, recv, peer):
    return pltpu.make_async_remote_copy(
        src_ref=src, dst_ref=dst, send_sem=send, recv_sem=recv, device_id=peer, device_id_type=MESH
    )


def start(*copies):
    for copy in copies:
        copy.start()


def wait(*copies):
    for copy in copies:
        copy.wait()


class Gather:
    def __init__(self, place, shard, whole, lo, size, order, send, recv, since=0):
        p = self.p = place
        cols = self.cols = pl.ds(lo, size)
        self.shard = None if shard is None else shard.at[:, cols]
        self.whole = whole
        self.order, self.since = order, since
        self.send, self.recv = send, recv
        if shard is not None:
            self.own = pltpu.make_async_copy(self.shard, self.at({}), self.send.at[2 * p.zs + 7])

    def at(self, index):
        p = self.p
        own = {"x": p.x, "y": p.y, "z": p.z}
        x, y, z = (index.get(d, own[d]) for d in "xyz")
        return self.whole.at[x, z, y, p.c, :, self.cols]

    def others(self, d):
        return self.p.along_z() if d == "z" else [1 - getattr(self.p, d)]

    def copies(self, base, i, pairs):
        base += sum(len(self.others(d)) for d in self.order[:i])
        return [remote(src, dst, self.send.at[base + k], self.recv.at[base + k], peer) for k, (src, dst, peer) in enumerate(pairs)]

    def stage(self, i):
        d = self.order[i]
        held = self.at({e: ALL for e in self.order[:i]})
        src = self.shard if i == 0 else held
        return self.copies(0, i, [(src, held, self.p.dev(**{d: to})) for to in self.others(d)])

    def core_parts(self, i):
        done = {e: ALL for e in self.order[:i]}
        d = self.order[i]
        if i == 0:
            refs = [self.at({d: ALL})]
        else:
            refs = [self.at({**done, d: to}) for to in self.others(d)]
        peer = self.p.dev(c=1 - self.p.c)
        return self.copies(self.p.zs + 1, i, [(ref, ref, peer) for ref in refs])

    def start(self, i):
        if i == 0:
            self.own.start()
        if i < 3:
            start(*self.stage(i))
        if i > 0:
            start(*self.core_parts(i - 1))

    def done(self, i):
        if i == 0:
            self.own.wait()
        if i < 3:
            wait(*self.stage(i))
        else:
            self.rest(self.since - 1 if self.since else 0, 3)

    def rest(self, lo, hi):
        for i in range(lo, hi):
            wait(*self.core_parts(i))


def gather_sems(zs):
    return 2 * zs + 8


CHUNKS = 4


class Swap:
    def __init__(self, place, src, dst, sems):
        rows = src.shape[0] // CHUNKS
        part = lambda ref, i: ref.at[pl.ds(i * rows, rows)]
        self.copies = [remote(part(src, i), part(dst, i), sems.at[0, i], sems.at[1, i], place.dev(x=1 - place.x)) for i in range(CHUNKS)]

    def start(self, i):
        self.copies[i].start()

    def done(self, i):
        self.copies[i].wait()


def half_rows(ref, which, rows):
    return ref.at[pl.ds(pl.multiple_of(which * rows, rows), rows)]


class Sum:
    def __init__(self, place, total, got, send, recv):
        self.p, self.total, self.got, self.send, self.recv = place, total, got, send, recv

    def copies(self, i):
        p = self.p
        if i < 3:
            peers = [(p.dev(c=1 - p.c), p.dev(x=1 - p.x), p.dev(y=1 - p.y))[i]]
        else:
            peers = [p.dev(z=z) for z in p.along_z()]
        return [remote(self.total, self.got.at[i + k], self.send.at[i + k], self.recv.at[i + k], peer)
                for k, peer in enumerate(peers)]

    def start(self, i):
        start(*self.copies(i))

    def done(self, i):
        copies = self.copies(i)
        wait(*copies)
        total = self.total[...]
        for k in range(len(copies)):
            total = total + self.got[i + k]
        self.total[...] = total


def add_slabs(count, pair):
    def body(i, _):
        into, from_ = pair(i)
        into[...] = into[...] + from_[...]
        return 0
    lax.fori_loop(0, count, body, 0)


class Scatter:
    def __init__(self, place, order, held, away, landings, send, recv, out=None):
        self.p, self.order, self.held, self.away = place, order, held, away
        self.landings, self.send, self.recv, self.out = landings, send, recv, out

    def size(self, d):
        return self.p.zs if d == "z" else 2

    def others(self, d):
        return self.p.along_z() if d == "z" else [1 - getattr(self.p, d)]

    def part(self, i, value, rest=None):
        at = {e: ALL for e in "xzy"}
        at.update(rest or {})
        at.update({e: getattr(self.p, e) for e in self.order[:i]})
        at[self.order[i]] = value
        return self.held(at["x"], at["z"], at["y"])

    def copies(self, i):
        p = self.p
        if i == 0:
            return [remote(self.away, self.landings[0], self.send.at[0], self.recv.at[0], p.dev(c=1 - p.c))]
        d = self.order[i - 1]
        base = 1 + sum(len(self.others(e)) for e in self.order[:i - 1])
        return [remote(self.part(i - 1, to), self.landings[i].at[k], self.send.at[base + k], self.recv.at[base + k], p.dev(**{d: to}))
                for k, to in enumerate(self.others(d))]

    def start(self, i):
        start(*self.copies(i))

    def done(self, i):
        p = self.p
        wait(*self.copies(i))
        if i == 3:
            value = self.part(2, getattr(p, self.order[2]))[...].astype(F32)
            for k in range(len(self.others(self.order[2]))):
                value = value + self.landings[3][k].astype(F32)
            self.out[...] = value
            return
        dims = [e for e in "xzy" if e not in self.order[:i]]
        count = 1
        for e in dims:
            count *= self.size(e)

        def body(j, _):
            at, left = {}, j
            for e in reversed(dims):
                at[e] = lax.rem(left, self.size(e))
                left = lax.div(left, self.size(e))
            index = tuple(at[e] for e in dims)
            if i == 0:
                into, froms = self.held(at["x"], at["z"], at["y"]), [self.landings[0].at[index]]
            else:
                d = self.order[i - 1]
                into = self.part(i - 1, getattr(p, d), at)
                froms = [self.landings[i].at[(k,) + index] for k in range(len(self.others(d)))]
            value = into[...]
            if len(froms) == 1:
                value = value + froms[0][...]
            else:
                value = value.astype(F32)
                for from_ in froms:
                    value = value + from_[...].astype(F32)
                value = value.astype(BF16)
            into[...] = value
            return 0
        lax.fori_loop(0, count, body, 0)

    def state(self):
        return self.part(0, getattr(self.p, self.order[0]))


def scatter_sems(zs):
    return zs + 2


def rest_shape(zs, rows, m, gone):
    size = {"x": 2, "z": zs, "y": 2}
    return tuple(size[e] for e in "xzy" if e not in gone) + (rows, m)


def landing(zs, rows, m, order, since=0):
    shapes = [rest_shape(zs, rows, m, "")]
    for i, d in enumerate(order):
        shapes.append((zs - 1 if d == "z" else 1,) + rest_shape(zs, rows, m, order[:i + 1]))
    return [pltpu.VMEM(shape, BF16) for shape in shapes[since:]]


def follow(chains, plan):
    for name, i in plan:
        if i < 0:
            chains[name].start(-1 - i)
        else:
            chains[name].done(i)


def at_steps(step, chains, plans):
    for at, plan in enumerate(plans):
        if plan:
            pl.when(step == at)(functools.partial(follow, chains, plan))


def on(step, hooks):
    for at, hook in hooks.items():
        pl.when(step == at)(hook)


HBM = pl.BlockSpec(memory_space=pl.ANY)
WHOLE_VMEM = pl.BlockSpec(memory_space=pltpu.VMEM)
DMA = pltpu.SemaphoreType.DMA


def params(collective_id):
    return pltpu.CompilerParams(collective_id=collective_id, has_side_effects=True, vmem_limit_bytes=LIMIT)


Q_ORDERS = ('zxy', 'xyz', 'zxy', 'yzx', 'zyx', 'yzx')
O_ORDER = 'xzy'
U_ORDERS = ('xzy', 'zxy', 'xzy', 'yzx')
D_ORDERS = ('yzx', 'yzx', 'zyx', 'xyz')
FEED_SINCE = (2, 1, 1)
FEED_ORDERS = ('xyz', 'xzy', 'yxz', 'xyz')
LATE_ORDERS = ('yxz', 'yxz', 'xzy', 'xyz')
O_BACK_ORDER = 'yxz'
CLOSING = ((0, 0, 384, 'yxz'), (0, 384, 384, 'xyz'), (1, 0, 384, 'yzx'), (1, 384, 384, 'zxy'))
ATTENTION_LEAVES = (('U1', 2), ('D1', 2), ('U2', 1), ('D2', 1), ('U3', 1), ('D3', 1))
OPENING_PLAN = (('T', -1), (0, -1), (1, -1), (2, -1), (3, -1), (5, -1), (1, 0), ('O', -1), (3, 0), (1, -2), (5, 0), ('D0', -1), (2, 0), (3, -2), (1, 1), ('D1', -1), ('O', 0), (2, -2), ('D0', 0), ('U3', -1), (0, 0), (1, -3), ('T', 0), ('T', -2), ('D1', 0), ('U3', 0), (2, 1), (0, -2), (2, -3), (3, 1), (4, -1), ('T', 1), ('T', -3), (2, 2), (2, -4), (0, 1), (0, -3), (3, -3), (2, 3), (4, 0), (4, -2), (5, -2), (1, 2), (1, -4), ('O', -2), ('T', 2), ('T', -4), (1, 3), (3, 2), (3, -4), ('U0', -1), (4, 1), (0, 2), (0, -4), (3, 3), (5, 1), ('D0', -2), ('U0', 0), (4, -3), (0, 3), ('T', 3), (5, -3),)
ATTENTION_PLANS = (
    (),
    (),
    (),
    (),
    (),
    ((4, 2), (4, -4), ('C', -1),),
    (('O', 1), ('O', -3), ('U0', -2), (5, 2), (5, -4), ('U2', -1),),
    ((4, 3),),
    ((5, 3), ('D0', 1), ('U1', -1), ('U2', 0), ('D0', -3),),
    (('C', 0), ('C', -2),),
    (),
    (),
    (('O', 2), ('O', -4),),
    (),
    (('U1', 0), ('D1', -2), ('O', 3), ('U0', 1), ('U0', -3), ('D2', -1),),
    (('C', 1), ('C', -3),),
    (('D0', 2), ('D0', -4), ('U1', -2),),
    (),
    (('D0', 3),),
    (('U0', 2), ('U0', -4), ('D2', 0), ('C', 2), ('C', -4),),
    (),
    (('U1', 1), ('D3', -1), ('U0', 3),),
    (('D1', 1),),
    (),
)
ATTENTION_END = (('D3', 0), ('C', 3),)
FEED_PLANS = (
    (('U1', -3), ('D1', -3), ('U2', -2), ('D2', -2), ('U3', -2),),
    (),
    (),
    (('D1', 2), ('D1', -4), ('D2', 1), ('D2', -3), ('D3', -2),),
    (('u0', -1), ('d0', -1), ('U1', 2), ('U1', -4), ('D1', 3), ('D3', 1), ('U2', 1), ('U2', -3), ('D3', -3), ('U3', 1), ('U3', -3), ('U1', 3),),
    (('u0', 0), ('d0', 0),),
    (('D2', 2), ('D2', -4), ('u0', -2),),
    (('U2', 2), ('U2', -4), ('D2', 3),),
    (('u1', -1), ('d1', -1), ('U3', 2), ('d0', -2), ('U3', -4), ('U2', 3),),
    (('D3', 2), ('D3', -4),),
    (('U3', 3),),
    (('u1', 0), ('u1', -2), ('d1', 0), ('D3', 3), ('u0', 1), ('d1', -2),),
    (),
    (('d0', 1),),
    (),
    (('u1', 1), ('d1', 1),),
)
FEED_END = ()
BACKWARD_PLANS = (
    (('u0', -3), ('d0', -3), ('u1', -3), ('d1', -3), ('u2', -1), ('d2', -1), ('u3', -1), ('d3', -1), ('R', -1),),
    (),
    (),
    (),
    (),
    (('u0', 2), ('u0', -4), ('d0', 2), ('d0', -4), ('u1', 2), ('u1', -4), ('d1', 2), ('d1', -4), ('R', 0), ('R', -2), ('u2', 0), ('o', -1), ('u2', -2), ('d2', 0), ('u3', 0), ('u3', -2), ('d3', 0),),
    (('d0', 3), ('d2', -2),),
    (('o', 0),),
    (('R', 1), ('d3', -2),),
    (),
    (('u0', 3), ('u1', 3), ('d1', 3), ('u2', 1), ('o', -2),),
    (('u3', 1), ('u2', -3), ('u3', -3),),
    (('d2', 1),),
    (('d3', 1), ('d2', -3), ('d3', -3),),
    (('u2', 2), ('u2', -4), ('R', -3),),
    (('o', 1), ('u3', 2), ('u3', -4),),
    (('d3', 2), ('d3', -4), ('d2', 2), ('o', -3), ('d2', -4), ('u3', 3), ('u2', 3),),
    (('R', 2), ('R', -4),),
    (),
    (('o', 2), ('o', -4),),
)
BACKWARD_END = (('d3', 3), ('d2', 3), ('R', 3), ('o', 3),)
CLOSING_PLANS = (
    ((0, -1), (1, -1),),
    ((2, -1), (3, -1),),
    ((0, 0), (0, -2), (1, 0), (1, -2),),
    ((2, 0), (2, -2), (3, 0), (3, -2),),
)
CLOSING_END = (('S', -1), ('G', -1), (1, 1), ('S', 0), ('S', -2), (0, 1), (1, -3), ('S', 1), (0, -3), ('G', 0), ('G', -2), (2, 1), ('S', -3), (2, -3), (1, 2), (0, 2), (3, 1), (0, -4), (3, -3), ('S', 2), ('G', 1), ('G', -3), (3, 2), (3, -4), (3, 3), (0, 3), ('S', -4), ('G', 2), ('G', -4), (2, 2), (1, -4), (2, -4), (2, 3), ('S', 3), (1, 3), ('G', 3),)


Q_TILE = 256
ROWS = 256
FF_GROUP = 512


def full(shape):
    return pl.BlockSpec(shape, lambda s: (0,) * len(shape), pipeline_mode=pl.Buffered(1))


def clipped(shape, axis, first, count):
    def at(s):
        i = jnp.clip(s - first, 0, count - 1)
        return (i, 0) if axis == 0 else (0, i)
    return pl.BlockSpec(shape, at)


def tile_of(part, s):
    i = jnp.clip(s - 4 * part, 0, 3)
    column = lax.div(i, 2)
    return lax.rem(i, 2) * 2 + (1 - column if part == 0 else column)


def project_step(step, joined, gains, kept, blocks):
    tile = joined.shape[1]
    qn_s, kn_s, v_s = kept
    qn, kn, v, q_raw, k_raw = blocks
    matrix = head_mean_matrix(tile)

    def cols(part):
        return pl.ds(pl.multiple_of(tile_of(part, step) * tile, tile), tile)

    @pl.when(step < 4)
    def _():
        value = joined.astype(BF16)
        v[...] = value
        v_s[:, cols(0)] = value

    @pl.when((step >= 4) & (step < 8))
    def _():
        hat, _f = head_stats(joined, matrix)
        value = (hat * gains[1:2]).astype(BF16)
        kn[...] = value
        kn_s[:, cols(1)] = value
        k_raw[...] = joined.astype(BF16)

    @pl.when(step >= 8)
    def _():
        hat, _f = head_stats(joined, matrix)
        value = (hat * gains[0:1] * (HD ** -0.5)).astype(BF16)
        qn[...] = value
        qn_s[:, cols(2)] = value
        q_raw[...] = joined.astype(BF16)


def attend_step(query_all, keys, values, mixed_s, cols, mixed, inverse):
    length = keys.shape[0]
    lane = lax.broadcasted_iota(jnp.int32, (1, PAIR), 1) < HD
    values = jnp.concatenate([values, jnp.ones((length, PAIR), BF16)], axis=1)
    zero = jnp.zeros((), BF16)
    for i in range(length // Q_TILE):
        at = slice(i * Q_TILE, (i + 1) * Q_TILE)
        query = query_all[at]
        got = []
        for mask in (lane, ~lane):
            scores = nt(jnp.where(mask, query, zero), keys)
            got.append(nn(jnp.exp(scores).astype(BF16), values))
        inv = 1.0 / jnp.where(lane, got[0][:, PAIR:], got[1][:, PAIR:])
        value = (jnp.where(lane, got[0][:, :PAIR], got[1][:, :PAIR]) * inv).astype(BF16)
        mixed[at] = value
        mixed_s[at, cols] = value
        inverse[at] = inv


PROJECT_STEPS = 12


def first_after(plans, name):
    return max([at for at, plan in enumerate(plans) if (name, 3) in plan], default=0)


def attention_body(
    zs, pairs, qk_gains, q_in, o_in, u_in, d_in, tokens, cot_in,
    first, qn, kn, v, q_raw, k_raw, mixed, inverse, middle, second, norms, image, cot, whole_q, whole_o, whole_u, whole_d,
    image_v, qn_s, kn_s, v_s, mixed_s, out_w, tiles, q_v, o_v, u_v, d_v, cot_v, side_v, local_sem, send, recv, swap_sem,
):
    step = pl.program_id(0)
    p = Place(zs)
    length = image_v.shape[0]
    half = whole_o.shape[5]
    tile = half // 2
    head0, row0 = PROJECT_STEPS, PROJECT_STEPS + pairs
    n = FF_GROUP
    mine = pl.ds(pl.multiple_of(p.x * (length // 2), length // 2), length // 2)
    chains = {
        "T": Swap(p, tokens.at[1 - p.x], half_rows(image_v, p.x, length // 2), swap_sem.at[0]),
        "C": Swap(p, cot_in.at[1 - p.x], half_rows(cot, p.x, length // 2), swap_sem.at[1]),
    }
    local = lambda i, src, dst: pltpu.make_async_copy(src, dst, local_sem.at[i])
    own_shards = [local(i, a, b) for i, (a, b) in enumerate(((q_in, q_v), (o_in, o_v), (u_in, u_v), (d_in, d_v)))]
    own_tokens = local(4, tokens.at[p.x], image_v.at[mine])
    own_cot = [local(5, cot_in.at[p.x], cot_v), local(6, cot_v, cot.at[mine])]
    keep_image = local(7, image_v, image)
    side = local(8, whole_q.at[0, :, :, :, :, pl.ds(3 * half, PAIR)], side_v)
    load_out = local(9, whole_o, out_w)
    starts = (2 * half + tile, 2 * half, half, half + tile, 0, tile)
    for i, lo in enumerate(starts):
        chains[i] = Gather(p, q_v, whole_q, lo, tile + PAIR if i == 0 else tile, Q_ORDERS[i], send.at[i], recv.at[i])

    def load_tile(i):
        return local(10 + i % 2, whole_q.at[:, :, :, :, :, pl.ds(starts[i], tile)], tiles.at[i % 2])

    chains["O"] = Gather(p, o_v, whole_o, 0, half, O_ORDER, send.at[6], recv.at[6])
    for j in range(4):
        chains[f"U{j}"] = Gather(p, u_v, whole_u, j * n, n, U_ORDERS[j], send.at[7 + j], recv.at[7 + j])
        chains[f"D{j}"] = Gather(p, d_v, whole_d, j * n, n, D_ORDERS[j], send.at[11 + j], recv.at[11 + j])

    @pl.when(step == 0)
    def _():
        start(*own_shards, own_tokens, own_cot[0])
        meet(p)
        wait(*own_shards)
        follow(chains, OPENING_PLAN)
        load_tile(0).start()
        side.start()
        own_cot[0].wait()
        own_cot[1].start()
        side.wait()
        norms[...] = side_v[...].reshape(-1, PAIR).astype(F32).T[:8]
        own_tokens.wait()
        keep_image.start()

        def norm(i, _):
            at = pl.ds(pl.multiple_of(i * ROWS, ROWS), ROWS)
            hat, _f = stats(image_v[at].astype(F32))
            first[at] = (hat * norms[0:1] + norms[2:3]).astype(BF16)
            return 0
        lax.fori_loop(0, length // ROWS, norm, 0)

    at_steps(step, chains, ATTENTION_PLANS)

    on(step, {0: lambda: load_tile(0).wait()})
    for i in range(1, 6):
        on(step, {max(2 * i - 2, first_after(ATTENTION_PLANS, i)): lambda i=i: load_tile(i).start()})
        on(step, {2 * i: lambda i=i: load_tile(i).wait()})
    on(step, {max(1, first_after(ATTENTION_PLANS, "O")): lambda: load_out.start()})
    on(step, {row0: lambda: load_out.wait()})

    @pl.when(step < head0)
    def _():
        gains = qk_gains[...].astype(F32)
        gains = jnp.concatenate([gains] * (tile // HD), axis=1)
        w = tiles[lax.rem(lax.div(step, 2), 2), lax.rem(step, 2)].reshape(-1, tile)
        project_step(step, nn(first[...], w), gains, (qn_s, kn_s, v_s), (qn, kn, v, q_raw, k_raw))

    @pl.when((step >= head0) & (step < row0))
    def _():
        cols = pl.ds(pl.multiple_of((step - head0) * PAIR, PAIR), PAIR)
        attend_step(qn_s[:, cols], kn_s[:, cols], v_s[:, cols], mixed_s, cols, mixed, inverse)

    @pl.when(step >= row0)
    def _():
        at = pl.ds(pl.multiple_of((step - row0) * ROWS, ROWS), ROWS)
        w0, w1 = (out_w[t].reshape(-1, half) for t in range(2))
        value = image_v[at].astype(F32) + nt(mixed_s[at, :half], w0) + nt(mixed_s[at, half:], w1)
        middle[...] = value
        hat, _f = stats(value)
        second[...] = (hat * norms[1:2] + norms[3:4]).astype(BF16)

    @pl.when(step == pl.num_programs(0) - 1)
    def _():
        follow(chains, ATTENTION_END)
        for name, stages in ATTENTION_LEAVES:
            chains[name].rest(0, stages - 1)
        wait(own_cot[1], keep_image)


def attention(qk_gains, q, o, u, d, tokens, cot, zs):
    rows = q.shape[0]
    length, width = 2 * tokens.shape[1], tokens.shape[2]
    half = o.shape[1]
    pairs = 2 * half // PAIR
    head0, row0 = PROJECT_STEPS, PROJECT_STEPS + pairs
    tile = half // 2
    tiles = lambda part: pl.BlockSpec((length, tile), lambda s: (0, tile_of(part, s)))
    heads = clipped((length, PAIR), 1, head0, pairs)
    by_rows = clipped((ROWS, width), 0, row0, length // ROWS)
    bf = jax.ShapeDtypeStruct((length, 2 * half), BF16)
    square = jax.ShapeDtypeStruct((length, width), BF16)
    f32 = lambda *shape: jax.ShapeDtypeStruct(shape, F32)
    whole = lambda s: jax.ShapeDtypeStruct((2, zs, 2, 2) + s.shape, BF16)
    store = pltpu.VMEM((length, 2 * half), BF16)
    same = lambda s: pltpu.VMEM(s.shape, BF16)
    return pl.pallas_call(
        functools.partial(attention_body, zs, pairs),
        grid=(row0 + length // ROWS,),
        in_specs=[full(qk_gains.shape)] + [HBM] * 6,
        out_specs=[full((length, width)), tiles(2), tiles(1), tiles(0), tiles(2), tiles(1), heads, heads, by_rows, by_rows,
                   full((8, width))] + [HBM] * 6,
        out_shape=[square, bf, bf, bf, bf, bf, bf, f32(length, 2 * half), f32(length, width), square, f32(8, width),
                   square, square, whole(q), whole(o), whole(u), whole(d)],
        scratch_shapes=[pltpu.VMEM((length, width), BF16), store, store, store, store, pltpu.VMEM((2, zs, 2, 2, rows, half), BF16),
                        pltpu.VMEM((2, 2, zs, 2, 2, rows, tile), BF16), same(q), same(o), same(u), same(d),
                        pltpu.VMEM((length // 2, width), BF16), pltpu.VMEM((zs, 2, 2, rows, PAIR), BF16),
                        DMA((12,)), DMA((15, gather_sems(zs))), DMA((15, gather_sems(zs))), DMA((2, 2, CHUNKS))],
        compiler_params=params(0),
        name="attention",
    )(qk_gains, q, o, u, d, tokens, cot)


def gelu_parts(v):
    bell = jnp.exp(v * v * -0.5)
    t = 1.0 / (1.0 + (0.3275911 * 0.7071067811865476) * jnp.abs(v))
    poly = t * (0.127414796 + t * (-0.142248368 + t * (0.7107068705 + t * (-0.7265760135 + t * 0.5307027145))))
    tail = poly * bell
    return jnp.where(v >= 0, 1.0 - tail, tail), bell * 0.3989422804014327


def feed_body(
    zs, second, cot, middle, _u, _d,
    result, grad_second, grad_u, grad_d, state_0, state_1, state_2, state_3, outputs, whole_u, whole_d,
    acc, second_t, cot_t, active, grad_hidden, tiles, g, tile_sem, misc_sem, send, recv, *landings,
):
    step = pl.program_id(0)
    p = Place(zs)
    length = second.shape[0]
    n = FF_GROUP
    state_refs = (state_0, state_1, state_2, state_3)
    chains = {}
    for j in (1, 2, 3):
        for i, (name, w, orders) in enumerate((("U", whole_u, U_ORDERS), ("D", whole_d, D_ORDERS))):
            k = 2 * j - 2 + i
            chains[f"{name}{j}"] = Gather(p, None, w, j * n, n, orders[j], send.at[k], recv.at[k], FEED_SINCE[j - 1])
    at, states = iter(landings), []
    for j in range(2):
        for k in range(2):
            i = 2 * j + k
            held = lambda x, z, y, j=j, k=k: g.at[k, j, x, z, y, p.c]
            s = Scatter(p, FEED_ORDERS[i], held, g.at[k, j, :, :, :, 1 - p.c], [next(at), next(at)], send.at[6 + i], recv.at[6 + i])
            chains[f"{'ud'[k]}{j}"] = s
            states.append(pltpu.make_async_copy(s.state(), state_refs[i], misc_sem.at[1 + i]))
    init = pltpu.make_async_copy(middle, acc, misc_sem.at[0])
    mine = pl.ds(pl.multiple_of(p.x * (length // 2), length // 2), length // 2)
    own = pltpu.make_async_copy(result.at[mine], outputs.at[p.x], misc_sem.at[9])
    outs = [pltpu.make_async_copy(g.at[k, j], (grad_u, grad_d)[k].at[j - 2], misc_sem.at[5 + 2 * (j - 2) + k])
            for j in (2, 3) for k in range(2)]

    def loads(s):
        j, t = (s // 2, s % 2) if isinstance(s, int) else (lax.div(s, 2), lax.rem(s, 2))
        slot = t
        cols = pl.ds(j * n if isinstance(s, int) else pl.multiple_of(j * n, n), n)
        return [pltpu.make_async_copy(w.at[t, :, :, :, :, cols], tiles.at[k, slot], tile_sem.at[k, slot])
                for k, w in ((0, whole_u), (1, whole_d))]

    @pl.when(step == 0)
    def _():
        meet(p)
        start(*loads(0))
        start(*loads(1))
        init.start()
        follow(chains, FEED_PLANS[0])
        second_t[...] = second[...].T
        cot_t[...] = cot[...].T
        grad_second[...] = jnp.zeros_like(grad_second)

    at_steps(step, chains, ((),) + FEED_PLANS[2::2])
    for s in range(2, 8):
        here = first_after(FEED_PLANS, f"U{s // 2}"), first_after(FEED_PLANS, f"D{s // 2}")
        on(step, {max(s - 1, (max(here) + 1) // 2): lambda s=s: start(*loads(s))})
    on(step, {7: lambda: start(*outs[:2])})
    wait(*loads(step))

    @pl.when(step == 0)
    def _():
        init.wait()
    slot = lax.rem(step, 2)
    w_up = tiles[0, slot].reshape(-1, n)
    w_down = tiles[1, slot].reshape(-1, n)
    for i in range(length // ROWS):
        at = slice(i * ROWS, (i + 1) * ROWS)
        hidden = nn(second[at], w_up)
        grad_active = nn(cot[at], w_down)
        cumulative, density = gelu_parts(hidden)
        a = (hidden * cumulative).astype(BF16)
        b = (grad_active * (cumulative + hidden * density)).astype(BF16)
        active[at] = a
        grad_hidden[at] = b
        acc[at] += nt(a, w_down)
        grad_second[at] += nt(b, w_up)
    at_steps(step, chains, FEED_PLANS[1::2])
    j, t = lax.div(step, 2), lax.rem(step, 2)
    shape = g.shape[3:]
    g[0, j, t] = nn(second_t[...], grad_hidden[...]).astype(BF16).reshape(shape)
    g[1, j, t] = nn(cot_t[...], active[...]).astype(BF16).reshape(shape)

    @pl.when(step == pl.num_programs(0) - 1)
    def _():
        start(*outs[2:])
        result[...] = acc[...].astype(BF16)
        own.start()
        follow(chains, FEED_END)
        start(*states)
        wait(*states)
        wait(*outs)
        own.wait()


def feed(second, cot, middle, whole_u, whole_d, zs):
    length, width = second.shape
    rows, n = whole_u.shape[4], FF_GROUP
    same = lambda a: jax.ShapeDtypeStruct(a.shape, a.dtype)
    tile = (2, zs, 2, 2, rows, n)
    grads = jax.ShapeDtypeStruct((2,) + tile, BF16)
    square = pltpu.VMEM((length, width), BF16)
    strip = pltpu.VMEM((length, n), BF16)
    scratch = [pltpu.VMEM((length, width), F32), square, square, strip, strip, pltpu.VMEM((2, 2) + tile[1:], BF16),
               pltpu.VMEM((2, 4) + tile, BF16), DMA((2, 2)), DMA((10,)), DMA((10, gather_sems(zs))), DMA((10, gather_sems(zs)))]
    for i in range(4):
        scratch += landing(zs, rows, n, FEED_ORDERS[i])[:2]
    return pl.pallas_call(
        functools.partial(feed_body, zs),
        grid=(8,),
        in_specs=[full(second.shape), full(cot.shape), HBM, HBM, HBM],
        out_specs=[full(second.shape), full(second.shape)] + [HBM] * 9,
        out_shape=[same(second), jax.ShapeDtypeStruct((length, width), F32), grads, grads]
        + [jax.ShapeDtypeStruct(rest_shape(zs, rows, n, o[0]), BF16) for o in FEED_ORDERS]
        + [jax.ShapeDtypeStruct((2, length // 2, width), BF16), same(whole_u), same(whole_d)],
        scratch_shapes=scratch,
        input_output_aliases={3: 9, 4: 10},
        compiler_params=params(1),
        name="feed",
    )(second, cot, middle, whole_u, whole_d)


def attend_back_step(between, gains, go, inv, query, keys, values, q_raw, k_raw, mixed, grad_q, grad_k, grad_v, grad_gains):
    length = query.shape[0]
    lanes = lax.broadcasted_iota(jnp.int32, (1, PAIR), 1)
    first = lanes < HD
    zero = jnp.zeros((), BF16)
    go = go.astype(F32)
    product = go * mixed.astype(F32) * inv
    go_inv = (go * inv).astype(BF16)
    heads = []
    for h, mask in ((0, first), (1, ~first)):
        delta = -jnp.sum(jnp.where(mask, product, 0.0), -1, keepdims=True)
        high = delta.astype(BF16)
        low = (delta - high.astype(F32)).astype(BF16)
        spare = (1 - h) * HD
        grad_aug = jnp.where(mask, go_inv, jnp.where(lanes == spare, high, jnp.where(lanes == spare + 1, low, zero)))
        values_aug = jnp.where(mask, values, jnp.where((lanes == spare) | (lanes == spare + 1), jnp.ones((), BF16), zero))
        heads.append((jnp.where(mask, query, zero), jnp.where(mask, keys, zero), jnp.where(mask, go_inv, zero), grad_aug, values_aug))
    dq = []
    dk = jnp.zeros((length, PAIR), F32)
    dv = jnp.zeros((length, PAIR), F32)
    for i in range(length // Q_TILE):
        if 2 * i == length // Q_TILE:
            between()
        at = slice(i * Q_TILE, (i + 1) * Q_TILE)
        part = jnp.zeros((Q_TILE, PAIR), F32)
        for qm, km, gm, ga, va in heads:
            exponent = jnp.exp(nt(km, qm[at]))
            grad_scores = (exponent * nt(va, ga[at])).astype(BF16)
            dv = dv + nn(exponent.astype(BF16), gm[at])
            dk = dk + nn(grad_scores, qm[at])
            part = part + lax.dot_general(grad_scores, km, (((0,), (0,)), ((), ())), preferred_element_type=F32)
        dq.append(part)
    dq = jnp.concatenate(dq, axis=0)
    grad_v[...] = dv.astype(BF16)
    matrix = head_mean_matrix(PAIR)
    hat, factor = head_stats(q_raw.astype(F32), matrix)
    scale = HD ** -0.5
    sum_q = jnp.sum(dq * hat, 0, keepdims=True) * scale
    grad_q[...] = head_back(dq * gains[0:1] * scale, hat, factor, matrix).astype(BF16)
    hat, factor = head_stats(k_raw.astype(F32), matrix)
    sum_k = jnp.sum(dk * hat, 0, keepdims=True)
    grad_k[...] = head_back(dk * gains[1:2], hat, factor, matrix).astype(BF16)
    grad_gains[...] += jnp.concatenate([sum_q, sum_k], axis=0)


def backward_body(
    zs, rows_steps, norms, gains, cot, grad_second, middle, mixed_rows, w, qn, kn, v, q_raw, k_raw, mixed, inverse,
    grads_u, grads_d, state_0, state_1, state_2, state_3, result, _outputs,
    grad_middle, grad_q, grad_k, grad_v, grad_gains, sums, shard_u, shard_d, shard_o, outputs,
    grad_mixed, acc, g_o, own_late, load_sem, swap_sem, send, recv, *landings,
):
    step = pl.program_id(0)
    p = Place(zs)
    n = FF_GROUP
    half = w.shape[2]
    at = iter(landings)
    take = lambda count: [next(at) for _ in range(count)]
    chains, loads = {}, []

    def out(k, j):
        return (shard_u, shard_d)[k].at[:, pl.ds(j * n, n)]

    for i, state in enumerate((state_0, state_1, state_2, state_3)):
        j, k = divmod(i, 2)
        order = FEED_ORDERS[i]
        own = next(at)

        def held(x, z, y, own=own, order=order):
            return own.at[tuple(index for e, index in zip("xzy", (x, z, y)) if e != order[0])]
        chains[f"{'ud'[k]}{j}"] = Scatter(p, order, held, None, [None, None] + take(2), send.at[i], recv.at[i], out(k, j))
        loads.append(pltpu.make_async_copy(state, own, load_sem.at[i]))
    for i in range(4):
        j, k = divmod(i, 2)
        grad = (grads_u, grads_d)[k].at[j]
        chains[f"{'ud'[k]}{2 + j}"] = Scatter(
            p, LATE_ORDERS[i], lambda x, z, y, i=i: own_late.at[i, x, z, y], grad.at[:, :, :, 1 - p.c], take(4),
            send.at[4 + i], recv.at[4 + i], out(k, 2 + j))
        loads.append(pltpu.make_async_copy(grad.at[:, :, :, p.c], own_late.at[i], load_sem.at[4 + i]))
    chains["o"] = Scatter(p, O_BACK_ORDER, lambda x, z, y: g_o.at[x, z, y, p.c], g_o.at[:, :, :, 1 - p.c], take(4),
                          send.at[8], recv.at[8], shard_o)
    half_length = result.shape[0] // 2
    chains["R"] = Swap(p, half_rows(result, 1 - p.x, half_length), outputs.at[p.x], swap_sem)

    @pl.when(step == 0)
    def _():
        start(*loads)
        meet(p)
        wait(*loads)
        follow(chains, BACKWARD_PLANS[0])

    at_steps(step, chains, ((),) + BACKWARD_PLANS[1:rows_steps] + BACKWARD_PLANS[rows_steps::2])

    def between():
        at_steps(step, chains, ((),) * rows_steps + BACKWARD_PLANS[rows_steps + 1::2])

    @pl.when(step == 0)
    def _():
        sums[...] = jnp.zeros_like(sums)
        acc[...] = jnp.zeros_like(acc)
        grad_gains[...] = jnp.zeros_like(grad_gains)

    @pl.when(step < rows_steps)
    def _():
        hat, factor = stats(middle[...])
        gs = grad_second[...]
        gm = cot[...].astype(F32) + back(gs * norms[1:2], hat, factor)
        grad_middle[...] = gm
        branch_grad = gm.astype(BF16)
        branch_t = branch_grad.T
        here = pl.ds(pl.multiple_of(step * ROWS, ROWS), ROWS)
        for t in range(2):
            cols = slice(t * half, (t + 1) * half)
            grad_mixed[here, cols] = nn(branch_grad, w[t]).astype(BF16)
            acc[t] += nn(branch_t, mixed_rows[:, cols])
        sums[0:1] += jnp.sum(gs * hat, 0, keepdims=True)
        sums[1:2] += jnp.sum(gs, 0, keepdims=True)

    @pl.when(step == rows_steps - 1)
    def _():
        g_o[...] = acc[...].astype(BF16).reshape(g_o.shape)

    @pl.when(step >= rows_steps)
    def _():
        cols = pl.ds(pl.multiple_of((step - rows_steps) * PAIR, PAIR), PAIR)
        attend_back_step(between, gains, grad_mixed[:, cols], inverse[...], qn[...], kn[...], v[...], q_raw[...], k_raw[...], mixed[...],
                         grad_q, grad_k, grad_v, grad_gains)

    @pl.when(step == pl.num_programs(0) - 1)
    def _():
        follow(chains, BACKWARD_END)


def backward(norms, gains, cot, grad_second, middle, mixed, w, kept, inverse, grads_u, grads_d, states, result, outputs, zs):
    length, width = middle.shape
    half = w.shape[2]
    rows, n = grads_u.shape[5], FF_GROUP
    row_steps, pairs = length // ROWS, 2 * half // PAIR
    row = clipped((ROWS, width), 0, 0, row_steps)
    head = clipped((length, PAIR), 1, row_steps, pairs)
    heads = jax.ShapeDtypeStruct((length, 2 * half), BF16)
    f32 = lambda *shape: jax.ShapeDtypeStruct(shape, F32)
    scratch = [
        pltpu.VMEM((length, 2 * half), BF16), pltpu.VMEM(w.shape, F32), pltpu.VMEM((2, zs, 2, 2, rows, half), BF16),
        pltpu.VMEM((4, 2, zs, 2, rows, n), BF16), DMA((8,)), DMA((2, CHUNKS)),
        DMA((9, scatter_sems(zs))), DMA((9, scatter_sems(zs))),
    ]
    for i in range(4):
        scratch += [pltpu.VMEM(rest_shape(zs, rows, n, FEED_ORDERS[i][0]), BF16)] + landing(zs, rows, n, FEED_ORDERS[i], 2)
    for i in range(4):
        scratch += landing(zs, rows, n, LATE_ORDERS[i])
    scratch += landing(zs, rows, half, O_BACK_ORDER)
    return pl.pallas_call(
        functools.partial(backward_body, zs, row_steps),
        grid=(row_steps + pairs,),
        in_specs=[full(norms.shape), full(gains.shape), row, row, row, row, full(w.shape)] + [head] * 7 + [HBM] * 8,
        out_specs=[row, head, head, head, full((2, PAIR)), full((2, width)), full((rows, 4 * n)), full((rows, 4 * n)),
                   full((rows, half)), HBM],
        out_shape=[f32(length, width), heads, heads, heads, f32(2, PAIR), f32(2, width), f32(rows, 4 * n), f32(rows, 4 * n),
                   f32(rows, half), jax.ShapeDtypeStruct((2, length // 2, width), BF16)],
        scratch_shapes=scratch,
        input_output_aliases={21: 9},
        compiler_params=params(2),
        name="backward",
    )(norms, gains, cot, grad_second, middle, mixed, w, *kept, mixed, inverse, grads_u, grads_d, *states, result, outputs)


PART_GROUP = 256


def closing_body(
    zs, norms, sums_second, sums_qk, image_in, first_in, grad_middle_in, gq_in, gk_in, gv_in, w_in,
    shard_q, total, grad_tokens,
    image, first, grad_middle, grads, w, first_t, acc, grad_image, g, load_sem, swap_sem, got, sum_send, sum_recv, send, recv, *landings,
):
    p = Place(zs)
    meet(p)
    length, width = image.shape
    half = grads.shape[2] // 2
    load_grads = [pltpu.make_async_copy(a, grads.at[i], load_sem.at[i]) for i, a in enumerate((gq_in, gk_in, gv_in))]
    load_first = pltpu.make_async_copy(first_in, first, load_sem.at[3])
    load_w = pltpu.make_async_copy(w_in, w, load_sem.at[4])
    load_image = pltpu.make_async_copy(image_in, image, load_sem.at[5])
    load_middle = pltpu.make_async_copy(grad_middle_in, grad_middle, load_sem.at[6])
    start(load_first, *load_grads, load_w, load_image, load_middle)
    chains = {}
    at = iter(landings)
    for i, (k, lo, m, order) in enumerate(CLOSING):
        cols = pl.ds(lo, m)
        held = lambda x, z, y, k=k, cols=cols: g.at[k, x, z, y, p.c, :, cols]
        chains[i] = Scatter(p, order, held, g.at[k, :, :, :, 1 - p.c, :, cols], [next(at) for _ in range(4)], send.at[i], recv.at[i],
                            shard_q.at[k, :, cols])
    half_length = length // 2
    chains["G"] = Swap(p, half_rows(grad_image, 1 - p.x, half_length), grad_tokens.at[p.x], swap_sem)
    chains["S"] = Sum(p, total, got, sum_send, sum_recv)
    own = pltpu.make_async_copy(half_rows(grad_image, p.x, half_length), grad_tokens.at[p.x], load_sem.at[7])

    load_first.wait()
    first_t[...] = first[...].T
    wait(*load_grads)

    def weight_grad(k):
        def one(i, _):
            t, part = lax.div(i, 3), lax.rem(i, 3)
            cols = pl.ds(pl.multiple_of(t * half + k * PART_GROUP, PART_GROUP), PART_GROUP)
            value = nn(first_t[...], grads[part, :, cols]).astype(BF16)
            g[k, t, :, :, :, :, pl.ds(pl.multiple_of(part * PART_GROUP, PART_GROUP), PART_GROUP)] = value.reshape(
                g.shape[2:6] + (PART_GROUP,))
            return 0
        lax.fori_loop(0, 6, one, 0)

    weight_grad(0)
    follow(chains, CLOSING_PLANS[0])
    weight_grad(1)
    follow(chains, CLOSING_PLANS[1])
    load_w.wait()
    acc[...] = jnp.zeros_like(acc)

    def to_first(i, _):
        t, part = lax.div(i, 3), lax.rem(i, 3)
        cols = pl.ds(pl.multiple_of(t * half, half), half)
        acc[...] += nt(grads[part, :, cols], w[t, :, pl.ds(pl.multiple_of(part * half, half), half)])
        return 0
    lax.fori_loop(0, 3, to_first, 0)
    follow(chains, CLOSING_PLANS[2])
    lax.fori_loop(3, 6, to_first, 0)
    wait(load_image, load_middle)
    follow(chains, CLOSING_PLANS[3])

    def norm_back(i, carry):
        at = pl.ds(pl.multiple_of(i * ROWS, ROWS), ROWS)
        hat, factor = stats(image[at].astype(F32))
        gf = acc[at]
        grad_image[at] = (grad_middle[at] + back(gf * norms[0:1], hat, factor)).astype(BF16)
        return carry[0] + jnp.sum(gf * hat, 0, keepdims=True), carry[1] + jnp.sum(gf, 0, keepdims=True)
    zero = jnp.zeros((1, width), F32)
    sum_hat, sum_all = lax.fori_loop(0, length // ROWS, norm_back, (zero, zero))
    own.start()
    total[...] = jnp.zeros_like(total)
    total[0:1] = sum_hat
    total[1:2] = sum_all
    total[2:4] = sums_second[...]
    total[4:6, 0:PAIR] = sums_qk[...]
    follow(chains, CLOSING_END)
    own.wait()


def closing(norms, sums_second, sums_qk, image, first, grad_middle, gq, gk, gv, w, zs):
    length, width = image.shape
    rows = width // (4 * zs)
    wide = 3 * PART_GROUP
    square = pltpu.VMEM((length, width), BF16)
    scratch = [
        square, square, pltpu.VMEM((length, width), F32), pltpu.VMEM((3,) + gq.shape, BF16), pltpu.VMEM(w.shape, BF16), square,
        pltpu.VMEM((length, width), F32), square, pltpu.VMEM((2, 2, zs, 2, 2, rows, wide), BF16), DMA((8,)), DMA((2, CHUNKS)),
        pltpu.VMEM((zs + 2, 8, width), F32), DMA((zs + 2,)), DMA((zs + 2,)),
        DMA((len(CLOSING), scatter_sems(zs))), DMA((len(CLOSING), scatter_sems(zs))),
    ]
    for k, lo, m, order in CLOSING:
        scratch += landing(zs, rows, m, order)
    return pl.pallas_call(
        functools.partial(closing_body, zs),
        in_specs=[WHOLE_VMEM] * 3 + [HBM] * 7,
        out_specs=[WHOLE_VMEM, WHOLE_VMEM, HBM],
        out_shape=[jax.ShapeDtypeStruct((2, rows, wide), F32), jax.ShapeDtypeStruct((8, width), F32),
                   jax.ShapeDtypeStruct((2, length // 2, width), BF16)],
        scratch_shapes=scratch,
        compiler_params=params(3),
        name="closing",
    )(norms, sums_second, sums_qk, image, first, grad_middle, gq, gk, gv, w)


def whole_images(tokens, cotangent, w_qkv, wo_t, w_up, w_down_t, norm_gains, norm_shifts, qk_gains):
    zs = lax.axis_size("fsdp") // 4
    rows = w_qkv.shape[0]
    width = tokens.shape[2]
    half = w_qkv.shape[2]
    cols = 3 * half
    side = jnp.concatenate([norm_gains, norm_shifts, jnp.zeros((rows, 124), BF16)], axis=1)
    shard_q = jnp.concatenate([w_qkv.reshape(rows, cols), side], axis=1)
    first, qn, kn, v, q_raw, k_raw, mixed, inverse, middle, second, norms, image, cot, whole_q, whole_o, whole_u, whole_d = attention(
        qk_gains, shard_q, wo_t, w_up, w_down_t, tokens, cotangent, zs
    )
    result, grad_second, grads_u, grads_d, *states, outputs, whole_u, whole_d = feed(
        second, cot, middle, whole_u, whole_d, zs
    )
    qkv = whole_q.reshape(2, width, cols + 128)
    grad_middle, gq, gk, gv, sums_qk, sums_second, shard_u, shard_d, shard_o, outputs = backward(
        norms, jnp.tile(qk_gains.astype(F32), (1, 2)), cot, grad_second, middle, mixed, whole_o.reshape(2, width, half),
        (qn, kn, v, q_raw, k_raw), inverse, grads_u, grads_d, states, result, outputs, zs
    )
    grad_q, small, grad_tokens = closing(norms, sums_second, sums_qk, image, first, grad_middle, gq, gk, gv, qkv, zs)
    grad_q = grad_q.reshape(2, rows, 3, PART_GROUP).transpose(1, 2, 0, 3).reshape(w_qkv.shape)
    mine = lax.dynamic_slice_in_dim(small, lax.axis_index("fsdp") * rows, rows, 1)
    return (
        outputs,
        grad_tokens.astype(F32),
        grad_q,
        shard_o,
        shard_u,
        shard_d,
        jnp.stack([mine[0], mine[2]], 1),
        jnp.stack([mine[1], mine[3]], 1),
        small[4:6, :HD] + small[4:6, HD:2 * HD],
    )


def layer(tokens, *rest):
    if tokens.shape[0] == lax.axis_size("tensor") == 2 and lax.axis_size("fsdp") % 4 == 0:
        return whole_images(tokens, *rest)
    return per_device(tokens, *rest)


def solution(mesh):
    in_specs = (
        P("fsdp", "tensor", None),
        P("fsdp", "tensor", None),
        P("fsdp", None, "tensor"),
        P("fsdp", "tensor"),
        P("fsdp", "tensor"),
        P("fsdp", "tensor"),
        P("fsdp", None),
        P("fsdp", None),
        P(),
    )
    out_specs = (
        P("fsdp", "tensor", None),
        P("fsdp", "tensor", None),
        P("fsdp", None, "tensor"),
        P("fsdp", "tensor"),
        P("fsdp", "tensor"),
        P("fsdp", "tensor"),
        P("fsdp", None),
        P("fsdp", None),
        P(),
    )
    return jax.shard_map(
        layer, mesh=mesh, in_specs=in_specs, out_specs=out_specs, check_vma=False
    )
```

```python
import functools

import jax
import jax.numpy as jnp
from jax import lax
from jax.experimental import pallas as pl
from jax.experimental.pallas import tpu as pltpu
from jax.sharding import PartitionSpec as P

HD = 64


EPSILON = 1e-06


def norm_stats(value):
    center = value - jnp.mean(value, -1, keepdims=True)
    factor = lax.rsqrt(jnp.mean(center * center, -1, keepdims=True) + EPSILON)
    return (center * factor, factor)


def norm_back(grad_hat, normed, factor):
    return factor * (
        grad_hat
        - jnp.mean(grad_hat, -1, keepdims=True)
        - normed * jnp.mean(grad_hat * normed, -1, keepdims=True)
    )


def contract_rows(left, right):
    return lax.dot_general(
        left, right, (((0,), (0,)), ((), ())), preferred_element_type=jnp.float32
    )


def contract_cols(left, right):
    return lax.dot_general(
        left, right, (((1,), (1,)), ((), ())), preferred_element_type=jnp.float32
    )


def per_device(tokens, cotangent, w_qkv, wo_t, w_up, w_down_t, norm_gains, norm_shifts, qk_gains):
    local_rows = tokens.shape[1]
    width = tokens.shape[2]
    head_cols = w_qkv.shape[2]
    local_heads = head_cols // HD
    hidden_cols = w_up.shape[1]
    tensor_count = lax.axis_size("tensor")
    full_len = local_rows * tensor_count
    block = min(512, full_len)
    blocks = full_len // block
    gain_query = qk_gains[0].astype(jnp.float32)
    gain_keys = qk_gains[1].astype(jnp.float32)
    scale_query = HD ** (-0.5)

    def fetch():
        return (
            lax.all_gather(w_qkv, "fsdp", axis=0, tiled=True),
            lax.all_gather(wo_t, "fsdp", axis=0, tiled=True),
            lax.all_gather(w_up, "fsdp", axis=0, tiled=True),
            lax.all_gather(w_down_t, "fsdp", axis=0, tiled=True),
            lax.all_gather(norm_gains, "fsdp", axis=0, tiled=True),
            lax.all_gather(norm_shifts, "fsdp", axis=0, tiled=True),
        )

    def forward(weights, inputs):
        whole_qkv, whole_out, whole_up, whole_down, gains, shifts = weights
        gains = gains.astype(jnp.float32)
        shifts = shifts.astype(jnp.float32)
        flat_qkv = whole_qkv.reshape(width, 3 * head_cols)
        residual = inputs.astype(jnp.float32)
        first_hat, first_factor = norm_stats(residual)
        first = (first_hat * gains[:, 0] + shifts[:, 0]).astype(jnp.bfloat16)
        piece = lax.all_gather(first, "tensor", axis=0, tiled=True)
        first_full = piece
        joined = jnp.dot(piece, flat_qkv, preferred_element_type=jnp.float32)
        joined = joined.reshape(full_len, 3, local_heads, HD)
        query_hat, query_factor = norm_stats(joined[:, 0])
        keys_hat, keys_factor = norm_stats(joined[:, 1])
        query_n = (query_hat * gain_query * scale_query).astype(jnp.bfloat16)
        keys_n = (keys_hat * gain_keys).astype(jnp.bfloat16)
        values = joined[:, 2].astype(jnp.bfloat16)

        def attend(query_block):
            scores = jnp.einsum(
                "qhd,khd->hqk", query_block, keys_n, preferred_element_type=jnp.float32
            )
            largest = jnp.max(scores, -1, keepdims=True)
            exponent = jnp.exp(scores - largest)
            total_sum = jnp.sum(exponent, -1, keepdims=True)
            probs_low = (exponent / total_sum).astype(jnp.bfloat16)
            mixed_block = jnp.einsum(
                "hqk,khd->qhd", probs_low, values, preferred_element_type=jnp.float32
            )
            return (mixed_block.astype(jnp.bfloat16), (largest + jnp.log(total_sum))[..., 0])

        mixed, log_total = lax.map(attend, query_n.reshape(blocks, block, local_heads, HD))
        mixed = mixed.reshape(full_len, head_cols)
        middle = residual + lax.psum_scatter(
            contract_cols(mixed, whole_out), "tensor", scatter_dimension=0, tiled=True
        )
        second_hat, second_factor = norm_stats(middle)
        second = (second_hat * gains[:, 1] + shifts[:, 1]).astype(jnp.bfloat16)
        piece = lax.all_gather(second, "tensor", axis=0, tiled=True)
        hidden = jnp.dot(piece, whole_up, preferred_element_type=jnp.float32)
        active = jax.nn.gelu(hidden, approximate=False).astype(jnp.bfloat16)
        result = (
            middle
            + lax.psum_scatter(
                contract_cols(active, whole_down).astype(jnp.bfloat16),
                "tensor",
                scatter_dimension=0,
                tiled=True,
            ).astype(jnp.float32)
        ).astype(jnp.bfloat16)
        kept = (
            first_hat,
            first_factor,
            first_full,
            query_hat,
            query_factor,
            keys_hat,
            keys_factor,
            query_n,
            keys_n,
            values,
            mixed,
            log_total,
            second_hat,
            second_factor,
            piece,
            hidden,
            active,
        )
        return (kept, result)

    def backward(weights, kept, grad_out):
        whole_qkv, whole_out, whole_up, whole_down, gains, shifts = weights
        gains = gains.astype(jnp.float32)
        flat_qkv = whole_qkv.reshape(width, 3 * head_cols)
        (
            first_hat,
            first_factor,
            first_full,
            query_hat,
            query_factor,
            keys_hat,
            keys_factor,
            query_n,
            keys_n,
            values,
            mixed_keep,
            log_total,
            second_hat,
            second_factor,
            second_full,
            hidden,
            active,
        ) = kept
        piece = lax.all_gather(grad_out, "tensor", axis=0, tiled=True)
        grad_full = piece
        grad_active = jnp.dot(piece, whole_down, preferred_element_type=jnp.float32)
        grad_down = contract_rows(grad_full, active)
        unused_value, gelu_pull = jax.vjp(
            lambda value: jax.nn.gelu(value, approximate=False), hidden
        )
        grad_hidden = gelu_pull(grad_active)[0].astype(jnp.bfloat16)
        grad_up = contract_rows(second_full, grad_hidden)
        grad_second = lax.psum_scatter(
            contract_cols(grad_hidden, whole_up), "tensor", scatter_dimension=0, tiled=True
        )
        grad_middle = grad_out.astype(jnp.float32) + norm_back(
            grad_second * gains[:, 1], second_hat, second_factor
        )
        grad_branch = grad_middle.astype(jnp.bfloat16)
        piece = lax.all_gather(grad_branch, "tensor", axis=0, tiled=True)
        grad_mixed = jnp.dot(piece, whole_out, preferred_element_type=jnp.float32)
        grad_out_w = contract_rows(piece, mixed_keep)
        grad_mixed = grad_mixed.astype(jnp.bfloat16)
        grad_mixed = grad_mixed.reshape(blocks, block, local_heads, HD)

        def attend_back(carry, item):
            grad_keys_sum, grad_values_sum = carry
            query_block, grad_block, log_block = item
            scores = jnp.einsum(
                "qhd,khd->hqk", query_block, keys_n, preferred_element_type=jnp.float32
            )
            probs = jnp.exp(scores - log_block[..., None])
            grad_probs = jnp.einsum(
                "qhd,khd->hqk", grad_block, values, preferred_element_type=jnp.float32
            )
            delta = jnp.sum(probs * grad_probs, -1, keepdims=True)
            grad_scores = (probs * (grad_probs - delta)).astype(jnp.bfloat16)
            grad_query_block = jnp.einsum(
                "hqk,khd->qhd", grad_scores, keys_n, preferred_element_type=jnp.float32
            )
            grad_keys_sum = grad_keys_sum + jnp.einsum(
                "hqk,qhd->khd", grad_scores, query_block, preferred_element_type=jnp.float32
            )
            grad_values_sum = grad_values_sum + jnp.einsum(
                "hqk,qhd->khd",
                probs.astype(jnp.bfloat16),
                grad_block,
                preferred_element_type=jnp.float32,
            )
            return ((grad_keys_sum, grad_values_sum), grad_query_block)

        empty_heads = jnp.zeros((full_len, local_heads, HD), jnp.float32)
        (grad_keys_n, grad_values), grad_query_n = lax.scan(
            attend_back,
            (empty_heads, empty_heads),
            (query_n.reshape(blocks, block, local_heads, HD), grad_mixed, log_total),
        )
        grad_query_n = grad_query_n.reshape(full_len, local_heads, HD)
        grad_query = norm_back(grad_query_n * gain_query * scale_query, query_hat, query_factor)
        grad_keys = norm_back(grad_keys_n * gain_keys, keys_hat, keys_factor)
        qk_grad = jnp.stack(
            [
                jnp.sum(grad_query_n * query_hat * scale_query, (0, 1)),
                jnp.sum(grad_keys_n * keys_hat, (0, 1)),
            ]
        )
        grad_joined = jnp.stack([grad_query, grad_keys, grad_values], 1).astype(jnp.bfloat16)
        grad_joined = grad_joined.reshape(full_len, 3 * head_cols)
        grad_qkv = contract_rows(first_full, grad_joined).reshape(width, 3, head_cols)
        grad_first = lax.psum_scatter(
            contract_cols(grad_joined, flat_qkv).astype(jnp.bfloat16),
            "tensor",
            scatter_dimension=0,
            tiled=True,
        ).astype(jnp.float32)
        grad_input = grad_middle + norm_back(grad_first * gains[:, 0], first_hat, first_factor)
        gain_grad = jnp.stack(
            [jnp.sum(grad_first * first_hat, 0), jnp.sum(grad_second * second_hat, 0)], 1
        )
        shift_grad = jnp.stack([jnp.sum(grad_first, 0), jnp.sum(grad_second, 0)], 1)
        return (
            (grad_qkv, grad_out_w, grad_up, grad_down, gain_grad, shift_grad, qk_grad),
            grad_input,
        )

    def micro_step(totals, item):
        inputs, grad_out = item
        forward_weights = fetch()
        kept, result = forward(forward_weights, inputs)
        backward_weights = fetch()
        grads, grad_input = backward(backward_weights, kept, grad_out)
        totals = tuple((total + part for total, part in zip(totals, grads)))
        return (totals, (result, grad_input))

    out_cols_count = wo_t.shape[1]
    start_sums = (
        jnp.zeros((width, 3, head_cols), jnp.float32),
        jnp.zeros((width, out_cols_count), jnp.float32),
        jnp.zeros((width, hidden_cols), jnp.float32),
        jnp.zeros((width, hidden_cols), jnp.float32),
        jnp.zeros((width, 2), jnp.float32),
        jnp.zeros((width, 2), jnp.float32),
        jnp.zeros((2, HD), jnp.float32),
    )
    totals, (outputs, grad_tokens) = lax.scan(micro_step, start_sums, (tokens, cotangent))
    out_total = totals[1]
    grad_qkv, grad_out_w, grad_up, grad_down = (
        lax.psum_scatter(
            totals[0].astype(jnp.bfloat16), "fsdp", scatter_dimension=0, tiled=True
        ).astype(jnp.float32),
        lax.psum_scatter(
            out_total.astype(jnp.bfloat16), "fsdp", scatter_dimension=0, tiled=True
        ).astype(jnp.float32),
        lax.psum_scatter(
            totals[2].astype(jnp.bfloat16), "fsdp", scatter_dimension=0, tiled=True
        ).astype(jnp.float32),
        lax.psum_scatter(
            totals[3].astype(jnp.bfloat16), "fsdp", scatter_dimension=0, tiled=True
        ).astype(jnp.float32),
    )
    gain_total, shift_total, qk_total = lax.psum(
        (totals[4], totals[5], totals[6]), ("fsdp", "tensor")
    )
    own_rows = width // lax.axis_size("fsdp")
    offset = lax.axis_index("fsdp") * own_rows
    gain_part = lax.dynamic_slice_in_dim(gain_total, offset, own_rows, 0)
    shift_part = lax.dynamic_slice_in_dim(shift_total, offset, own_rows, 0)
    return (
        outputs,
        grad_tokens,
        grad_qkv,
        grad_out_w,
        grad_up,
        grad_down,
        gain_part,
        shift_part,
        qk_total,
    )


PAIR = 2 * HD
F32, BF16 = jnp.float32, jnp.bfloat16
LIMIT = 60 << 20


def nn(a, b):
    return lax.dot_general(a, b, (((1,), (0,)), ((), ())), preferred_element_type=F32)


def nt(a, b):
    return lax.dot_general(a, b, (((1,), (1,)), ((), ())), preferred_element_type=F32)


def stats(value):
    center = value - jnp.mean(value, -1, keepdims=True)
    factor = lax.rsqrt(jnp.mean(center * center, -1, keepdims=True) + EPSILON)
    return center * factor, factor


def back(grad_hat, normed, factor):
    return factor * (
        grad_hat
        - jnp.mean(grad_hat, -1, keepdims=True)
        - normed * jnp.mean(grad_hat * normed, -1, keepdims=True)
    )


def head_mean_matrix(width):
    row = lax.broadcasted_iota(jnp.int32, (width, width), 0) // HD
    col = lax.broadcasted_iota(jnp.int32, (width, width), 1) // HD
    return jnp.where(row == col, 1.0 / HD, 0.0).astype(BF16)


def head_mean(value, matrix):
    high = value.astype(BF16)
    low = (value - high.astype(F32)).astype(BF16)
    return nn(high, matrix) + nn(low, matrix)


def head_stats(value, matrix):
    center = value - head_mean(value, matrix)
    factor = lax.rsqrt(head_mean(center * center, matrix) + EPSILON)
    return center * factor, factor


def head_back(grad_hat, normed, factor, matrix):
    return factor * (
        grad_hat - head_mean(grad_hat, matrix) - normed * head_mean(grad_hat * normed, matrix)
    )


MESH = pl.DeviceIdType.MESH
ALL = slice(None)


class Place:
    def __init__(self, zs):
        f = lax.axis_index("fsdp")
        self.zs = zs
        self.x = lax.axis_index("tensor")
        self.c = lax.rem(f, 2)
        self.y = lax.rem(lax.div(f, 2), 2)
        self.z = lax.div(f, 4)

    def dev(self, z=None, y=None, c=None, x=None):
        z = self.z if z is None else z
        y = self.y if y is None else y
        c = self.c if c is None else c
        x = self.x if x is None else x
        return {"fsdp": (z * 2 + y) * 2 + c, "tensor": x}

    def along_z(self):
        return [lax.rem(self.z + k, self.zs) for k in range(1, self.zs)]

    def peers(self):
        out = [self.dev(z=z) for z in self.along_z()]
        return out + [self.dev(y=1 - self.y), self.dev(c=1 - self.c), self.dev(x=1 - self.x)]


def meet(place):
    barrier = pltpu.get_barrier_semaphore()
    peers = place.peers()
    for peer in peers:
        pl.semaphore_signal(barrier, inc=1, device_id=peer, device_id_type=MESH)
    pl.semaphore_wait(barrier, len(peers))


def remote(src, dst, send, recv, peer):
    return pltpu.make_async_remote_copy(
        src_ref=src, dst_ref=dst, send_sem=send, recv_sem=recv, device_id=peer, device_id_type=MESH
    )


def start(*copies):
    for copy in copies:
        copy.start()


def wait(*copies):
    for copy in copies:
        copy.wait()


class Gather:
    def __init__(self, place, shard, whole, lo, size, order, send, recv, since=0):
        p = self.p = place
        cols = self.cols = pl.ds(lo, size)
        self.shard = None if shard is None else shard.at[:, cols]
        self.whole = whole
        self.order, self.since = order, since
        self.send, self.recv = send, recv
        if shard is not None:
            self.own = pltpu.make_async_copy(self.shard, self.at({}), self.send.at[2 * p.zs + 7])

    def at(self, index):
        p = self.p
        own = {"x": p.x, "y": p.y, "z": p.z}
        x, y, z = (index.get(d, own[d]) for d in "xyz")
        return self.whole.at[x, z, y, p.c, :, self.cols]

    def others(self, d):
        return self.p.along_z() if d == "z" else [1 - getattr(self.p, d)]

    def copies(self, base, i, pairs):
        base += sum(len(self.others(d)) for d in self.order[:i])
        return [remote(src, dst, self.send.at[base + k], self.recv.at[base + k], peer) for k, (src, dst, peer) in enumerate(pairs)]

    def stage(self, i):
        d = self.order[i]
        held = self.at({e: ALL for e in self.order[:i]})
        src = self.shard if i == 0 and self.shard is not None else held
        return self.copies(0, i, [(src, held, self.p.dev(**{d: to})) for to in self.others(d)])

    def core_parts(self, i):
        done = {e: ALL for e in self.order[:i]}
        d = self.order[i]
        if i == 0:
            refs = [self.at({d: ALL})]
        else:
            refs = [self.at({**done, d: to}) for to in self.others(d)]
        peer = self.p.dev(c=1 - self.p.c)
        return self.copies(self.p.zs + 1, i, [(ref, ref, peer) for ref in refs])

    def start(self, i):
        if i == 0 and self.shard is not None:
            self.own.start()
        if i < 3:
            start(*self.stage(i))
        if i > 0:
            start(*self.core_parts(i - 1))

    def done(self, i):
        if i == 0 and self.shard is not None:
            self.own.wait()
        if i < 3:
            wait(*self.stage(i))
        else:
            self.rest(self.since - 1 if self.since else 0, 3)

    def rest(self, lo, hi):
        for i in range(lo, hi):
            wait(*self.core_parts(i))


def gather_sems(zs):
    return 2 * zs + 8


CHUNKS = 4


class Swap:
    def __init__(self, place, src, dst, sems):
        rows = src.shape[0] // CHUNKS
        part = lambda ref, i: ref.at[pl.ds(i * rows, rows)]
        self.copies = [remote(part(src, i), part(dst, i), sems.at[0, i], sems.at[1, i], place.dev(x=1 - place.x)) for i in range(CHUNKS)]

    def start(self, i):
        self.copies[i].start()

    def done(self, i):
        self.copies[i].wait()


def half_rows(ref, which, rows):
    return ref.at[pl.ds(pl.multiple_of(which * rows, rows), rows)]


class Sum:
    def __init__(self, place, total, got, send, recv):
        self.p, self.total, self.got, self.send, self.recv = place, total, got, send, recv

    def copies(self, i):
        p = self.p
        if i < 3:
            peers = [(p.dev(c=1 - p.c), p.dev(x=1 - p.x), p.dev(y=1 - p.y))[i]]
        else:
            peers = [p.dev(z=z) for z in p.along_z()]
        return [remote(self.total, self.got.at[i + k], self.send.at[i + k], self.recv.at[i + k], peer)
                for k, peer in enumerate(peers)]

    def start(self, i):
        start(*self.copies(i))

    def done(self, i):
        copies = self.copies(i)
        wait(*copies)
        total = self.total[...]
        for k in range(len(copies)):
            total = total + self.got[i + k]
        self.total[...] = total


def add_slabs(count, pair):
    def body(i, _):
        into, from_ = pair(i)
        into[...] = into[...] + from_[...]
        return 0
    lax.fori_loop(0, count, body, 0)


class Scatter:
    def __init__(self, place, order, held, away, landings, send, recv, out=None):
        self.p, self.order, self.held, self.away = place, order, held, away
        self.landings, self.send, self.recv, self.out = landings, send, recv, out

    def size(self, d):
        return self.p.zs if d == "z" else 2

    def others(self, d):
        return self.p.along_z() if d == "z" else [1 - getattr(self.p, d)]

    def part(self, i, value, rest=None):
        at = {e: ALL for e in "xzy"}
        at.update(rest or {})
        at.update({e: getattr(self.p, e) for e in self.order[:i]})
        at[self.order[i]] = value
        return self.held(at["x"], at["z"], at["y"])

    def copies(self, i):
        p = self.p
        if i == 0:
            return [remote(self.away, self.landings[0], self.send.at[0], self.recv.at[0], p.dev(c=1 - p.c))]
        d = self.order[i - 1]
        base = 1 + sum(len(self.others(e)) for e in self.order[:i - 1])
        return [remote(self.part(i - 1, to), self.landings[i].at[k], self.send.at[base + k], self.recv.at[base + k], p.dev(**{d: to}))
                for k, to in enumerate(self.others(d))]

    def start(self, i):
        start(*self.copies(i))

    def done(self, i):
        p = self.p
        wait(*self.copies(i))
        if i == 3:
            value = self.part(2, getattr(p, self.order[2]))[...].astype(F32)
            for k in range(len(self.others(self.order[2]))):
                value = value + self.landings[3][k].astype(F32)
            for ref, lo, size in self.out:
                ref[...] = value[:, lo:lo + size]
            return
        dims = [e for e in "xzy" if e not in self.order[:i]]
        walked = [e for e in dims if e != "z"]

        def body(j, _):
            at, left = {"z": ALL}, j
            for e in reversed(walked):
                at[e] = lax.rem(left, 2)
                left = lax.div(left, 2)
            index = tuple(at[e] for e in dims)
            if i == 0:
                into, froms = self.held(at["x"], at["z"], at["y"]), [self.landings[0].at[index]]
            else:
                d = self.order[i - 1]
                into = self.part(i - 1, getattr(p, d), {e: at[e] for e in dims})
                froms = [self.landings[i].at[(k,) + index] for k in range(len(self.others(d)))]
            value = into[...]
            if len(froms) == 1:
                value = value + froms[0][...]
            else:
                value = value.astype(F32)
                for from_ in froms:
                    value = value + from_[...].astype(F32)
                value = value.astype(BF16)
            into[...] = value
            return 0
        lax.fori_loop(0, 2 ** len(walked), body, 0)

    def state(self, stages):
        return self.part(stages - 2, getattr(self.p, self.order[stages - 2]))


def scatter_sems(zs):
    return zs + 2


def rest_shape(zs, rows, m, gone):
    size = {"x": 2, "z": zs, "y": 2}
    return tuple(size[e] for e in "xzy" if e not in gone) + (rows, m)


def landing(zs, rows, m, order, since=0):
    shapes = [rest_shape(zs, rows, m, "")]
    for i, d in enumerate(order):
        shapes.append((zs - 1 if d == "z" else 1,) + rest_shape(zs, rows, m, order[:i + 1]))
    return [pltpu.VMEM(shape, BF16) for shape in shapes[since:]]


def follow(chains, plan):
    for name, i in plan:
        if i < 0:
            chains[name].start(-1 - i)
        else:
            chains[name].done(i)


def at_steps(step, chains, plans):
    for at, plan in enumerate(plans):
        if plan:
            pl.when(step == at)(functools.partial(follow, chains, plan))


def on(step, hooks):
    for at, hook in hooks.items():
        pl.when(step == at)(hook)


HBM = pl.BlockSpec(memory_space=pl.ANY)
WHOLE_VMEM = pl.BlockSpec(memory_space=pltpu.VMEM)
DMA = pltpu.SemaphoreType.DMA


def params(collective_id):
    return pltpu.CompilerParams(collective_id=collective_id, has_side_effects=True, vmem_limit_bytes=LIMIT)


Q_ORDERS = ('zxy', 'zxy', 'xzy', 'zyx', 'xyz', 'xzy', 'zxy')
O_ORDER = 'zxy'
U_ORDERS = ('zxy', 'xzy', 'yzx', 'yzx')
D_ORDERS = ('yzx', 'yxz', 'zxy', 'xyz')
FEED_SINCE = (3, 1, 0)
FEED_ORDERS = ('xzy', 'yzx', 'yxz', 'xyz')
FEED_DONE = (3, 3)
LATE_ORDERS = ('yxz', 'yzx', 'xzy', 'zxy')
O_BACK_ORDER = 'yxz'
CLOSING = ((0, 0, 256, 'zyx'), (0, 256, 256, 'yxz'), (0, 512, 256, 'xyz'), (1, 0, 256, 'yxz'), (1, 256, 256, 'zyx'), (1, 512, 256, 'yxz'))
ATTENTION_LEAVES = (('U1', 3), ('D1', 3), ('U2', 1), ('D2', 1), ('U3', 0), ('D3', 0))
OPENING_PLANS = (
    ((6, -1), ('T', -1), (0, -1), (2, -1), ('D0', -1), ('D1', -1), (2, 0), (4, -1), (6, 0), (1, -1), ('D0', 0), ('U2', -1), ('D1', 0), (0, 0), (2, -2), (4, 0), (6, -2), (4, -2), ('U2', 0), ('T', 0), ('T', -2), (6, 1), (6, -3), (0, -2), (4, 1), (1, 0), (3, -1), (6, 2), (6, -4), (2, 1), (2, -3), (4, -3), (6, 3), (3, 0), (3, -2), ('O', -1), (0, 1), (1, -2),),
    (('T', 1), ('T', -3), (1, 1), (5, -1), (3, 1), (0, -3), (5, 0), (3, -3), (2, 2), (1, -3), (2, -4), ('T', 2), ('T', -4), (2, 3), ('O', 0), (5, -2), (0, 2), (0, -4), (3, 2), (3, -4), ('O', -2), (4, 2), (4, -4), ('U0', -1), (1, 2), (1, -4), (0, 3), (3, 3), ('T', 3), ('U1', -1),),
)
ATTENTION_PLANS = (
    ((5, 1), (5, -3), ('D0', -2), (1, 3), (4, 3),),
    (),
    (),
    (('U1', 0), ('C', -1),),
    (('O', 1), ('O', -3), ('D1', -2),),
    (('U0', 0), ('U1', -2), (5, 2), (5, -4),),
    (),
    ((5, 3), ('D1', 1), ('U0', -2),),
    (('C', 0), ('C', -2),),
    (),
    (('O', 2), ('O', -4), ('D0', 1), ('D1', -3),),
    (),
    (('U0', 1), ('U0', -3), ('D0', -3), ('O', 3),),
    (('C', 1), ('C', -3),),
    (('U1', 1), ('U1', -3), ('D2', -1),),
    (),
    (),
    (),
    (),
    (('C', 2), ('C', -4),),
    (('D2', 0), ('D0', 2), ('D0', -4), ('U0', 2), ('U0', -4),),
    (),
    (),
    (('U1', 2), ('C', 3), ('D0', 3), ('U0', 3),),
)
ATTENTION_END = (('D1', 2),)
FEED_PLANS = (
    (('U1', -4), ('D1', -4), ('U2', -2), ('D2', -2), ('U3', -1), ('D3', -1),),
    (('U3', 0), ('U3', -2), ('U1', 3), ('D3', 0), ('D3', -2), ('D1', 3), ('D2', 1), ('D2', -3),),
    (),
    (('U2', 1), ('U2', -3), ('D3', 1), ('D3', -3),),
    (('u0', -1), ('d0', -1),),
    (('D2', 2), ('D2', -4),),
    (('U3', 1), ('U3', -3),),
    (('u0', 0), ('u0', -2), ('d0', 0), ('d0', -2), ('U2', 2), ('U2', -4), ('D2', 3),),
    (('u1', -1), ('d1', -1), ('U2', 3),),
    (),
    (('D3', 2), ('D3', -4), ('u1', 0), ('u1', -2), ('d1', 0), ('d1', -2), ('U3', 2), ('U3', -4), ('d0', 1), ('d0', -3),),
    (('D3', 3), ('U3', 3),),
    (('u0', 1), ('u0', -3),),
    (('u1', 1), ('u1', -3),),
    (('d0', 2), ('d1', 1), ('d1', -3),),
    (('u1', 2),),
)
FEED_END = (('u0', 2), ('d1', 2),)
BACKWARD_PLANS = (
    (('u0', -4), ('d0', -4), ('u1', -4), ('d1', -4), ('u2', -1), ('d2', -1), ('u3', -1), ('d3', -1), ('R', -1),),
    (('u0', 3), ('d0', 3),),
    (),
    (('R', 0), ('R', -2),),
    (('u1', 3), ('d1', 3), ('u2', 0), ('o', -1), ('u2', -2), ('d2', 0), ('d2', -2), ('u3', 0), ('u3', -2), ('d3', 0), ('d3', -2),),
    (('R', 1), ('R', -3), ('o', 0), ('o', -2),),
    (),
    (),
    (),
    (('R', 2), ('R', -4),),
    (('u3', 1), ('u3', -3),),
    (),
    (('R', 3), ('d3', 1), ('d3', -3),),
    (('u2', 1), ('u2', -3), ('d2', 1), ('d2', -3),),
    (('d3', 2), ('d3', -4), ('o', 1), ('o', -3), ('u3', 2), ('u3', -4),),
    (('d3', 3),),
    (('u2', 2), ('u2', -4), ('u3', 3),),
    (('o', 2), ('o', -4), ('d2', 2), ('d2', -4),),
    (('d2', 3),),
    (('u2', 3),),
)
BACKWARD_END = (('o', 3),)
CLOSING_PLANS = (
    ((0, -1), (1, -1), (2, -1),),
    (),
    (('G', -1),),
    ((3, -1), (0, 0), (0, -2), (4, -1), (1, 0), (1, -2), (5, -1), (2, 0), (2, -2),),
    (('G', 0), ('G', -2),),
)
CLOSING_END = (('S', -1), (3, 0), (3, -2), (4, 0), (4, -2), (5, 0), (1, 1), (5, -2), ('S', 0), (2, 1), ('S', -2), ('S', 1), (1, -3), ('G', 1), ('G', -3), (0, 1), (3, 1), ('S', -3), (5, 1), (0, -3), (1, 2), (1, -4), (3, -3), ('S', 2), ('S', -4), (2, -3), (0, 2), (4, 1), (4, -3), ('G', 2), (0, -4), (3, 2), (3, -4), (5, -3), (2, 2), (1, 3), (2, -4), (0, 3), ('G', -4), (4, 2), ('S', 3), (5, 2), (4, -4), (5, -4), (3, 3), (2, 3), (4, 3), (5, 3), ('G', 3),)


Q_TILE = 256
ATTEND_TILE = 512
ROWS = 256
FF_GROUP = 512


def full(shape):
    return pl.BlockSpec(shape, lambda s: (0,) * len(shape), pipeline_mode=pl.Buffered(1))


def clipped(shape, axis, first, count):
    def at(s):
        i = jnp.clip(s - first, 0, count - 1)
        return (i, 0) if axis == 0 else (0, i)
    return pl.BlockSpec(shape, at)


def tile_of(part, s):
    i = jnp.clip(s - 4 * part, 0, 3)
    column = lax.div(i, 2)
    return lax.rem(i, 2) * 2 + (1 - column if part == 0 else column)


def project_step(step, joined, gains, kept, blocks):
    tile = joined.shape[1]
    qn_s, kn_s, v_s = kept
    qn, kn, v, q_raw, k_raw = blocks
    matrix = head_mean_matrix(tile)

    def cols(part):
        return pl.ds(pl.multiple_of(tile_of(part, step) * tile, tile), tile)

    @pl.when(step < 4)
    def _():
        value = joined.astype(BF16)
        v[...] = value
        v_s[:, cols(0)] = value

    @pl.when((step >= 4) & (step < 8))
    def _():
        hat, _f = head_stats(joined, matrix)
        value = (hat * gains[1:2]).astype(BF16)
        kn[...] = value
        kn_s[:, cols(1)] = value
        k_raw[...] = joined.astype(BF16)

    @pl.when(step >= 8)
    def _():
        hat, _f = head_stats(joined, matrix)
        value = (hat * gains[0:1] * (HD ** -0.5)).astype(BF16)
        qn[...] = value
        qn_s[:, cols(2)] = value
        q_raw[...] = joined.astype(BF16)


def attend_step(query_all, keys, values, mixed_s, cols, mixed, inverse):
    length = keys.shape[0]
    lane = lax.broadcasted_iota(jnp.int32, (1, PAIR), 1) < HD
    zero = jnp.zeros((), BF16)
    values_t = values.astype(F32).T.astype(BF16)
    ones = jnp.ones((16, length), BF16)
    heads = [(jnp.where(mask, keys, zero), jnp.concatenate([values_t[h * HD:(h + 1) * HD], ones], axis=0))
             for h, mask in ((0, lane), (1, ~lane))]
    for i in range(length // ATTEND_TILE):
        at = slice(i * ATTEND_TILE, (i + 1) * ATTEND_TILE)
        query = query_all[at]
        got, inv = [], []
        for keys_h, values_h in heads:
            both = nn(values_h, jnp.exp(nt(keys_h, query)).astype(BF16))
            one_over = 1.0 / both[HD:HD + 1]
            got.append(both[:HD] * one_over)
            inv.append(jnp.broadcast_to(one_over, (HD, ATTEND_TILE)))
        value = jnp.concatenate(got, axis=0).T.astype(BF16)
        mixed[at] = value
        mixed_s[at, cols] = value
        inverse[at] = jnp.concatenate(inv, axis=0).T


PROJECT_STEPS = 12


def first_after(plans, name):
    return max([at for at, plan in enumerate(plans) if (name, 3) in plan], default=0)


def attention_body(
    zs, pairs, qk_gains, norm_gains, norm_shifts, q_in, o_in, u_in, d_in, tokens, cot_in,
    first, qn, kn, v, q_raw, k_raw, mixed, inverse, middle, second, norms, image, cot, whole_q, whole_o, whole_u, whole_d,
    image_v, qn_s, kn_s, v_s, mixed_s, out_w, tiles, q_v, o_v, u_v, d_v, cot_v, side_v, turn, local_sem, send, recv, swap_sem,
):
    step = pl.program_id(0)
    p = Place(zs)
    length = image_v.shape[0]
    half, rows = whole_o.shape[5], whole_o.shape[4]
    tile = half // 2
    head0, row0 = PROJECT_STEPS, PROJECT_STEPS + pairs
    n = FF_GROUP
    mine = pl.ds(pl.multiple_of(p.x * (length // 2), length // 2), length // 2)
    chains = {
        "T": Swap(p, tokens.at[1 - p.x], half_rows(image_v, p.x, length // 2), swap_sem.at[0]),
        "C": Swap(p, cot_in.at[1 - p.x], half_rows(cot, p.x, length // 2), swap_sem.at[1]),
    }
    local = lambda i, src, dst: pltpu.make_async_copy(src, dst, local_sem.at[i])
    own_shards = [local(i, a, b) for i, (a, b) in enumerate(((o_in, o_v), (u_in, u_v), (d_in, d_v)))]
    own_shards += [local(i, q_in.at[k], q_v.at[:, pl.ds(k * half, half)]) for i, k in ((3, 0), (12, 1), (13, 2))]
    own_tokens = local(4, tokens.at[p.x], image_v.at[mine])
    own_cot = [local(5, cot_in.at[p.x], cot_v), local(6, cot_v, cot.at[mine])]
    keep_image = local(7, image_v, image)
    side = local(8, whole_q.at[0, :, :, :, :, pl.ds(3 * half, PAIR)], side_v)
    load_out = local(9, whole_o, out_w)
    starts = (2 * half + tile, 2 * half, half, half + tile, 0, tile)
    for i, lo in enumerate(starts):
        chains[i] = Gather(p, q_v, whole_q, lo, tile, Q_ORDERS[i], send.at[i], recv.at[i])
    chains[6] = Gather(p, q_v, whole_q, 3 * half, PAIR, Q_ORDERS[6], send.at[15], recv.at[15])

    def load_tile(i):
        return local(10 + i % 2, whole_q.at[:, :, :, :, :, pl.ds(starts[i], tile)], tiles.at[i % 2])

    chains["O"] = Gather(p, o_v, whole_o, 0, half, O_ORDER, send.at[6], recv.at[6])
    for j in range(4):
        chains[f"U{j}"] = Gather(p, u_v, whole_u, j * n, n, U_ORDERS[j], send.at[7 + j], recv.at[7 + j])
        chains[f"D{j}"] = Gather(p, d_v, whole_d, j * n, n, D_ORDERS[j], send.at[11 + j], recv.at[11 + j])

    @pl.when(step == 0)
    def _():
        start(*own_shards, own_tokens, own_cot[0])
        turn[...] = jnp.zeros_like(turn)
        turn[0:2, 0:rows] = norm_gains[...].astype(F32)
        turn[2:4, 0:rows] = norm_shifts[...].astype(F32)
        q_v[:, 3 * half:] = turn[...].T[:rows].astype(BF16)
        meet(p)
        wait(*own_shards)
        for name, stages in ATTENTION_LEAVES:
            if stages == 0:
                chains[name].own.start()

        def norm(which):
            def rows_norm(i, _):
                at = pl.ds(pl.multiple_of(which * (length // 2) + i * ROWS, ROWS), ROWS)
                hat, _f = stats(image_v[at].astype(F32))
                first[at] = (hat * norms[0:1] + norms[2:3]).astype(BF16)
                return 0
            lax.fori_loop(0, length // 2 // ROWS, rows_norm, 0)

        follow(chains, OPENING_PLANS[0])
        side.start()
        own_cot[0].wait()
        own_cot[1].start()
        side.wait()
        norms[...] = side_v[...].reshape(-1, PAIR).astype(F32).T[:8]
        own_tokens.wait()
        norm(p.x)
        follow(chains, OPENING_PLANS[1])
        load_tile(0).start()
        keep_image.start()
        norm(1 - p.x)

    at_steps(step, chains, ATTENTION_PLANS)

    on(step, {0: lambda: load_tile(0).wait()})
    for i in range(1, 6):
        on(step, {max(2 * i - 2, first_after(ATTENTION_PLANS, i)): lambda i=i: load_tile(i).start()})
        on(step, {2 * i: lambda i=i: load_tile(i).wait()})
    on(step, {max(1, first_after(ATTENTION_PLANS, "O")): lambda: load_out.start()})
    on(step, {row0: lambda: load_out.wait()})

    @pl.when(step < head0)
    def _():
        gains = qk_gains[...].astype(F32)
        gains = jnp.concatenate([gains] * (tile // HD), axis=1)
        w = tiles[lax.rem(lax.div(step, 2), 2), lax.rem(step, 2)].reshape(-1, tile)
        project_step(step, nn(first[...], w), gains, (qn_s, kn_s, v_s), (qn, kn, v, q_raw, k_raw))

    @pl.when((step >= head0) & (step < row0))
    def _():
        cols = pl.ds(pl.multiple_of((step - head0) * PAIR, PAIR), PAIR)
        attend_step(qn_s[:, cols], kn_s[:, cols], v_s[:, cols], mixed_s, cols, mixed, inverse)

    @pl.when(step >= row0)
    def _():
        at = pl.ds(pl.multiple_of((step - row0) * ROWS, ROWS), ROWS)
        w0, w1 = (out_w[t].reshape(-1, half) for t in range(2))
        value = image_v[at].astype(F32) + nt(mixed_s[at, :half], w0) + nt(mixed_s[at, half:], w1)
        middle[...] = value
        hat, _f = stats(value)
        second[...] = (hat * norms[1:2] + norms[3:4]).astype(BF16)

    @pl.when(step == pl.num_programs(0) - 1)
    def _():
        follow(chains, ATTENTION_END)
        for name, stages in ATTENTION_LEAVES:
            chains[name].rest(0, stages - 1)
            if stages == 0:
                chains[name].own.wait()
        wait(own_cot[1], keep_image)


def attention(qk_gains, norm_gains, norm_shifts, q, o, u, d, tokens, cot, zs):
    rows = o.shape[0]
    length, width = 2 * tokens.shape[1], tokens.shape[2]
    half = o.shape[1]
    pairs = 2 * half // PAIR
    head0, row0 = PROJECT_STEPS, PROJECT_STEPS + pairs
    tile = half // 2
    tiles = lambda part: pl.BlockSpec((length, tile), lambda s: (0, tile_of(part, s)))
    heads = clipped((length, PAIR), 1, head0, pairs)
    by_rows = clipped((ROWS, width), 0, row0, length // ROWS)
    bf = jax.ShapeDtypeStruct((length, 2 * half), BF16)
    square = jax.ShapeDtypeStruct((length, width), BF16)
    f32 = lambda *shape: jax.ShapeDtypeStruct(shape, F32)
    whole = lambda n: jax.ShapeDtypeStruct((2, zs, 2, 2, rows, n), BF16)
    store = pltpu.VMEM((length, 2 * half), BF16)
    wide = lambda n: pltpu.VMEM((rows, n), BF16)
    return pl.pallas_call(
        functools.partial(attention_body, zs, pairs),
        grid=(row0 + length // ROWS,),
        in_specs=[full(qk_gains.shape), full(norm_gains.shape), full(norm_shifts.shape)] + [HBM] * 6,
        out_specs=[full((length, width)), tiles(2), tiles(1), tiles(0), tiles(2), tiles(1), heads, heads, by_rows, by_rows,
                   full((8, width))] + [HBM] * 6,
        out_shape=[square, bf, bf, bf, bf, bf, bf, f32(length, 2 * half), f32(length, width), square, f32(8, width),
                   square, square, whole(3 * half + PAIR), whole(half), whole(u.shape[1]), whole(d.shape[1])],
        scratch_shapes=[pltpu.VMEM((length, width), BF16), store, store, store, store, pltpu.VMEM((2, zs, 2, 2, rows, half), BF16),
                        pltpu.VMEM((2, 2, zs, 2, 2, rows, tile), BF16), wide(3 * half + PAIR), wide(half), wide(u.shape[1]), wide(d.shape[1]),
                        pltpu.VMEM((length // 2, width), BF16), pltpu.VMEM((zs, 2, 2, rows, PAIR), BF16),
                        pltpu.VMEM((PAIR, PAIR), F32), DMA((14,)), DMA((16, gather_sems(zs))), DMA((16, gather_sems(zs))), DMA((2, 2, CHUNKS))],
        compiler_params=params(0),
        name="attention",
    )(qk_gains, norm_gains, norm_shifts, q, o, u, d, tokens, cot)


def gelu_parts(v):
    bell = jnp.exp(v * v * -0.5)
    t = 1.0 / (1.0 + (0.3275911 * 0.7071067811865476) * jnp.abs(v))
    poly = t * (0.127414796 + t * (-0.142248368 + t * (0.7107068705 + t * (-0.7265760135 + t * 0.5307027145))))
    tail = poly * bell
    return jnp.where(v >= 0, 1.0 - tail, tail), bell * 0.3989422804014327


def feed_body(
    zs, second, cot, middle, _u, _d,
    result, grad_second, grad_u, grad_d, state_0, state_1, state_2, state_3, outputs, whole_u, whole_d,
    acc, second_t, cot_t, active, grad_hidden, tiles, g, tile_sem, misc_sem, send, recv, *landings,
):
    step = pl.program_id(0)
    p = Place(zs)
    length = second.shape[0]
    n = FF_GROUP
    state_refs = (state_0, state_1, state_2, state_3)
    chains = {}
    for j in (1, 2, 3):
        for i, (name, w, orders) in enumerate((("U", whole_u, U_ORDERS), ("D", whole_d, D_ORDERS))):
            k = 2 * j - 2 + i
            chains[f"{name}{j}"] = Gather(p, None, w, j * n, n, orders[j], send.at[k], recv.at[k], FEED_SINCE[j - 1])
    at, states = iter(landings), []
    for j in range(2):
        for k in range(2):
            i = 2 * j + k
            held = lambda x, z, y, j=j, k=k: g.at[k, j, x, z, y, p.c]
            s = Scatter(p, FEED_ORDERS[i], held, g.at[k, j, :, :, :, 1 - p.c], [next(at) for _ in range(FEED_DONE[j])], send.at[6 + i], recv.at[6 + i])
            chains[f"{'ud'[k]}{j}"] = s
            states.append(pltpu.make_async_copy(s.state(FEED_DONE[j]), state_refs[i], misc_sem.at[1 + i]))
    init = pltpu.make_async_copy(middle, acc, misc_sem.at[0])
    mine = pl.ds(pl.multiple_of(p.x * (length // 2), length // 2), length // 2)
    own = pltpu.make_async_copy(result.at[mine], outputs.at[p.x], misc_sem.at[9])
    outs = [pltpu.make_async_copy(g.at[k, j], (grad_u, grad_d)[k].at[j - 2], misc_sem.at[5 + 2 * (j - 2) + k])
            for j in (2, 3) for k in range(2)]

    def loads(s):
        j, t = (s // 2, s % 2) if isinstance(s, int) else (lax.div(s, 2), lax.rem(s, 2))
        slot = t
        cols = pl.ds(j * n if isinstance(s, int) else pl.multiple_of(j * n, n), n)
        return [pltpu.make_async_copy(w.at[t, :, :, :, :, cols], tiles.at[k, slot], tile_sem.at[k, slot])
                for k, w in ((0, whole_u), (1, whole_d))]

    @pl.when(step == 0)
    def _():
        meet(p)
        start(*loads(0))
        start(*loads(1))
        init.start()
        follow(chains, FEED_PLANS[0])
        second_t[...] = second[...].T
        cot_t[...] = cot[...].T
        grad_second[...] = jnp.zeros_like(grad_second)

    at_steps(step, chains, ((),) + FEED_PLANS[2::2])
    for s in range(2, 8):
        here = first_after(FEED_PLANS, f"U{s // 2}"), first_after(FEED_PLANS, f"D{s // 2}")
        on(step, {max(s - 1, (max(here) + 1) // 2): lambda s=s: start(*loads(s))})
    on(step, {7: lambda: start(*outs[:2])})
    wait(*loads(step))

    @pl.when(step == 0)
    def _():
        init.wait()
    slot = lax.rem(step, 2)
    w_up = tiles[0, slot].reshape(-1, n)
    w_down = tiles[1, slot].reshape(-1, n)
    for i in range(length // ROWS):
        at = slice(i * ROWS, (i + 1) * ROWS)
        hidden = nn(second[at], w_up)
        grad_active = nn(cot[at], w_down)
        cumulative, density = gelu_parts(hidden)
        a = (hidden * cumulative).astype(BF16)
        b = (grad_active * (cumulative + hidden * density)).astype(BF16)
        active[at] = a
        grad_hidden[at] = b
        acc[at] += nt(a, w_down)
        grad_second[at] += nt(b, w_up)
    at_steps(step, chains, FEED_PLANS[1::2])
    j, t = lax.div(step, 2), lax.rem(step, 2)
    shape = g.shape[3:]
    g[0, j, t] = nn(second_t[...], grad_hidden[...]).astype(BF16).reshape(shape)
    g[1, j, t] = nn(cot_t[...], active[...]).astype(BF16).reshape(shape)

    @pl.when(step == pl.num_programs(0) - 1)
    def _():
        start(*outs[2:])
        result[...] = acc[...].astype(BF16)
        own.start()
        follow(chains, FEED_END)
        start(*states)
        wait(*states)
        wait(*outs)
        own.wait()


def feed(second, cot, middle, whole_u, whole_d, zs):
    length, width = second.shape
    rows, n = whole_u.shape[4], FF_GROUP
    same = lambda a: jax.ShapeDtypeStruct(a.shape, a.dtype)
    tile = (2, zs, 2, 2, rows, n)
    grads = jax.ShapeDtypeStruct((2,) + tile, BF16)
    square = pltpu.VMEM((length, width), BF16)
    strip = pltpu.VMEM((length, n), BF16)
    scratch = [pltpu.VMEM((length, width), F32), square, square, strip, strip, pltpu.VMEM((2, 2) + tile[1:], BF16),
               pltpu.VMEM((2, 4) + tile, BF16), DMA((2, 2)), DMA((10,)), DMA((10, gather_sems(zs))), DMA((10, gather_sems(zs)))]
    for i in range(4):
        scratch += landing(zs, rows, n, FEED_ORDERS[i])[:FEED_DONE[i // 2]]
    return pl.pallas_call(
        functools.partial(feed_body, zs),
        grid=(8,),
        in_specs=[full(second.shape), full(cot.shape), HBM, HBM, HBM],
        out_specs=[full(second.shape), full(second.shape)] + [HBM] * 9,
        out_shape=[same(second), jax.ShapeDtypeStruct((length, width), F32), grads, grads]
        + [jax.ShapeDtypeStruct(rest_shape(zs, rows, n, o[:FEED_DONE[i // 2] - 1]), BF16) for i, o in enumerate(FEED_ORDERS)]
        + [jax.ShapeDtypeStruct((2, length // 2, width), BF16), same(whole_u), same(whole_d)],
        scratch_shapes=scratch,
        input_output_aliases={3: 9, 4: 10},
        compiler_params=params(1),
        name="feed",
    )(second, cot, middle, whole_u, whole_d)


def attend_back_step(between, gains, go, inv, query, keys, values, q_raw, k_raw, mixed, grad_q, grad_k, grad_v, grad_gains):
    length = query.shape[0]
    lanes = lax.broadcasted_iota(jnp.int32, (1, PAIR), 1)
    first = lanes < HD
    zero = jnp.zeros((), BF16)
    go = go.astype(F32)
    product = go * mixed.astype(F32) * inv
    go_inv = go * inv
    go_t = go_inv.T.astype(BF16)
    go_inv = go_inv.astype(BF16)
    query_t = query.astype(F32).T.astype(BF16)
    heads = []
    for h, mask in ((0, first), (1, ~first)):
        delta = -jnp.sum(jnp.where(mask, product, 0.0), -1, keepdims=True)
        high = delta.astype(BF16)
        low = (delta - high.astype(F32)).astype(BF16)
        spare = (1 - h) * HD
        grad_aug = jnp.where(mask, go_inv, jnp.where(lanes == spare, high, jnp.where(lanes == spare + 1, low, zero)))
        values_aug = jnp.where(mask, values, jnp.where((lanes == spare) | (lanes == spare + 1), jnp.ones((), BF16), zero))
        mine = slice(h * HD, (h + 1) * HD)
        heads.append((jnp.where(mask, keys, zero), grad_aug, values_aug, go_t[mine], query_t[mine]))
    dq = []
    dk = [jnp.zeros((HD, length), F32)] * 2
    dv = [jnp.zeros((HD, length), F32)] * 2
    for i in range(length // Q_TILE):
        if 2 * i == length // Q_TILE:
            between()
        at = slice(i * Q_TILE, (i + 1) * Q_TILE)
        parts = []
        for h, (km, ga, va, gt, qt) in enumerate(heads):
            exponent = jnp.exp(nt(query[at], km))
            grad_scores = (exponent * nt(ga[at], va)).astype(BF16)
            dv[h] = dv[h] + nn(gt[:, at], exponent.astype(BF16))
            dk[h] = dk[h] + nn(qt[:, at], grad_scores)
            parts.append(nn(grad_scores, km))
        dq.append(parts[0] + parts[1])
    dq = jnp.concatenate(dq, axis=0)
    dk = jnp.concatenate(dk, axis=0).T
    dv = jnp.concatenate(dv, axis=0).T
    grad_v[...] = dv.astype(BF16)
    matrix = head_mean_matrix(PAIR)
    hat, factor = head_stats(q_raw.astype(F32), matrix)
    scale = HD ** -0.5
    sum_q = jnp.sum(dq * hat, 0, keepdims=True) * scale
    grad_q[...] = head_back(dq * gains[0:1] * scale, hat, factor, matrix).astype(BF16)
    hat, factor = head_stats(k_raw.astype(F32), matrix)
    sum_k = jnp.sum(dk * hat, 0, keepdims=True)
    grad_k[...] = head_back(dk * gains[1:2], hat, factor, matrix).astype(BF16)
    grad_gains[...] += jnp.concatenate([sum_q, sum_k], axis=0)


def backward_body(
    zs, rows_steps, norms, gains, cot, grad_second, middle, mixed_rows, w, qn, kn, v, q_raw, k_raw, mixed, inverse,
    grads_u, grads_d, state_0, state_1, state_2, state_3, result, _outputs,
    grad_middle, grad_q, grad_k, grad_v, grad_gains, sums, shard_u, shard_d, shard_o, outputs,
    grad_mixed, acc, g_o, own_late, load_sem, swap_sem, send, recv, *landings,
):
    step = pl.program_id(0)
    p = Place(zs)
    n = FF_GROUP
    half = w.shape[2]
    at = iter(landings)
    take = lambda count: [next(at) for _ in range(count)]
    chains, loads = {}, []

    def out(k, j):
        return [((shard_u, shard_d)[k].at[:, pl.ds(j * n, n)], 0, n)]

    for i, state in enumerate((state_0, state_1, state_2, state_3)):
        j, k = divmod(i, 2)
        order = FEED_ORDERS[i]
        own = next(at)

        def held(x, z, y, own=own, gone=order[:FEED_DONE[j] - 1]):
            return own.at[tuple(index for e, index in zip("xzy", (x, z, y)) if e not in gone)]
        skip = FEED_DONE[j]
        chains[f"{'ud'[k]}{j}"] = Scatter(p, order, held, None, [None] * skip + take(4 - skip), send.at[i], recv.at[i], out(k, j))
        loads.append(pltpu.make_async_copy(state, own, load_sem.at[i]))
    for i in range(4):
        j, k = divmod(i, 2)
        grad = (grads_u, grads_d)[k].at[j]
        chains[f"{'ud'[k]}{2 + j}"] = Scatter(
            p, LATE_ORDERS[i], lambda x, z, y, i=i: own_late.at[i, x, z, y], grad.at[:, :, :, 1 - p.c], take(4),
            send.at[4 + i], recv.at[4 + i], out(k, 2 + j))
        loads.append(pltpu.make_async_copy(grad.at[:, :, :, p.c], own_late.at[i], load_sem.at[4 + i]))
    chains["o"] = Scatter(p, O_BACK_ORDER, lambda x, z, y: g_o.at[x, z, y, p.c], g_o.at[:, :, :, 1 - p.c], take(4),
                          send.at[8], recv.at[8], [(shard_o, 0, half)])
    half_length = result.shape[0] // 2
    chains["R"] = Swap(p, half_rows(result, 1 - p.x, half_length), outputs.at[p.x], swap_sem)

    @pl.when(step == 0)
    def _():
        start(*loads)
        meet(p)
        wait(*loads)
        follow(chains, BACKWARD_PLANS[0])

    at_steps(step, chains, ((),) + BACKWARD_PLANS[1:rows_steps] + BACKWARD_PLANS[rows_steps::2])

    def between():
        at_steps(step, chains, ((),) * rows_steps + BACKWARD_PLANS[rows_steps + 1::2])

    @pl.when(step == 0)
    def _():
        sums[...] = jnp.zeros_like(sums)
        acc[...] = jnp.zeros_like(acc)
        grad_gains[...] = jnp.zeros_like(grad_gains)

    @pl.when(step < rows_steps)
    def _():
        hat, factor = stats(middle[...])
        gs = grad_second[...]
        gm = cot[...].astype(F32) + back(gs * norms[1:2], hat, factor)
        grad_middle[...] = gm
        branch_grad = gm.astype(BF16)
        branch_t = branch_grad.T
        here = pl.ds(pl.multiple_of(step * ROWS, ROWS), ROWS)
        for t in range(2):
            cols = slice(t * half, (t + 1) * half)
            grad_mixed[here, cols] = nn(branch_grad, w[t]).astype(BF16)
            acc[t] += nn(branch_t, mixed_rows[:, cols])
        sums[0:1] += jnp.sum(gs * hat, 0, keepdims=True)
        sums[1:2] += jnp.sum(gs, 0, keepdims=True)

    @pl.when(step == rows_steps - 1)
    def _():
        g_o[...] = acc[...].astype(BF16).reshape(g_o.shape)

    @pl.when(step >= rows_steps)
    def _():
        cols = pl.ds(pl.multiple_of((step - rows_steps) * PAIR, PAIR), PAIR)
        attend_back_step(between, gains, grad_mixed[:, cols], inverse[...], qn[...], kn[...], v[...], q_raw[...], k_raw[...], mixed[...],
                         grad_q, grad_k, grad_v, grad_gains)

    @pl.when(step == pl.num_programs(0) - 1)
    def _():
        follow(chains, BACKWARD_END)


def backward(norms, gains, cot, grad_second, middle, mixed, w, kept, inverse, grads_u, grads_d, states, result, outputs, zs):
    length, width = middle.shape
    half = w.shape[2]
    rows, n = grads_u.shape[5], FF_GROUP
    row_steps, pairs = length // ROWS, 2 * half // PAIR
    row = clipped((ROWS, width), 0, 0, row_steps)
    head = clipped((length, PAIR), 1, row_steps, pairs)
    heads = jax.ShapeDtypeStruct((length, 2 * half), BF16)
    f32 = lambda *shape: jax.ShapeDtypeStruct(shape, F32)
    scratch = [
        pltpu.VMEM((length, 2 * half), BF16), pltpu.VMEM(w.shape, F32), pltpu.VMEM((2, zs, 2, 2, rows, half), BF16),
        pltpu.VMEM((4, 2, zs, 2, rows, n), BF16), DMA((8,)), DMA((2, CHUNKS)),
        DMA((9, scatter_sems(zs))), DMA((9, scatter_sems(zs))),
    ]
    for i in range(4):
        skip = FEED_DONE[i // 2]
        scratch += [pltpu.VMEM(rest_shape(zs, rows, n, FEED_ORDERS[i][:skip - 1]), BF16)] + landing(zs, rows, n, FEED_ORDERS[i], skip)
    for i in range(4):
        scratch += landing(zs, rows, n, LATE_ORDERS[i])
    scratch += landing(zs, rows, half, O_BACK_ORDER)
    return pl.pallas_call(
        functools.partial(backward_body, zs, row_steps),
        grid=(row_steps + pairs,),
        in_specs=[full(norms.shape), full(gains.shape), row, row, row, row, full(w.shape)] + [head] * 7 + [HBM] * 8,
        out_specs=[row, head, head, head, full((2, PAIR)), full((2, width)), full((rows, 4 * n)), full((rows, 4 * n)),
                   full((rows, half)), HBM],
        out_shape=[f32(length, width), heads, heads, heads, f32(2, PAIR), f32(2, width), f32(rows, 4 * n), f32(rows, 4 * n),
                   f32(rows, half), jax.ShapeDtypeStruct((2, length // 2, width), BF16)],
        scratch_shapes=scratch,
        input_output_aliases={21: 9},
        compiler_params=params(2),
        name="backward",
    )(norms, gains, cot, grad_second, middle, mixed, w, *kept, mixed, inverse, grads_u, grads_d, *states, result, outputs)


PART_GROUP = 256


def pieces(lo, size):
    out = []
    for part in range(3):
        first, last = max(lo, part * PART_GROUP), min(lo + size, (part + 1) * PART_GROUP)
        if first < last:
            out.append((part, first - lo, last - first))
    return out


def closing_body(
    zs, norms, sums_second, sums_qk, image_in, first_in, grad_middle_in, gq_in, gk_in, gv_in, w_in,
    shard_q, total, grad_tokens,
    image, first, grad_middle, grads, w, first_t, acc, grad_image, g, load_sem, swap_sem, got, sum_send, sum_recv, send, recv, *landings,
):
    p = Place(zs)
    meet(p)
    length, width = image.shape
    half = grads.shape[2] // 2
    load_grads = [pltpu.make_async_copy(a, grads.at[i], load_sem.at[i]) for i, a in enumerate((gq_in, gk_in, gv_in))]
    load_first = pltpu.make_async_copy(first_in, first, load_sem.at[3])
    load_w = pltpu.make_async_copy(w_in, w, load_sem.at[4])
    load_image = pltpu.make_async_copy(image_in, image, load_sem.at[5])
    load_middle = pltpu.make_async_copy(grad_middle_in, grad_middle, load_sem.at[6])
    start(load_first, *load_grads, load_w, load_image, load_middle)
    chains = {}
    at = iter(landings)
    for i, (k, lo, m, order) in enumerate(CLOSING):
        cols = pl.ds(lo, m)
        held = lambda x, z, y, k=k, cols=cols: g.at[k, x, z, y, p.c, :, cols]
        chains[i] = Scatter(p, order, held, g.at[k, :, :, :, 1 - p.c, :, cols], [next(at) for _ in range(4)], send.at[i], recv.at[i],
                            [(shard_q.at[part, :, pl.ds(k * PART_GROUP + max(lo - part * PART_GROUP, 0), n)], at0, n)
                             for part, at0, n in pieces(lo, m)])
    half_length = length // 2
    chains["G"] = Swap(p, half_rows(grad_image, 1 - p.x, half_length), grad_tokens.at[p.x], swap_sem)
    chains["S"] = Sum(p, total, got, sum_send, sum_recv)
    own = pltpu.make_async_copy(half_rows(grad_image, p.x, half_length), grad_tokens.at[p.x], load_sem.at[7])

    load_first.wait()
    first_t[...] = first[...].T
    wait(*load_grads)

    def weight_grad(k):
        def one(i, _):
            t, part = lax.div(i, 3), lax.rem(i, 3)
            cols = pl.ds(pl.multiple_of(t * half + k * PART_GROUP, PART_GROUP), PART_GROUP)
            value = nn(first_t[...], grads[part, :, cols]).astype(BF16)
            g[k, t, :, :, :, :, pl.ds(pl.multiple_of(part * PART_GROUP, PART_GROUP), PART_GROUP)] = value.reshape(
                g.shape[2:6] + (PART_GROUP,))
            return 0
        lax.fori_loop(0, 6, one, 0)

    def first_norm_back(which, carry, plan):
        here = pl.ds(pl.multiple_of(which * half_length, half_length), half_length)
        acc[...] = jnp.zeros_like(acc)

        def to_first(i, _):
            t, part = lax.div(i, 3), lax.rem(i, 3)
            cols = pl.ds(pl.multiple_of(t * half, half), half)
            acc[...] += nt(grads[part, here, cols], w[t, :, pl.ds(pl.multiple_of(part * half, half), half)])
            return 0
        lax.fori_loop(0, 6, to_first, 0)
        follow(chains, plan)

        def norm_back(i, carry):
            at = pl.ds(pl.multiple_of(which * half_length + i * ROWS, ROWS), ROWS)
            hat, factor = stats(image[at].astype(F32))
            gf = acc[pl.ds(pl.multiple_of(i * ROWS, ROWS), ROWS)]
            grad_image[at] = (grad_middle[at] + back(gf * norms[0:1], hat, factor)).astype(BF16)
            return carry[0] + jnp.sum(gf * hat, 0, keepdims=True), carry[1] + jnp.sum(gf, 0, keepdims=True)
        return lax.fori_loop(0, half_length // ROWS, norm_back, carry)

    zero = jnp.zeros((1, width), F32)
    weight_grad(0)
    follow(chains, CLOSING_PLANS[0])
    load_w.wait()
    wait(load_image, load_middle)
    sums = first_norm_back(1 - p.x, (zero, zero), CLOSING_PLANS[1])
    follow(chains, CLOSING_PLANS[2])
    weight_grad(1)
    follow(chains, CLOSING_PLANS[3])
    sum_hat, sum_all = first_norm_back(p.x, sums, CLOSING_PLANS[4])
    own.start()
    total[...] = jnp.zeros_like(total)
    total[0:1] = sum_hat
    total[1:2] = sum_all
    total[2:4] = sums_second[...]
    total[4:6, 0:HD] = sums_qk[:, :HD] + sums_qk[:, HD:]
    follow(chains, CLOSING_END)
    own.wait()


def closing(norms, sums_second, sums_qk, image, first, grad_middle, gq, gk, gv, w, zs):
    length, width = image.shape
    rows = width // (4 * zs)
    wide = 3 * PART_GROUP
    square = pltpu.VMEM((length, width), BF16)
    scratch = [
        square, square, pltpu.VMEM((length, width), F32), pltpu.VMEM((3,) + gq.shape, BF16), pltpu.VMEM(w.shape, BF16), square,
        pltpu.VMEM((length // 2, width), F32), square, pltpu.VMEM((2, 2, zs, 2, 2, rows, wide), BF16), DMA((8,)), DMA((2, CHUNKS)),
        pltpu.VMEM((zs + 2, 8, width), F32), DMA((zs + 2,)), DMA((zs + 2,)),
        DMA((len(CLOSING), scatter_sems(zs))), DMA((len(CLOSING), scatter_sems(zs))),
    ]
    for k, lo, m, order in CLOSING:
        scratch += landing(zs, rows, m, order)
    return pl.pallas_call(
        functools.partial(closing_body, zs),
        in_specs=[WHOLE_VMEM] * 3 + [HBM] * 7,
        out_specs=[WHOLE_VMEM, WHOLE_VMEM, HBM],
        out_shape=[jax.ShapeDtypeStruct((3, rows, gq.shape[1] // 2), F32), jax.ShapeDtypeStruct((8, width), F32),
                   jax.ShapeDtypeStruct((2, length // 2, width), BF16)],
        scratch_shapes=scratch,
        compiler_params=params(3),
        name="closing",
    )(norms, sums_second, sums_qk, image, first, grad_middle, gq, gk, gv, w)


def whole_images(tokens, cotangent, w_qkv, wo_t, w_up, w_down_t, norm_gains, norm_shifts, qk_gains):
    zs = lax.axis_size("fsdp") // 4
    rows = w_qkv.shape[0]
    width = tokens.shape[2]
    half = w_qkv.shape[2]
    cols = 3 * half
    first, qn, kn, v, q_raw, k_raw, mixed, inverse, middle, second, norms, image, cot, whole_q, whole_o, whole_u, whole_d = attention(
        qk_gains, norm_gains.T, norm_shifts.T, w_qkv.transpose(1, 0, 2), wo_t, w_up, w_down_t, tokens, cotangent, zs
    )
    result, grad_second, grads_u, grads_d, *states, outputs, whole_u, whole_d = feed(
        second, cot, middle, whole_u, whole_d, zs
    )
    qkv = whole_q.reshape(2, width, cols + 128)
    grad_middle, gq, gk, gv, sums_qk, sums_second, shard_u, shard_d, shard_o, outputs = backward(
        norms, jnp.tile(qk_gains.astype(F32), (1, 2)), cot, grad_second, middle, mixed, whole_o.reshape(2, width, half),
        (qn, kn, v, q_raw, k_raw), inverse, grads_u, grads_d, states, result, outputs, zs
    )
    grad_q, small, grad_tokens = closing(norms, sums_second, sums_qk, image, first, grad_middle, gq, gk, gv, qkv, zs)
    mine = lax.dynamic_slice_in_dim(small, lax.axis_index("fsdp") * rows, rows, 1)
    return (
        outputs,
        grad_tokens.astype(F32),
        grad_q.transpose(1, 0, 2),
        shard_o,
        shard_u,
        shard_d,
        jnp.stack([mine[0], mine[2]], 1),
        jnp.stack([mine[1], mine[3]], 1),
        small[4:6, :HD],
    )


def layer(tokens, *rest):
    if tokens.shape[0] == lax.axis_size("tensor") == 2 and lax.axis_size("fsdp") % 4 == 0:
        return whole_images(tokens, *rest)
    return per_device(tokens, *rest)


def solution(mesh):
    in_specs = (
        P("fsdp", "tensor", None),
        P("fsdp", "tensor", None),
        P("fsdp", None, "tensor"),
        P("fsdp", "tensor"),
        P("fsdp", "tensor"),
        P("fsdp", "tensor"),
        P("fsdp", None),
        P("fsdp", None),
        P(),
    )
    out_specs = (
        P("fsdp", "tensor", None),
        P("fsdp", "tensor", None),
        P("fsdp", None, "tensor"),
        P("fsdp", "tensor"),
        P("fsdp", "tensor"),
        P("fsdp", "tensor"),
        P("fsdp", None),
        P("fsdp", None),
        P(),
    )
    return jax.shard_map(
        layer, mesh=mesh, in_specs=in_specs, out_specs=out_specs, check_vma=False
    )
```

```python
import functools

import jax
import jax.numpy as jnp
from jax import lax
from jax.experimental import pallas as pl
from jax.experimental.pallas import tpu as pltpu
from jax.sharding import PartitionSpec as P

HD = 64


EPSILON = 1e-06


def norm_stats(value):
    center = value - jnp.mean(value, -1, keepdims=True)
    factor = lax.rsqrt(jnp.mean(center * center, -1, keepdims=True) + EPSILON)
    return (center * factor, factor)


def norm_back(grad_hat, normed, factor):
    return factor * (
        grad_hat
        - jnp.mean(grad_hat, -1, keepdims=True)
        - normed * jnp.mean(grad_hat * normed, -1, keepdims=True)
    )


def contract_rows(left, right):
    return lax.dot_general(
        left, right, (((0,), (0,)), ((), ())), preferred_element_type=jnp.float32
    )


def contract_cols(left, right):
    return lax.dot_general(
        left, right, (((1,), (1,)), ((), ())), preferred_element_type=jnp.float32
    )


def per_device(tokens, cotangent, w_qkv, wo_t, w_up, w_down_t, norm_gains, norm_shifts, qk_gains):
    local_rows = tokens.shape[1]
    width = tokens.shape[2]
    head_cols = w_qkv.shape[2]
    local_heads = head_cols // HD
    hidden_cols = w_up.shape[1]
    tensor_count = lax.axis_size("tensor")
    full_len = local_rows * tensor_count
    block = min(512, full_len)
    blocks = full_len // block
    gain_query = qk_gains[0].astype(jnp.float32)
    gain_keys = qk_gains[1].astype(jnp.float32)
    scale_query = HD ** (-0.5)

    def fetch():
        return (
            lax.all_gather(w_qkv, "fsdp", axis=0, tiled=True),
            lax.all_gather(wo_t, "fsdp", axis=0, tiled=True),
            lax.all_gather(w_up, "fsdp", axis=0, tiled=True),
            lax.all_gather(w_down_t, "fsdp", axis=0, tiled=True),
            lax.all_gather(norm_gains, "fsdp", axis=0, tiled=True),
            lax.all_gather(norm_shifts, "fsdp", axis=0, tiled=True),
        )

    def forward(weights, inputs):
        whole_qkv, whole_out, whole_up, whole_down, gains, shifts = weights
        gains = gains.astype(jnp.float32)
        shifts = shifts.astype(jnp.float32)
        flat_qkv = whole_qkv.reshape(width, 3 * head_cols)
        residual = inputs.astype(jnp.float32)
        first_hat, first_factor = norm_stats(residual)
        first = (first_hat * gains[:, 0] + shifts[:, 0]).astype(jnp.bfloat16)
        piece = lax.all_gather(first, "tensor", axis=0, tiled=True)
        first_full = piece
        joined = jnp.dot(piece, flat_qkv, preferred_element_type=jnp.float32)
        joined = joined.reshape(full_len, 3, local_heads, HD)
        query_hat, query_factor = norm_stats(joined[:, 0])
        keys_hat, keys_factor = norm_stats(joined[:, 1])
        query_n = (query_hat * gain_query * scale_query).astype(jnp.bfloat16)
        keys_n = (keys_hat * gain_keys).astype(jnp.bfloat16)
        values = joined[:, 2].astype(jnp.bfloat16)

        def attend(query_block):
            scores = jnp.einsum(
                "qhd,khd->hqk", query_block, keys_n, preferred_element_type=jnp.float32
            )
            largest = jnp.max(scores, -1, keepdims=True)
            exponent = jnp.exp(scores - largest)
            total_sum = jnp.sum(exponent, -1, keepdims=True)
            probs_low = (exponent / total_sum).astype(jnp.bfloat16)
            mixed_block = jnp.einsum(
                "hqk,khd->qhd", probs_low, values, preferred_element_type=jnp.float32
            )
            return (mixed_block.astype(jnp.bfloat16), (largest + jnp.log(total_sum))[..., 0])

        mixed, log_total = lax.map(attend, query_n.reshape(blocks, block, local_heads, HD))
        mixed = mixed.reshape(full_len, head_cols)
        middle = residual + lax.psum_scatter(
            contract_cols(mixed, whole_out), "tensor", scatter_dimension=0, tiled=True
        )
        second_hat, second_factor = norm_stats(middle)
        second = (second_hat * gains[:, 1] + shifts[:, 1]).astype(jnp.bfloat16)
        piece = lax.all_gather(second, "tensor", axis=0, tiled=True)
        hidden = jnp.dot(piece, whole_up, preferred_element_type=jnp.float32)
        active = jax.nn.gelu(hidden, approximate=False).astype(jnp.bfloat16)
        result = (
            middle
            + lax.psum_scatter(
                contract_cols(active, whole_down).astype(jnp.bfloat16),
                "tensor",
                scatter_dimension=0,
                tiled=True,
            ).astype(jnp.float32)
        ).astype(jnp.bfloat16)
        kept = (
            first_hat,
            first_factor,
            first_full,
            query_hat,
            query_factor,
            keys_hat,
            keys_factor,
            query_n,
            keys_n,
            values,
            mixed,
            log_total,
            second_hat,
            second_factor,
            piece,
            hidden,
            active,
        )
        return (kept, result)

    def backward(weights, kept, grad_out):
        whole_qkv, whole_out, whole_up, whole_down, gains, shifts = weights
        gains = gains.astype(jnp.float32)
        flat_qkv = whole_qkv.reshape(width, 3 * head_cols)
        (
            first_hat,
            first_factor,
            first_full,
            query_hat,
            query_factor,
            keys_hat,
            keys_factor,
            query_n,
            keys_n,
            values,
            mixed_keep,
            log_total,
            second_hat,
            second_factor,
            second_full,
            hidden,
            active,
        ) = kept
        piece = lax.all_gather(grad_out, "tensor", axis=0, tiled=True)
        grad_full = piece
        grad_active = jnp.dot(piece, whole_down, preferred_element_type=jnp.float32)
        grad_down = contract_rows(grad_full, active)
        unused_value, gelu_pull = jax.vjp(
            lambda value: jax.nn.gelu(value, approximate=False), hidden
        )
        grad_hidden = gelu_pull(grad_active)[0].astype(jnp.bfloat16)
        grad_up = contract_rows(second_full, grad_hidden)
        grad_second = lax.psum_scatter(
            contract_cols(grad_hidden, whole_up), "tensor", scatter_dimension=0, tiled=True
        )
        grad_middle = grad_out.astype(jnp.float32) + norm_back(
            grad_second * gains[:, 1], second_hat, second_factor
        )
        grad_branch = grad_middle.astype(jnp.bfloat16)
        piece = lax.all_gather(grad_branch, "tensor", axis=0, tiled=True)
        grad_mixed = jnp.dot(piece, whole_out, preferred_element_type=jnp.float32)
        grad_out_w = contract_rows(piece, mixed_keep)
        grad_mixed = grad_mixed.astype(jnp.bfloat16)
        grad_mixed = grad_mixed.reshape(blocks, block, local_heads, HD)

        def attend_back(carry, item):
            grad_keys_sum, grad_values_sum = carry
            query_block, grad_block, log_block = item
            scores = jnp.einsum(
                "qhd,khd->hqk", query_block, keys_n, preferred_element_type=jnp.float32
            )
            probs = jnp.exp(scores - log_block[..., None])
            grad_probs = jnp.einsum(
                "qhd,khd->hqk", grad_block, values, preferred_element_type=jnp.float32
            )
            delta = jnp.sum(probs * grad_probs, -1, keepdims=True)
            grad_scores = (probs * (grad_probs - delta)).astype(jnp.bfloat16)
            grad_query_block = jnp.einsum(
                "hqk,khd->qhd", grad_scores, keys_n, preferred_element_type=jnp.float32
            )
            grad_keys_sum = grad_keys_sum + jnp.einsum(
                "hqk,qhd->khd", grad_scores, query_block, preferred_element_type=jnp.float32
            )
            grad_values_sum = grad_values_sum + jnp.einsum(
                "hqk,qhd->khd",
                probs.astype(jnp.bfloat16),
                grad_block,
                preferred_element_type=jnp.float32,
            )
            return ((grad_keys_sum, grad_values_sum), grad_query_block)

        empty_heads = jnp.zeros((full_len, local_heads, HD), jnp.float32)
        (grad_keys_n, grad_values), grad_query_n = lax.scan(
            attend_back,
            (empty_heads, empty_heads),
            (query_n.reshape(blocks, block, local_heads, HD), grad_mixed, log_total),
        )
        grad_query_n = grad_query_n.reshape(full_len, local_heads, HD)
        grad_query = norm_back(grad_query_n * gain_query * scale_query, query_hat, query_factor)
        grad_keys = norm_back(grad_keys_n * gain_keys, keys_hat, keys_factor)
        qk_grad = jnp.stack(
            [
                jnp.sum(grad_query_n * query_hat * scale_query, (0, 1)),
                jnp.sum(grad_keys_n * keys_hat, (0, 1)),
            ]
        )
        grad_joined = jnp.stack([grad_query, grad_keys, grad_values], 1).astype(jnp.bfloat16)
        grad_joined = grad_joined.reshape(full_len, 3 * head_cols)
        grad_qkv = contract_rows(first_full, grad_joined).reshape(width, 3, head_cols)
        grad_first = lax.psum_scatter(
            contract_cols(grad_joined, flat_qkv).astype(jnp.bfloat16),
            "tensor",
            scatter_dimension=0,
            tiled=True,
        ).astype(jnp.float32)
        grad_input = grad_middle + norm_back(grad_first * gains[:, 0], first_hat, first_factor)
        gain_grad = jnp.stack(
            [jnp.sum(grad_first * first_hat, 0), jnp.sum(grad_second * second_hat, 0)], 1
        )
        shift_grad = jnp.stack([jnp.sum(grad_first, 0), jnp.sum(grad_second, 0)], 1)
        return (
            (grad_qkv, grad_out_w, grad_up, grad_down, gain_grad, shift_grad, qk_grad),
            grad_input,
        )

    def micro_step(totals, item):
        inputs, grad_out = item
        forward_weights = fetch()
        kept, result = forward(forward_weights, inputs)
        backward_weights = fetch()
        grads, grad_input = backward(backward_weights, kept, grad_out)
        totals = tuple((total + part for total, part in zip(totals, grads)))
        return (totals, (result, grad_input))

    out_cols_count = wo_t.shape[1]
    start_sums = (
        jnp.zeros((width, 3, head_cols), jnp.float32),
        jnp.zeros((width, out_cols_count), jnp.float32),
        jnp.zeros((width, hidden_cols), jnp.float32),
        jnp.zeros((width, hidden_cols), jnp.float32),
        jnp.zeros((width, 2), jnp.float32),
        jnp.zeros((width, 2), jnp.float32),
        jnp.zeros((2, HD), jnp.float32),
    )
    totals, (outputs, grad_tokens) = lax.scan(micro_step, start_sums, (tokens, cotangent))
    out_total = totals[1]
    grad_qkv, grad_out_w, grad_up, grad_down = (
        lax.psum_scatter(
            totals[0].astype(jnp.bfloat16), "fsdp", scatter_dimension=0, tiled=True
        ).astype(jnp.float32),
        lax.psum_scatter(
            out_total.astype(jnp.bfloat16), "fsdp", scatter_dimension=0, tiled=True
        ).astype(jnp.float32),
        lax.psum_scatter(
            totals[2].astype(jnp.bfloat16), "fsdp", scatter_dimension=0, tiled=True
        ).astype(jnp.float32),
        lax.psum_scatter(
            totals[3].astype(jnp.bfloat16), "fsdp", scatter_dimension=0, tiled=True
        ).astype(jnp.float32),
    )
    gain_total, shift_total, qk_total = lax.psum(
        (totals[4], totals[5], totals[6]), ("fsdp", "tensor")
    )
    own_rows = width // lax.axis_size("fsdp")
    offset = lax.axis_index("fsdp") * own_rows
    gain_part = lax.dynamic_slice_in_dim(gain_total, offset, own_rows, 0)
    shift_part = lax.dynamic_slice_in_dim(shift_total, offset, own_rows, 0)
    return (
        outputs,
        grad_tokens,
        grad_qkv,
        grad_out_w,
        grad_up,
        grad_down,
        gain_part,
        shift_part,
        qk_total,
    )


PAIR = 2 * HD
F32, BF16 = jnp.float32, jnp.bfloat16
LIMIT = 60 << 20


def nn(a, b):
    return lax.dot_general(a, b, (((1,), (0,)), ((), ())), preferred_element_type=F32)


def nt(a, b):
    return lax.dot_general(a, b, (((1,), (1,)), ((), ())), preferred_element_type=F32)


def stats(value):
    center = value - jnp.mean(value, -1, keepdims=True)
    factor = lax.rsqrt(jnp.mean(center * center, -1, keepdims=True) + EPSILON)
    return center * factor, factor


def back(grad_hat, normed, factor):
    return factor * (
        grad_hat
        - jnp.mean(grad_hat, -1, keepdims=True)
        - normed * jnp.mean(grad_hat * normed, -1, keepdims=True)
    )


def head_mean_matrix(width):
    row = lax.broadcasted_iota(jnp.int32, (width, width), 0) // HD
    col = lax.broadcasted_iota(jnp.int32, (width, width), 1) // HD
    return jnp.where(row == col, 1.0 / HD, 0.0).astype(BF16)


def head_mean(value, matrix):
    high = value.astype(BF16)
    low = (value - high.astype(F32)).astype(BF16)
    return nn(high, matrix) + nn(low, matrix)


def head_stats(value, matrix):
    center = value - head_mean(value, matrix)
    factor = lax.rsqrt(head_mean(center * center, matrix) + EPSILON)
    return center * factor, factor


def head_back(grad_hat, normed, factor, matrix):
    return factor * (
        grad_hat - head_mean(grad_hat, matrix) - normed * head_mean(grad_hat * normed, matrix)
    )


MESH = pl.DeviceIdType.MESH
ALL = slice(None)


class Place:
    def __init__(self, zs):
        f = lax.axis_index("fsdp")
        self.zs = zs
        self.x = lax.axis_index("tensor")
        self.c = lax.rem(f, 2)
        self.y = lax.rem(lax.div(f, 2), 2)
        self.z = lax.div(f, 4)

    def dev(self, z=None, y=None, c=None, x=None):
        z = self.z if z is None else z
        y = self.y if y is None else y
        c = self.c if c is None else c
        x = self.x if x is None else x
        return {"fsdp": (z * 2 + y) * 2 + c, "tensor": x}

    def along_z(self):
        return [lax.rem(self.z + k, self.zs) for k in range(1, self.zs)]

    def peers(self):
        out = [self.dev(z=z) for z in self.along_z()]
        return out + [self.dev(y=1 - self.y), self.dev(c=1 - self.c), self.dev(x=1 - self.x)]


def meet(place):
    barrier = pltpu.get_barrier_semaphore()
    peers = place.peers()
    for peer in peers:
        pl.semaphore_signal(barrier, inc=1, device_id=peer, device_id_type=MESH)
    pl.semaphore_wait(barrier, len(peers))


def remote(src, dst, send, recv, peer):
    return pltpu.make_async_remote_copy(
        src_ref=src, dst_ref=dst, send_sem=send, recv_sem=recv, device_id=peer, device_id_type=MESH
    )


def start(*copies):
    for copy in copies:
        copy.start()


def wait(*copies):
    for copy in copies:
        copy.wait()


class Gather:
    def __init__(self, place, shard, whole, lo, size, order, send, recv, since=0):
        p = self.p = place
        cols = self.cols = pl.ds(lo, size)
        self.shard = None if shard is None else shard.at[:, cols]
        self.whole = whole
        self.order, self.since = order, since
        self.send, self.recv = send, recv
        if shard is not None:
            self.own = pltpu.make_async_copy(self.shard, self.at({}), self.send.at[2 * p.zs + 7])

    def at(self, index):
        p = self.p
        own = {"x": p.x, "y": p.y, "z": p.z}
        x, y, z = (index.get(d, own[d]) for d in "xyz")
        return self.whole.at[x, z, y, p.c, :, self.cols]

    def others(self, d):
        return self.p.along_z() if d == "z" else [1 - getattr(self.p, d)]

    def copies(self, base, i, pairs):
        base += sum(len(self.others(d)) for d in self.order[:i])
        return [remote(src, dst, self.send.at[base + k], self.recv.at[base + k], peer) for k, (src, dst, peer) in enumerate(pairs)]

    def stage(self, i):
        d = self.order[i]
        held = self.at({e: ALL for e in self.order[:i]})
        src = self.shard if i == 0 and self.shard is not None else held
        return self.copies(0, i, [(src, held, self.p.dev(**{d: to})) for to in self.others(d)])

    def core_parts(self, i):
        done = {e: ALL for e in self.order[:i]}
        d = self.order[i]
        if i == 0:
            refs = [self.at({d: ALL})]
        else:
            refs = [self.at({**done, d: to}) for to in self.others(d)]
        peer = self.p.dev(c=1 - self.p.c)
        return self.copies(self.p.zs + 1, i, [(ref, ref, peer) for ref in refs])

    def start(self, i):
        if i == 0 and self.shard is not None:
            self.own.start()
        if i < 3:
            start(*self.stage(i))
        if i > 0:
            start(*self.core_parts(i - 1))

    def done(self, i):
        if i == 0 and self.shard is not None:
            self.own.wait()
        if i < 3:
            wait(*self.stage(i))
        else:
            self.rest(self.since - 1 if self.since else 0, 3)

    def rest(self, lo, hi):
        for i in range(lo, hi):
            wait(*self.core_parts(i))


def gather_sems(zs):
    return 2 * zs + 8


CHUNKS = 4


class Swap:
    def __init__(self, place, src, dst, sems):
        rows = src.shape[0] // CHUNKS
        part = lambda ref, i: ref.at[pl.ds(i * rows, rows)]
        self.copies = [remote(part(src, i), part(dst, i), sems.at[0, i], sems.at[1, i], place.dev(x=1 - place.x)) for i in range(CHUNKS)]

    def start(self, i):
        self.copies[i].start()

    def done(self, i):
        self.copies[i].wait()


def half_rows(ref, which, rows):
    return ref.at[pl.ds(pl.multiple_of(which * rows, rows), rows)]


class Sum:
    def __init__(self, place, total, got, send, recv):
        self.p, self.total, self.got, self.send, self.recv = place, total, got, send, recv

    def copies(self, i):
        p = self.p
        if i < 3:
            peers = [(p.dev(c=1 - p.c), p.dev(x=1 - p.x), p.dev(y=1 - p.y))[i]]
        else:
            peers = [p.dev(z=z) for z in p.along_z()]
        return [remote(self.total, self.got.at[i + k], self.send.at[i + k], self.recv.at[i + k], peer)
                for k, peer in enumerate(peers)]

    def start(self, i):
        start(*self.copies(i))

    def done(self, i):
        copies = self.copies(i)
        wait(*copies)
        total = self.total[...]
        for k in range(len(copies)):
            total = total + self.got[i + k]
        self.total[...] = total


def add_slabs(count, pair):
    def body(i, _):
        into, from_ = pair(i)
        into[...] = into[...] + from_[...]
        return 0
    lax.fori_loop(0, count, body, 0)


class Scatter:
    def __init__(self, place, order, held, away, landings, send, recv, out=None):
        self.p, self.order, self.held, self.away = place, order, held, away
        self.landings, self.send, self.recv, self.out = landings, send, recv, out

    def size(self, d):
        return self.p.zs if d == "z" else 2

    def others(self, d):
        return self.p.along_z() if d == "z" else [1 - getattr(self.p, d)]

    def part(self, i, value, rest=None):
        at = {e: ALL for e in "xzy"}
        at.update(rest or {})
        at.update({e: getattr(self.p, e) for e in self.order[:i]})
        at[self.order[i]] = value
        return self.held(at["x"], at["z"], at["y"])

    def copies(self, i):
        p = self.p
        if i == 0:
            return [remote(self.away, self.landings[0], self.send.at[0], self.recv.at[0], p.dev(c=1 - p.c))]
        d = self.order[i - 1]
        base = 1 + sum(len(self.others(e)) for e in self.order[:i - 1])
        return [remote(self.part(i - 1, to), self.landings[i].at[k], self.send.at[base + k], self.recv.at[base + k], p.dev(**{d: to}))
                for k, to in enumerate(self.others(d))]

    def start(self, i):
        start(*self.copies(i))

    def done(self, i):
        p = self.p
        wait(*self.copies(i))
        if i == 3:
            value = self.part(2, getattr(p, self.order[2]))[...].astype(F32)
            for k in range(len(self.others(self.order[2]))):
                value = value + self.landings[3][k].astype(F32)
            for ref, lo, size in self.out:
                ref[...] = value[:, lo:lo + size]
            return
        dims = [e for e in "xzy" if e not in self.order[:i]]
        walked = [e for e in dims if e != "z"]

        def body(j, _):
            at, left = {"z": ALL}, j
            for e in reversed(walked):
                at[e] = lax.rem(left, 2)
                left = lax.div(left, 2)
            index = tuple(at[e] for e in dims)
            if i == 0:
                into, froms = self.held(at["x"], at["z"], at["y"]), [self.landings[0].at[index]]
            else:
                d = self.order[i - 1]
                into = self.part(i - 1, getattr(p, d), {e: at[e] for e in dims})
                froms = [self.landings[i].at[(k,) + index] for k in range(len(self.others(d)))]
            value = into[...]
            if len(froms) == 1:
                value = value + froms[0][...]
            else:
                value = value.astype(F32)
                for from_ in froms:
                    value = value + from_[...].astype(F32)
                value = value.astype(BF16)
            into[...] = value
            return 0
        lax.fori_loop(0, 2 ** len(walked), body, 0)

    def state(self, stages):
        return self.part(stages - 2, getattr(self.p, self.order[stages - 2]))


def scatter_sems(zs):
    return zs + 2


def rest_shape(zs, rows, m, gone):
    size = {"x": 2, "z": zs, "y": 2}
    return tuple(size[e] for e in "xzy" if e not in gone) + (rows, m)


def landing(zs, rows, m, order, since=0):
    shapes = [rest_shape(zs, rows, m, "")]
    for i, d in enumerate(order):
        shapes.append((zs - 1 if d == "z" else 1,) + rest_shape(zs, rows, m, order[:i + 1]))
    return [pltpu.VMEM(shape, BF16) for shape in shapes[since:]]


def follow(chains, plan):
    for name, i in plan:
        if i < 0:
            chains[name].start(-1 - i)
        else:
            chains[name].done(i)


def at_steps(step, chains, plans):
    for at, plan in enumerate(plans):
        if plan:
            pl.when(step == at)(functools.partial(follow, chains, plan))


def on(step, hooks):
    for at, hook in hooks.items():
        pl.when(step == at)(hook)


HBM = pl.BlockSpec(memory_space=pl.ANY)
WHOLE_VMEM = pl.BlockSpec(memory_space=pltpu.VMEM)
DMA = pltpu.SemaphoreType.DMA


def params(collective_id):
    return pltpu.CompilerParams(collective_id=collective_id, has_side_effects=True, vmem_limit_bytes=LIMIT)


Q_ORDERS = ('zyx', 'xzy', 'zxy', 'xzy', 'zyx', 'zxy', 'xzy')
O_ORDER = 'zxy'
U_ORDERS = ('xyz', 'zyx', 'zxy', 'xzy')
D_ORDERS = ('xzy', 'xzy', 'yzx', 'yzx')
FEED_SINCE = (3, 1, 0)
FEED_ORDERS = ('zyx', 'xyz', 'yzx', 'xyz')
FEED_DONE = (2, 2)
LATE_ORDERS = ('xzy', 'xyz', 'yxz', 'yxz')
O_BACK_ORDER = 'zxy'
CLOSING = ((0, 0, 256, 'zyx'), (0, 256, 256, 'yxz'), (0, 512, 256, 'xyz'), (1, 0, 256, 'yxz'), (1, 256, 256, 'zyx'), (1, 512, 256, 'yxz'))
ATTENTION_LEAVES = (('U1', 3), ('D1', 3), ('U2', 1), ('D2', 1), ('U3', 0), ('D3', 0))
OPENING_PLANS = (
    ((6, -1), ('T', -1), (0, -1), (2, -1), ('D2', -1), (6, 0), (1, -1), ('D2', 0), (1, 0), (3, -1), (0, 0), (6, -2), (0, -2), (2, 0), (1, -2), ('T', 0), ('T', -2), (3, 0), (2, -2), (0, 1), (6, 1), (6, -3), (3, -2), (2, 1), (0, -3), (2, -3), (1, 1), (4, -1), ('T', 1), ('T', -3), (6, 2), (6, -4), (1, -3), (6, 3),),
    ((3, 1), (5, -1), (4, 0), ('O', -1), (2, 2), (2, -4), (3, -3), (0, 2), (0, -4), ('U0', -1), ('T', 2), ('T', -4), (2, 3), (1, 2), (1, -4), (4, -2), (0, 3), ('U0', 0), ('D0', -1), (5, 0), ('U1', -1), (1, 3), ('D0', 0), (5, -2), ('O', 0), ('D0', -2), (3, 2), (3, -4), ('U0', -2), (4, 1), ('T', 3), (4, -3),),
)
ATTENTION_PLANS = (
    ((3, 3), (5, 1), (5, -3), ('O', -2),),
    (('U0', 1),),
    (('U1', 0), ('U0', -3), ('U1', -2),),
    (),
    (),
    (),
    ((4, 2), (4, -4), ('D1', -1), (5, 2), (5, -4),),
    (('O', 1), ('O', -3), ('C', -1), ('U1', 1), (4, 3), ('D1', 0), ('U1', -3), (5, 3),),
    (('D0', 1), ('D0', -3), ('D1', -2),),
    (),
    (),
    (),
    (('C', 0), ('C', -2),),
    (),
    (),
    (),
    (('O', 2), ('O', -4), ('U1', 2),),
    (('D0', 2), ('D0', -4), ('C', 1), ('C', -3),),
    (('O', 3), ('D1', 1), ('D1', -3), ('U2', -1),),
    (('D0', 3),),
    (('U0', 2), ('U0', -4), ('C', 2), ('C', -4),),
    (),
    (('U2', 0),),
    (('U0', 3),),
)
ATTENTION_END = (('C', 3), ('D1', 2),)
FEED_PLANS = (
    (('U1', -4), ('D1', -4), ('U2', -2), ('D2', -2), ('U3', -1), ('D3', -1),),
    (('D3', 0), ('D3', -2), ('U3', 0), ('U1', 3), ('D1', 3), ('U2', 1), ('U2', -3),),
    (),
    (('D2', 1), ('D2', -3), ('U3', -2),),
    (('u0', -1), ('d0', -1),),
    (('U2', 2), ('U2', -4),),
    (('D3', 1), ('D3', -3),),
    (('u0', 0), ('u0', -2), ('d0', 0), ('D2', 2), ('D2', -4), ('d0', -2), ('U2', 3), ('U3', 1), ('U3', -3),),
    (('u1', -1), ('d1', -1), ('D2', 3),),
    (),
    (('D3', 2), ('D3', -4), ('u1', 0), ('u1', -2), ('d1', 0), ('d1', -2),),
    (('U3', 2), ('U3', -4), ('D3', 3),),
    (('d0', 1), ('U3', 3),),
    (('u0', 1), ('u1', 1),),
    (('d1', 1),),
    (),
)
FEED_END = ()
BACKWARD_PLANS = (
    (('u0', -3), ('d0', -3), ('u1', -3), ('u2', -1), ('d2', -1), ('u3', -1), ('d3', -1), ('R', -1),),
    (),
    (),
    (('u0', 2), ('u0', -4), ('d1', -3), ('R', 0), ('R', -2), ('d0', 2), ('d0', -4),),
    (('u1', 2),),
    (('u0', 3), ('u1', -4), ('u2', 0), ('o', -1), ('d2', 0), ('u3', 0), ('u3', -2), ('d3', 0), ('d1', 2), ('d1', -4), ('d3', -2), ('d0', 3), ('R', 1), ('u2', -2),),
    (('u1', 3), ('d2', -2), ('o', 0), ('o', -2),),
    (('d1', 3),),
    (),
    (),
    (),
    (('u2', 1), ('u2', -3), ('R', -3),),
    (('u3', 1), ('d3', 1), ('d2', 1), ('d2', -3), ('u3', -3),),
    (),
    (('R', 2), ('d3', -3),),
    (('d2', 2), ('d2', -4), ('o', 1), ('u3', 2), ('o', -3), ('u3', -4),),
    (),
    (('d3', 2), ('R', -4), ('u2', 2), ('u2', -4), ('d3', -4), ('o', 2), ('o', -4),),
    (),
    (('u2', 3), ('o', 3), ('R', 3),),
)
BACKWARD_END = (('d2', 3), ('u3', 3), ('d3', 3),)
CLOSING_PLANS = (
    ((0, -1), (1, -1), (2, -1),),
    (),
    (('G', -1),),
    ((3, -1), (0, 0), (0, -2), (4, -1), (1, 0), (1, -2), (5, -1), (2, 0), (2, -2),),
    (('G', 0), ('G', -2),),
)
CLOSING_END = (('S', -1), (3, 0), (3, -2), (4, 0), (4, -2), (5, 0), (1, 1), (5, -2), ('S', 0), (2, 1), ('S', -2), ('S', 1), (1, -3), ('G', 1), ('G', -3), (0, 1), (3, 1), ('S', -3), (5, 1), (0, -3), (1, 2), (1, -4), (3, -3), ('S', 2), ('S', -4), (2, -3), (0, 2), (4, 1), (4, -3), ('G', 2), (0, -4), (3, 2), (3, -4), (5, -3), (2, 2), (1, 3), (2, -4), (0, 3), ('G', -4), (4, 2), ('S', 3), (5, 2), (4, -4), (5, -4), (3, 3), (2, 3), (4, 3), (5, 3), ('G', 3),)


Q_TILE = 256
ATTEND_TILE = 512
ROWS = 256
FF_GROUP = 512


def full(shape):
    return pl.BlockSpec(shape, lambda s: (0,) * len(shape), pipeline_mode=pl.Buffered(1))


def clipped(shape, axis, first, count):
    def at(s):
        i = jnp.clip(s - first, 0, count - 1)
        return (i, 0) if axis == 0 else (0, i)
    return pl.BlockSpec(shape, at)


def tile_of(part, s):
    i = jnp.clip(s - 4 * part, 0, 3)
    column = lax.div(i, 2)
    return lax.rem(i, 2) * 2 + (1 - column if part == 0 else column)


def project_step(step, joined, gains, kept, blocks):
    tile = joined.shape[1]
    qn_s, kn_s, v_s = kept
    qn, kn, v, q_raw, k_raw = blocks
    matrix = head_mean_matrix(tile)

    def cols(part):
        return pl.ds(pl.multiple_of(tile_of(part, step) * tile, tile), tile)

    @pl.when(step < 4)
    def _():
        value = joined.astype(BF16)
        v[...] = value
        v_s[:, cols(0)] = value

    @pl.when((step >= 4) & (step < 8))
    def _():
        hat, _f = head_stats(joined, matrix)
        value = (hat * gains[1:2]).astype(BF16)
        kn[...] = value
        kn_s[:, cols(1)] = value
        k_raw[...] = joined.astype(BF16)

    @pl.when(step >= 8)
    def _():
        hat, _f = head_stats(joined, matrix)
        value = (hat * gains[0:1] * (HD ** -0.5)).astype(BF16)
        qn[...] = value
        qn_s[:, cols(2)] = value
        q_raw[...] = joined.astype(BF16)


def attend_step(query_all, keys, values, mixed_s, cols, mixed, inverse):
    length = keys.shape[0]
    lane = lax.broadcasted_iota(jnp.int32, (1, PAIR), 1) < HD
    zero = jnp.zeros((), BF16)
    values_t = values.astype(F32).T.astype(BF16)
    ones = jnp.ones((16, length), BF16)
    heads = [(jnp.where(mask, keys, zero), jnp.concatenate([values_t[h * HD:(h + 1) * HD], ones], axis=0))
             for h, mask in ((0, lane), (1, ~lane))]
    for i in range(length // ATTEND_TILE):
        at = slice(i * ATTEND_TILE, (i + 1) * ATTEND_TILE)
        query = query_all[at]
        got, inv = [], []
        for keys_h, values_h in heads:
            both = nn(values_h, jnp.exp(nt(keys_h, query)).astype(BF16))
            one_over = 1.0 / both[HD:HD + 1]
            got.append(both[:HD] * one_over)
            inv.append(jnp.broadcast_to(one_over, (HD, ATTEND_TILE)))
        value = jnp.concatenate(got, axis=0).T.astype(BF16)
        mixed[at] = value
        mixed_s[at, cols] = value
        inverse[at] = jnp.concatenate(inv, axis=0).T


PROJECT_STEPS = 12


def first_after(plans, name):
    return max([at for at, plan in enumerate(plans) if (name, 3) in plan], default=0)


def attention_body(
    zs, pairs, qk_gains, norm_gains, norm_shifts, q_in, o_in, u_in, d_in, tokens, cot_in,
    first, qn, kn, v, q_raw, k_raw, mixed, inverse, middle, second, norms, image, cot, whole_q, whole_o, whole_u, whole_d,
    image_v, qn_s, kn_s, v_s, mixed_s, out_w, tiles, q_v, o_v, u_v, d_v, cot_v, side_v, turn, local_sem, send, recv, swap_sem,
):
    step = pl.program_id(0)
    p = Place(zs)
    length = image_v.shape[0]
    half, rows = whole_o.shape[5], whole_o.shape[4]
    tile = half // 2
    head0, row0 = PROJECT_STEPS, PROJECT_STEPS + pairs
    n = FF_GROUP
    mine = pl.ds(pl.multiple_of(p.x * (length // 2), length // 2), length // 2)
    chains = {
        "T": Swap(p, tokens.at[1 - p.x], half_rows(image_v, p.x, length // 2), swap_sem.at[0]),
        "C": Swap(p, cot_in.at[1 - p.x], half_rows(cot, p.x, length // 2), swap_sem.at[1]),
    }
    local = lambda i, src, dst: pltpu.make_async_copy(src, dst, local_sem.at[i])
    own_shards = [local(i, a, b) for i, (a, b) in enumerate(((o_in, o_v), (u_in, u_v), (d_in, d_v)))]
    own_shards += [local(i, q_in.at[k], q_v.at[:, pl.ds(k * half, half)]) for i, k in ((3, 0), (12, 1), (13, 2))]
    own_tokens = local(4, tokens.at[p.x], image_v.at[mine])
    own_cot = [local(5, cot_in.at[p.x], cot_v), local(6, cot_v, cot.at[mine])]
    keep_image = local(7, image_v, image)
    side = local(8, whole_q.at[0, :, :, :, :, pl.ds(3 * half, PAIR)], side_v)
    load_out = local(9, whole_o, out_w)
    starts = (2 * half + tile, 2 * half, half, half + tile, 0, tile)
    for i, lo in enumerate(starts):
        chains[i] = Gather(p, q_v, whole_q, lo, tile, Q_ORDERS[i], send.at[i], recv.at[i])
    chains[6] = Gather(p, q_v, whole_q, 3 * half, PAIR, Q_ORDERS[6], send.at[15], recv.at[15])

    def load_tile(i):
        return local(10 + i % 2, whole_q.at[:, :, :, :, :, pl.ds(starts[i], tile)], tiles.at[i % 2])

    chains["O"] = Gather(p, o_v, whole_o, 0, half, O_ORDER, send.at[6], recv.at[6])
    for j in range(4):
        chains[f"U{j}"] = Gather(p, u_v, whole_u, j * n, n, U_ORDERS[j], send.at[7 + j], recv.at[7 + j])
        chains[f"D{j}"] = Gather(p, d_v, whole_d, j * n, n, D_ORDERS[j], send.at[11 + j], recv.at[11 + j])

    @pl.when(step == 0)
    def _():
        start(*own_shards, own_tokens, own_cot[0])
        turn[...] = jnp.zeros_like(turn)
        turn[0:2, 0:rows] = norm_gains[...].astype(F32)
        turn[2:4, 0:rows] = norm_shifts[...].astype(F32)
        q_v[:, 3 * half:] = turn[...].T[:rows].astype(BF16)
        meet(p)
        wait(*own_shards)
        for name, stages in ATTENTION_LEAVES:
            if stages == 0:
                chains[name].own.start()

        def norm(which):
            def rows_norm(i, _):
                at = pl.ds(pl.multiple_of(which * (length // 2) + i * ROWS, ROWS), ROWS)
                hat, _f = stats(image_v[at].astype(F32))
                first[at] = (hat * norms[0:1] + norms[2:3]).astype(BF16)
                return 0
            lax.fori_loop(0, length // 2 // ROWS, rows_norm, 0)

        follow(chains, OPENING_PLANS[0])
        side.start()
        own_cot[0].wait()
        own_cot[1].start()
        side.wait()
        norms[...] = side_v[...].reshape(-1, PAIR).astype(F32).T[:8]
        own_tokens.wait()
        norm(p.x)
        follow(chains, OPENING_PLANS[1])
        load_tile(0).start()
        keep_image.start()
        norm(1 - p.x)

    at_steps(step, chains, ATTENTION_PLANS)

    on(step, {0: lambda: load_tile(0).wait()})
    for i in range(1, 6):
        on(step, {max(2 * i - 2, first_after(ATTENTION_PLANS, i)): lambda i=i: load_tile(i).start()})
        on(step, {2 * i: lambda i=i: load_tile(i).wait()})
    on(step, {max(1, first_after(ATTENTION_PLANS, "O")): lambda: load_out.start()})
    on(step, {row0: lambda: load_out.wait()})

    @pl.when(step < head0)
    def _():
        gains = qk_gains[...].astype(F32)
        gains = jnp.concatenate([gains] * (tile // HD), axis=1)
        w = tiles[lax.rem(lax.div(step, 2), 2), lax.rem(step, 2)].reshape(-1, tile)
        project_step(step, nn(first[...], w), gains, (qn_s, kn_s, v_s), (qn, kn, v, q_raw, k_raw))

    @pl.when((step >= head0) & (step < row0))
    def _():
        cols = pl.ds(pl.multiple_of((step - head0) * PAIR, PAIR), PAIR)
        attend_step(qn_s[:, cols], kn_s[:, cols], v_s[:, cols], mixed_s, cols, mixed, inverse)

    @pl.when(step >= row0)
    def _():
        at = pl.ds(pl.multiple_of((step - row0) * ROWS, ROWS), ROWS)
        w0, w1 = (out_w[t].reshape(-1, half) for t in range(2))
        value = image_v[at].astype(F32) + nt(mixed_s[at, :half], w0) + nt(mixed_s[at, half:], w1)
        middle[...] = value
        hat, _f = stats(value)
        second[...] = (hat * norms[1:2] + norms[3:4]).astype(BF16)

    @pl.when(step == pl.num_programs(0) - 1)
    def _():
        follow(chains, ATTENTION_END)
        for name, stages in ATTENTION_LEAVES:
            chains[name].rest(0, stages - 1)
            if stages == 0:
                chains[name].own.wait()
        wait(own_cot[1], keep_image)


def attention(qk_gains, norm_gains, norm_shifts, q, o, u, d, tokens, cot, zs):
    rows = o.shape[0]
    length, width = 2 * tokens.shape[1], tokens.shape[2]
    half = o.shape[1]
    pairs = 2 * half // PAIR
    head0, row0 = PROJECT_STEPS, PROJECT_STEPS + pairs
    tile = half // 2
    tiles = lambda part: pl.BlockSpec((length, tile), lambda s: (0, tile_of(part, s)))
    heads = clipped((length, PAIR), 1, head0, pairs)
    by_rows = clipped((ROWS, width), 0, row0, length // ROWS)
    bf = jax.ShapeDtypeStruct((length, 2 * half), BF16)
    square = jax.ShapeDtypeStruct((length, width), BF16)
    f32 = lambda *shape: jax.ShapeDtypeStruct(shape, F32)
    whole = lambda n: jax.ShapeDtypeStruct((2, zs, 2, 2, rows, n), BF16)
    store = pltpu.VMEM((length, 2 * half), BF16)
    wide = lambda n: pltpu.VMEM((rows, n), BF16)
    return pl.pallas_call(
        functools.partial(attention_body, zs, pairs),
        grid=(row0 + length // ROWS,),
        in_specs=[full(qk_gains.shape), full(norm_gains.shape), full(norm_shifts.shape)] + [HBM] * 6,
        out_specs=[full((length, width)), tiles(2), tiles(1), tiles(0), tiles(2), tiles(1), heads, heads, by_rows, by_rows,
                   full((8, width))] + [HBM] * 6,
        out_shape=[square, bf, bf, bf, bf, bf, bf, f32(length, 2 * half), f32(length, width), square, f32(8, width),
                   square, square, whole(3 * half + PAIR), whole(half), whole(u.shape[1]), whole(d.shape[1])],
        scratch_shapes=[pltpu.VMEM((length, width), BF16), store, store, store, store, pltpu.VMEM((2, zs, 2, 2, rows, half), BF16),
                        pltpu.VMEM((2, 2, zs, 2, 2, rows, tile), BF16), wide(3 * half + PAIR), wide(half), wide(u.shape[1]), wide(d.shape[1]),
                        pltpu.VMEM((length // 2, width), BF16), pltpu.VMEM((zs, 2, 2, rows, PAIR), BF16),
                        pltpu.VMEM((PAIR, PAIR), F32), DMA((14,)), DMA((16, gather_sems(zs))), DMA((16, gather_sems(zs))), DMA((2, 2, CHUNKS))],
        compiler_params=params(0),
        name="attention",
    )(qk_gains, norm_gains, norm_shifts, q, o, u, d, tokens, cot)


def gelu_parts(v):
    bell = jnp.exp(v * v * -0.5)
    t = 1.0 / (1.0 + (0.3275911 * 0.7071067811865476) * jnp.abs(v))
    poly = t * (0.127414796 + t * (-0.142248368 + t * (0.7107068705 + t * (-0.7265760135 + t * 0.5307027145))))
    tail = poly * bell
    return jnp.where(v >= 0, 1.0 - tail, tail), bell * 0.3989422804014327


def feed_body(
    zs, second, cot, middle, _u, _d,
    result, grad_second, grad_u, grad_d, state_0, state_1, state_2, state_3, outputs, whole_u, whole_d,
    acc, second_t, cot_t, active, grad_hidden, tiles, g, tile_sem, misc_sem, send, recv, *landings,
):
    step = pl.program_id(0)
    p = Place(zs)
    length = second.shape[0]
    n = FF_GROUP
    state_refs = (state_0, state_1, state_2, state_3)
    chains = {}
    for j in (1, 2, 3):
        for i, (name, w, orders) in enumerate((("U", whole_u, U_ORDERS), ("D", whole_d, D_ORDERS))):
            k = 2 * j - 2 + i
            chains[f"{name}{j}"] = Gather(p, None, w, j * n, n, orders[j], send.at[k], recv.at[k], FEED_SINCE[j - 1])
    at, states = iter(landings), []
    for j in range(2):
        for k in range(2):
            i = 2 * j + k
            held = lambda x, z, y, j=j, k=k: g.at[k, j, x, z, y, p.c]
            s = Scatter(p, FEED_ORDERS[i], held, g.at[k, j, :, :, :, 1 - p.c], [next(at) for _ in range(FEED_DONE[j])], send.at[6 + i], recv.at[6 + i])
            chains[f"{'ud'[k]}{j}"] = s
            states.append(pltpu.make_async_copy(s.state(FEED_DONE[j]), state_refs[i], misc_sem.at[1 + i]))
    init = pltpu.make_async_copy(middle, acc, misc_sem.at[0])
    mine = pl.ds(pl.multiple_of(p.x * (length // 2), length // 2), length // 2)
    own = pltpu.make_async_copy(result.at[mine], outputs.at[p.x], misc_sem.at[9])
    outs = [pltpu.make_async_copy(g.at[k, j], (grad_u, grad_d)[k].at[j - 2], misc_sem.at[5 + 2 * (j - 2) + k])
            for j in (2, 3) for k in range(2)]

    def loads(s):
        j, t = (s // 2, s % 2) if isinstance(s, int) else (lax.div(s, 2), lax.rem(s, 2))
        slot = t
        cols = pl.ds(j * n if isinstance(s, int) else pl.multiple_of(j * n, n), n)
        return [pltpu.make_async_copy(w.at[t, :, :, :, :, cols], tiles.at[k, slot], tile_sem.at[k, slot])
                for k, w in ((0, whole_u), (1, whole_d))]

    @pl.when(step == 0)
    def _():
        meet(p)
        start(*loads(0))
        start(*loads(1))
        init.start()
        follow(chains, FEED_PLANS[0])
        second_t[...] = second[...].T
        cot_t[...] = cot[...].T
        grad_second[...] = jnp.zeros_like(grad_second)

    at_steps(step, chains, ((),) + FEED_PLANS[2::2])
    for s in range(2, 8):
        here = first_after(FEED_PLANS, f"U{s // 2}"), first_after(FEED_PLANS, f"D{s // 2}")
        on(step, {max(s - 1, (max(here) + 1) // 2): lambda s=s: start(*loads(s))})
    on(step, {7: lambda: start(*outs[:2])})
    wait(*loads(step))

    @pl.when(step == 0)
    def _():
        init.wait()
    slot = lax.rem(step, 2)
    w_up = tiles[0, slot].reshape(-1, n)
    w_down = tiles[1, slot].reshape(-1, n)
    for i in range(length // ROWS):
        at = slice(i * ROWS, (i + 1) * ROWS)
        hidden = nn(second[at], w_up)
        grad_active = nn(cot[at], w_down)
        cumulative, density = gelu_parts(hidden)
        a = (hidden * cumulative).astype(BF16)
        b = (grad_active * (cumulative + hidden * density)).astype(BF16)
        active[at] = a
        grad_hidden[at] = b
        acc[at] += nt(a, w_down)
        grad_second[at] += nt(b, w_up)
    at_steps(step, chains, FEED_PLANS[1::2])
    j, t = lax.div(step, 2), lax.rem(step, 2)
    shape = g.shape[3:]
    g[0, j, t] = nn(second_t[...], grad_hidden[...]).astype(BF16).reshape(shape)
    g[1, j, t] = nn(cot_t[...], active[...]).astype(BF16).reshape(shape)

    @pl.when(step == pl.num_programs(0) - 1)
    def _():
        start(*outs[2:])
        result[...] = acc[...].astype(BF16)
        own.start()
        follow(chains, FEED_END)
        start(*states)
        wait(*states)
        wait(*outs)
        own.wait()


def feed(second, cot, middle, whole_u, whole_d, zs):
    length, width = second.shape
    rows, n = whole_u.shape[4], FF_GROUP
    same = lambda a: jax.ShapeDtypeStruct(a.shape, a.dtype)
    tile = (2, zs, 2, 2, rows, n)
    grads = jax.ShapeDtypeStruct((2,) + tile, BF16)
    square = pltpu.VMEM((length, width), BF16)
    strip = pltpu.VMEM((length, n), BF16)
    scratch = [pltpu.VMEM((length, width), F32), square, square, strip, strip, pltpu.VMEM((2, 2) + tile[1:], BF16),
               pltpu.VMEM((2, 4) + tile, BF16), DMA((2, 2)), DMA((10,)), DMA((10, gather_sems(zs))), DMA((10, gather_sems(zs)))]
    for i in range(4):
        scratch += landing(zs, rows, n, FEED_ORDERS[i])[:FEED_DONE[i // 2]]
    return pl.pallas_call(
        functools.partial(feed_body, zs),
        grid=(8,),
        in_specs=[full(second.shape), full(cot.shape), HBM, HBM, HBM],
        out_specs=[full(second.shape), full(second.shape)] + [HBM] * 9,
        out_shape=[same(second), jax.ShapeDtypeStruct((length, width), F32), grads, grads]
        + [jax.ShapeDtypeStruct(rest_shape(zs, rows, n, o[:FEED_DONE[i // 2] - 1]), BF16) for i, o in enumerate(FEED_ORDERS)]
        + [jax.ShapeDtypeStruct((2, length // 2, width), BF16), same(whole_u), same(whole_d)],
        scratch_shapes=scratch,
        input_output_aliases={3: 9, 4: 10},
        compiler_params=params(1),
        name="feed",
    )(second, cot, middle, whole_u, whole_d)


def attend_back_step(between, gains, go, inv, query, keys, values, q_raw, k_raw, mixed, grad_q, grad_k, grad_v, grad_gains):
    length = query.shape[0]
    lanes = lax.broadcasted_iota(jnp.int32, (1, PAIR), 1)
    first = lanes < HD
    zero = jnp.zeros((), BF16)
    go = go.astype(F32)
    product = go * mixed.astype(F32) * inv
    go_inv = go * inv
    go_t = go_inv.T.astype(BF16)
    go_inv = go_inv.astype(BF16)
    query_t = query.astype(F32).T.astype(BF16)
    heads = []
    for h, mask in ((0, first), (1, ~first)):
        delta = -jnp.sum(jnp.where(mask, product, 0.0), -1, keepdims=True)
        high = delta.astype(BF16)
        low = (delta - high.astype(F32)).astype(BF16)
        spare = (1 - h) * HD
        grad_aug = jnp.where(mask, go_inv, jnp.where(lanes == spare, high, jnp.where(lanes == spare + 1, low, zero)))
        values_aug = jnp.where(mask, values, jnp.where((lanes == spare) | (lanes == spare + 1), jnp.ones((), BF16), zero))
        mine = slice(h * HD, (h + 1) * HD)
        heads.append((jnp.where(mask, keys, zero), grad_aug, values_aug, go_t[mine], query_t[mine]))
    dq = []
    dk = [jnp.zeros((HD, length), F32)] * 2
    dv = [jnp.zeros((HD, length), F32)] * 2
    for i in range(length // Q_TILE):
        if 2 * i == length // Q_TILE:
            between()
        at = slice(i * Q_TILE, (i + 1) * Q_TILE)
        parts = []
        for h, (km, ga, va, gt, qt) in enumerate(heads):
            exponent = jnp.exp(nt(query[at], km))
            grad_scores = (exponent * nt(ga[at], va)).astype(BF16)
            dv[h] = dv[h] + nn(gt[:, at], exponent.astype(BF16))
            dk[h] = dk[h] + nn(qt[:, at], grad_scores)
            parts.append(nn(grad_scores, km))
        dq.append(parts[0] + parts[1])
    dq = jnp.concatenate(dq, axis=0)
    dk = jnp.concatenate(dk, axis=0).T
    dv = jnp.concatenate(dv, axis=0).T
    grad_v[...] = dv.astype(BF16)
    matrix = head_mean_matrix(PAIR)
    hat, factor = head_stats(q_raw.astype(F32), matrix)
    scale = HD ** -0.5
    sum_q = jnp.sum(dq * hat, 0, keepdims=True) * scale
    grad_q[...] = head_back(dq * gains[0:1] * scale, hat, factor, matrix).astype(BF16)
    hat, factor = head_stats(k_raw.astype(F32), matrix)
    sum_k = jnp.sum(dk * hat, 0, keepdims=True)
    grad_k[...] = head_back(dk * gains[1:2], hat, factor, matrix).astype(BF16)
    grad_gains[...] += jnp.concatenate([sum_q, sum_k], axis=0)


def backward_body(
    zs, rows_steps, norms, gains, cot, grad_second, middle, mixed_rows, w, qn, kn, v, q_raw, k_raw, mixed, inverse,
    grads_u, grads_d, state_0, state_1, state_2, state_3, result, _outputs,
    grad_middle, grad_q, grad_k, grad_v, grad_gains, sums, shard_u, shard_d, shard_o, outputs,
    grad_mixed, acc, g_o, own_late, load_sem, swap_sem, send, recv, *landings,
):
    step = pl.program_id(0)
    p = Place(zs)
    n = FF_GROUP
    half = w.shape[2]
    at = iter(landings)
    take = lambda count: [next(at) for _ in range(count)]
    chains, loads = {}, []

    def out(k, j):
        return [((shard_u, shard_d)[k].at[:, pl.ds(j * n, n)], 0, n)]

    for i, state in enumerate((state_0, state_1, state_2, state_3)):
        j, k = divmod(i, 2)
        order = FEED_ORDERS[i]
        own = next(at)

        def held(x, z, y, own=own, gone=order[:FEED_DONE[j] - 1]):
            return own.at[tuple(index for e, index in zip("xzy", (x, z, y)) if e not in gone)]
        skip = FEED_DONE[j]
        chains[f"{'ud'[k]}{j}"] = Scatter(p, order, held, None, [None] * skip + take(4 - skip), send.at[i], recv.at[i], out(k, j))
        loads.append(pltpu.make_async_copy(state, own, load_sem.at[i]))
    for i in range(4):
        j, k = divmod(i, 2)
        grad = (grads_u, grads_d)[k].at[j]
        chains[f"{'ud'[k]}{2 + j}"] = Scatter(
            p, LATE_ORDERS[i], lambda x, z, y, i=i: own_late.at[i, x, z, y], grad.at[:, :, :, 1 - p.c], take(4),
            send.at[4 + i], recv.at[4 + i], out(k, 2 + j))
        loads.append(pltpu.make_async_copy(grad.at[:, :, :, p.c], own_late.at[i], load_sem.at[4 + i]))
    chains["o"] = Scatter(p, O_BACK_ORDER, lambda x, z, y: g_o.at[x, z, y, p.c], g_o.at[:, :, :, 1 - p.c], take(4),
                          send.at[8], recv.at[8], [(shard_o, 0, half)])
    half_length = result.shape[0] // 2
    chains["R"] = Swap(p, half_rows(result, 1 - p.x, half_length), outputs.at[p.x], swap_sem)

    @pl.when(step == 0)
    def _():
        start(*loads)
        meet(p)
        wait(*loads)
        follow(chains, BACKWARD_PLANS[0])

    at_steps(step, chains, ((),) + BACKWARD_PLANS[1:rows_steps] + BACKWARD_PLANS[rows_steps::2])

    def between():
        at_steps(step, chains, ((),) * rows_steps + BACKWARD_PLANS[rows_steps + 1::2])

    @pl.when(step == 0)
    def _():
        sums[...] = jnp.zeros_like(sums)
        acc[...] = jnp.zeros_like(acc)
        grad_gains[...] = jnp.zeros_like(grad_gains)

    @pl.when(step < rows_steps)
    def _():
        hat, factor = stats(middle[...])
        gs = grad_second[...]
        gm = cot[...].astype(F32) + back(gs * norms[1:2], hat, factor)
        grad_middle[...] = gm
        branch_grad = gm.astype(BF16)
        branch_t = branch_grad.T
        here = pl.ds(pl.multiple_of(step * ROWS, ROWS), ROWS)
        for t in range(2):
            cols = slice(t * half, (t + 1) * half)
            grad_mixed[here, cols] = nn(branch_grad, w[t]).astype(BF16)
            acc[t] += nn(branch_t, mixed_rows[:, cols])
        sums[0:1] += jnp.sum(gs * hat, 0, keepdims=True)
        sums[1:2] += jnp.sum(gs, 0, keepdims=True)

    @pl.when(step == rows_steps - 1)
    def _():
        g_o[...] = acc[...].astype(BF16).reshape(g_o.shape)

    @pl.when(step >= rows_steps)
    def _():
        cols = pl.ds(pl.multiple_of((step - rows_steps) * PAIR, PAIR), PAIR)
        attend_back_step(between, gains, grad_mixed[:, cols], inverse[...], qn[...], kn[...], v[...], q_raw[...], k_raw[...], mixed[...],
                         grad_q, grad_k, grad_v, grad_gains)

    @pl.when(step == pl.num_programs(0) - 1)
    def _():
        follow(chains, BACKWARD_END)


def backward(norms, gains, cot, grad_second, middle, mixed, w, kept, inverse, grads_u, grads_d, states, result, outputs, zs):
    length, width = middle.shape
    half = w.shape[2]
    rows, n = grads_u.shape[5], FF_GROUP
    row_steps, pairs = length // ROWS, 2 * half // PAIR
    row = clipped((ROWS, width), 0, 0, row_steps)
    head = clipped((length, PAIR), 1, row_steps, pairs)
    heads = jax.ShapeDtypeStruct((length, 2 * half), BF16)
    f32 = lambda *shape: jax.ShapeDtypeStruct(shape, F32)
    scratch = [
        pltpu.VMEM((length, 2 * half), BF16), pltpu.VMEM(w.shape, F32), pltpu.VMEM((2, zs, 2, 2, rows, half), BF16),
        pltpu.VMEM((4, 2, zs, 2, rows, n), BF16), DMA((8,)), DMA((2, CHUNKS)),
        DMA((9, scatter_sems(zs))), DMA((9, scatter_sems(zs))),
    ]
    for i in range(4):
        skip = FEED_DONE[i // 2]
        scratch += [pltpu.VMEM(rest_shape(zs, rows, n, FEED_ORDERS[i][:skip - 1]), BF16)] + landing(zs, rows, n, FEED_ORDERS[i], skip)
    for i in range(4):
        scratch += landing(zs, rows, n, LATE_ORDERS[i])
    scratch += landing(zs, rows, half, O_BACK_ORDER)
    return pl.pallas_call(
        functools.partial(backward_body, zs, row_steps),
        grid=(row_steps + pairs,),
        in_specs=[full(norms.shape), full(gains.shape), row, row, row, row, full(w.shape)] + [head] * 7 + [HBM] * 8,
        out_specs=[row, head, head, head, full((2, PAIR)), full((2, width)), full((rows, 4 * n)), full((rows, 4 * n)),
                   full((rows, half)), HBM],
        out_shape=[f32(length, width), heads, heads, heads, f32(2, PAIR), f32(2, width), f32(rows, 4 * n), f32(rows, 4 * n),
                   f32(rows, half), jax.ShapeDtypeStruct((2, length // 2, width), BF16)],
        scratch_shapes=scratch,
        input_output_aliases={21: 9},
        compiler_params=params(2),
        name="backward",
    )(norms, gains, cot, grad_second, middle, mixed, w, *kept, mixed, inverse, grads_u, grads_d, *states, result, outputs)


PART_GROUP = 256


def pieces(lo, size):
    out = []
    for part in range(3):
        first, last = max(lo, part * PART_GROUP), min(lo + size, (part + 1) * PART_GROUP)
        if first < last:
            out.append((part, first - lo, last - first))
    return out


def closing_body(
    zs, norms, sums_second, sums_qk, image_in, first_in, grad_middle_in, gq_in, gk_in, gv_in, w_in,
    shard_q, total, grad_tokens,
    image, first, grad_middle, grads, w, first_t, acc, grad_image, g, load_sem, swap_sem, got, sum_send, sum_recv, send, recv, *landings,
):
    p = Place(zs)
    meet(p)
    length, width = image.shape
    half = grads.shape[2] // 2
    load_grads = [pltpu.make_async_copy(a, grads.at[i], load_sem.at[i]) for i, a in enumerate((gq_in, gk_in, gv_in))]
    load_first = pltpu.make_async_copy(first_in, first, load_sem.at[3])
    load_w = pltpu.make_async_copy(w_in, w, load_sem.at[4])
    load_image = pltpu.make_async_copy(image_in, image, load_sem.at[5])
    load_middle = pltpu.make_async_copy(grad_middle_in, grad_middle, load_sem.at[6])
    start(load_first, *load_grads, load_w, load_image, load_middle)
    chains = {}
    at = iter(landings)
    for i, (k, lo, m, order) in enumerate(CLOSING):
        cols = pl.ds(lo, m)
        held = lambda x, z, y, k=k, cols=cols: g.at[k, x, z, y, p.c, :, cols]
        chains[i] = Scatter(p, order, held, g.at[k, :, :, :, 1 - p.c, :, cols], [next(at) for _ in range(4)], send.at[i], recv.at[i],
                            [(shard_q.at[part, :, pl.ds(k * PART_GROUP + max(lo - part * PART_GROUP, 0), n)], at0, n)
                             for part, at0, n in pieces(lo, m)])
    half_length = length // 2
    chains["G"] = Swap(p, half_rows(grad_image, 1 - p.x, half_length), grad_tokens.at[p.x], swap_sem)
    chains["S"] = Sum(p, total, got, sum_send, sum_recv)
    own = pltpu.make_async_copy(half_rows(grad_image, p.x, half_length), grad_tokens.at[p.x], load_sem.at[7])

    load_first.wait()
    first_t[...] = first[...].T
    wait(*load_grads)

    def weight_grad(k):
        def one(i, _):
            t, part = lax.div(i, 3), lax.rem(i, 3)
            cols = pl.ds(pl.multiple_of(t * half + k * PART_GROUP, PART_GROUP), PART_GROUP)
            value = nn(first_t[...], grads[part, :, cols]).astype(BF16)
            g[k, t, :, :, :, :, pl.ds(pl.multiple_of(part * PART_GROUP, PART_GROUP), PART_GROUP)] = value.reshape(
                g.shape[2:6] + (PART_GROUP,))
            return 0
        lax.fori_loop(0, 6, one, 0)

    def first_norm_back(which, carry, plan):
        here = pl.ds(pl.multiple_of(which * half_length, half_length), half_length)
        acc[...] = jnp.zeros_like(acc)

        def to_first(i, _):
            t, part = lax.div(i, 3), lax.rem(i, 3)
            cols = pl.ds(pl.multiple_of(t * half, half), half)
            acc[...] += nt(grads[part, here, cols], w[t, :, pl.ds(pl.multiple_of(part * half, half), half)])
            return 0
        lax.fori_loop(0, 6, to_first, 0)
        follow(chains, plan)

        def norm_back(i, carry):
            at = pl.ds(pl.multiple_of(which * half_length + i * ROWS, ROWS), ROWS)
            hat, factor = stats(image[at].astype(F32))
            gf = acc[pl.ds(pl.multiple_of(i * ROWS, ROWS), ROWS)]
            grad_image[at] = (grad_middle[at] + back(gf * norms[0:1], hat, factor)).astype(BF16)
            return carry[0] + jnp.sum(gf * hat, 0, keepdims=True), carry[1] + jnp.sum(gf, 0, keepdims=True)
        return lax.fori_loop(0, half_length // ROWS, norm_back, carry)

    zero = jnp.zeros((1, width), F32)
    weight_grad(0)
    follow(chains, CLOSING_PLANS[0])
    load_w.wait()
    wait(load_image, load_middle)
    sums = first_norm_back(1 - p.x, (zero, zero), CLOSING_PLANS[1])
    follow(chains, CLOSING_PLANS[2])
    weight_grad(1)
    follow(chains, CLOSING_PLANS[3])
    sum_hat, sum_all = first_norm_back(p.x, sums, CLOSING_PLANS[4])
    own.start()
    total[...] = jnp.zeros_like(total)
    total[0:1] = sum_hat
    total[1:2] = sum_all
    total[2:4] = sums_second[...]
    total[4:6, 0:HD] = sums_qk[:, :HD] + sums_qk[:, HD:]
    follow(chains, CLOSING_END)
    own.wait()


def closing(norms, sums_second, sums_qk, image, first, grad_middle, gq, gk, gv, w, zs):
    length, width = image.shape
    rows = width // (4 * zs)
    wide = 3 * PART_GROUP
    square = pltpu.VMEM((length, width), BF16)
    scratch = [
        square, square, pltpu.VMEM((length, width), F32), pltpu.VMEM((3,) + gq.shape, BF16), pltpu.VMEM(w.shape, BF16), square,
        pltpu.VMEM((length // 2, width), F32), square, pltpu.VMEM((2, 2, zs, 2, 2, rows, wide), BF16), DMA((8,)), DMA((2, CHUNKS)),
        pltpu.VMEM((zs + 2, 8, width), F32), DMA((zs + 2,)), DMA((zs + 2,)),
        DMA((len(CLOSING), scatter_sems(zs))), DMA((len(CLOSING), scatter_sems(zs))),
    ]
    for k, lo, m, order in CLOSING:
        scratch += landing(zs, rows, m, order)
    return pl.pallas_call(
        functools.partial(closing_body, zs),
        in_specs=[WHOLE_VMEM] * 3 + [HBM] * 7,
        out_specs=[WHOLE_VMEM, WHOLE_VMEM, HBM],
        out_shape=[jax.ShapeDtypeStruct((3, rows, gq.shape[1] // 2), F32), jax.ShapeDtypeStruct((8, width), F32),
                   jax.ShapeDtypeStruct((2, length // 2, width), BF16)],
        scratch_shapes=scratch,
        compiler_params=params(3),
        name="closing",
    )(norms, sums_second, sums_qk, image, first, grad_middle, gq, gk, gv, w)


def whole_images(tokens, cotangent, w_qkv, wo_t, w_up, w_down_t, norm_gains, norm_shifts, qk_gains):
    zs = lax.axis_size("fsdp") // 4
    rows = w_qkv.shape[0]
    width = tokens.shape[2]
    half = w_qkv.shape[2]
    cols = 3 * half
    first, qn, kn, v, q_raw, k_raw, mixed, inverse, middle, second, norms, image, cot, whole_q, whole_o, whole_u, whole_d = attention(
        qk_gains, norm_gains.T, norm_shifts.T, w_qkv.transpose(1, 0, 2), wo_t, w_up, w_down_t, tokens, cotangent, zs
    )
    result, grad_second, grads_u, grads_d, *states, outputs, whole_u, whole_d = feed(
        second, cot, middle, whole_u, whole_d, zs
    )
    qkv = whole_q.reshape(2, width, cols + 128)
    grad_middle, gq, gk, gv, sums_qk, sums_second, shard_u, shard_d, shard_o, outputs = backward(
        norms, jnp.tile(qk_gains.astype(F32), (1, 2)), cot, grad_second, middle, mixed, whole_o.reshape(2, width, half),
        (qn, kn, v, q_raw, k_raw), inverse, grads_u, grads_d, states, result, outputs, zs
    )
    grad_q, small, grad_tokens = closing(norms, sums_second, sums_qk, image, first, grad_middle, gq, gk, gv, qkv, zs)
    mine = lax.dynamic_slice_in_dim(small, lax.axis_index("fsdp") * rows, rows, 1)
    return (
        outputs,
        grad_tokens.astype(F32),
        grad_q.transpose(1, 0, 2),
        shard_o,
        shard_u,
        shard_d,
        jnp.stack([mine[0], mine[2]], 1),
        jnp.stack([mine[1], mine[3]], 1),
        small[4:6, :HD],
    )


def layer(tokens, *rest):
    if tokens.shape[0] == lax.axis_size("tensor") == 2 and lax.axis_size("fsdp") % 4 == 0:
        return whole_images(tokens, *rest)
    return per_device(tokens, *rest)


def solution(mesh):
    in_specs = (
        P("fsdp", "tensor", None),
        P("fsdp", "tensor", None),
        P("fsdp", None, "tensor"),
        P("fsdp", "tensor"),
        P("fsdp", "tensor"),
        P("fsdp", "tensor"),
        P("fsdp", None),
        P("fsdp", None),
        P(),
    )
    out_specs = (
        P("fsdp", "tensor", None),
        P("fsdp", "tensor", None),
        P("fsdp", None, "tensor"),
        P("fsdp", "tensor"),
        P("fsdp", "tensor"),
        P("fsdp", "tensor"),
        P("fsdp", None),
        P("fsdp", None),
        P(),
    )
    return jax.shard_map(
        layer, mesh=mesh, in_specs=in_specs, out_specs=out_specs, check_vma=False
    )
```

```python
import functools

import jax
import jax.numpy as jnp
from jax import lax
from jax.experimental import pallas as pl
from jax.experimental.pallas import tpu as pltpu
from jax.sharding import PartitionSpec as P

HD = 64


EPSILON = 1e-06


def norm_stats(value):
    center = value - jnp.mean(value, -1, keepdims=True)
    factor = lax.rsqrt(jnp.mean(center * center, -1, keepdims=True) + EPSILON)
    return (center * factor, factor)


def norm_back(grad_hat, normed, factor):
    return factor * (
        grad_hat
        - jnp.mean(grad_hat, -1, keepdims=True)
        - normed * jnp.mean(grad_hat * normed, -1, keepdims=True)
    )


def contract_rows(left, right):
    return lax.dot_general(
        left, right, (((0,), (0,)), ((), ())), preferred_element_type=jnp.float32
    )


def contract_cols(left, right):
    return lax.dot_general(
        left, right, (((1,), (1,)), ((), ())), preferred_element_type=jnp.float32
    )


def per_device(tokens, cotangent, w_qkv, wo_t, w_up, w_down_t, norm_gains, norm_shifts, qk_gains):
    local_rows = tokens.shape[1]
    width = tokens.shape[2]
    head_cols = w_qkv.shape[2]
    local_heads = head_cols // HD
    hidden_cols = w_up.shape[1]
    tensor_count = lax.axis_size("tensor")
    full_len = local_rows * tensor_count
    block = min(512, full_len)
    blocks = full_len // block
    gain_query = qk_gains[0].astype(jnp.float32)
    gain_keys = qk_gains[1].astype(jnp.float32)
    scale_query = HD ** (-0.5)

    def fetch():
        return (
            lax.all_gather(w_qkv, "fsdp", axis=0, tiled=True),
            lax.all_gather(wo_t, "fsdp", axis=0, tiled=True),
            lax.all_gather(w_up, "fsdp", axis=0, tiled=True),
            lax.all_gather(w_down_t, "fsdp", axis=0, tiled=True),
            lax.all_gather(norm_gains, "fsdp", axis=0, tiled=True),
            lax.all_gather(norm_shifts, "fsdp", axis=0, tiled=True),
        )

    def forward(weights, inputs):
        whole_qkv, whole_out, whole_up, whole_down, gains, shifts = weights
        gains = gains.astype(jnp.float32)
        shifts = shifts.astype(jnp.float32)
        flat_qkv = whole_qkv.reshape(width, 3 * head_cols)
        residual = inputs.astype(jnp.float32)
        first_hat, first_factor = norm_stats(residual)
        first = (first_hat * gains[:, 0] + shifts[:, 0]).astype(jnp.bfloat16)
        piece = lax.all_gather(first, "tensor", axis=0, tiled=True)
        first_full = piece
        joined = jnp.dot(piece, flat_qkv, preferred_element_type=jnp.float32)
        joined = joined.reshape(full_len, 3, local_heads, HD)
        query_hat, query_factor = norm_stats(joined[:, 0])
        keys_hat, keys_factor = norm_stats(joined[:, 1])
        query_n = (query_hat * gain_query * scale_query).astype(jnp.bfloat16)
        keys_n = (keys_hat * gain_keys).astype(jnp.bfloat16)
        values = joined[:, 2].astype(jnp.bfloat16)

        def attend(query_block):
            scores = jnp.einsum(
                "qhd,khd->hqk", query_block, keys_n, preferred_element_type=jnp.float32
            )
            largest = jnp.max(scores, -1, keepdims=True)
            exponent = jnp.exp(scores - largest)
            total_sum = jnp.sum(exponent, -1, keepdims=True)
            probs_low = (exponent / total_sum).astype(jnp.bfloat16)
            mixed_block = jnp.einsum(
                "hqk,khd->qhd", probs_low, values, preferred_element_type=jnp.float32
            )
            return (mixed_block.astype(jnp.bfloat16), (largest + jnp.log(total_sum))[..., 0])

        mixed, log_total = lax.map(attend, query_n.reshape(blocks, block, local_heads, HD))
        mixed = mixed.reshape(full_len, head_cols)
        middle = residual + lax.psum_scatter(
            contract_cols(mixed, whole_out), "tensor", scatter_dimension=0, tiled=True
        )
        second_hat, second_factor = norm_stats(middle)
        second = (second_hat * gains[:, 1] + shifts[:, 1]).astype(jnp.bfloat16)
        piece = lax.all_gather(second, "tensor", axis=0, tiled=True)
        hidden = jnp.dot(piece, whole_up, preferred_element_type=jnp.float32)
        active = jax.nn.gelu(hidden, approximate=False).astype(jnp.bfloat16)
        result = (
            middle
            + lax.psum_scatter(
                contract_cols(active, whole_down).astype(jnp.bfloat16),
                "tensor",
                scatter_dimension=0,
                tiled=True,
            ).astype(jnp.float32)
        ).astype(jnp.bfloat16)
        kept = (
            first_hat,
            first_factor,
            first_full,
            query_hat,
            query_factor,
            keys_hat,
            keys_factor,
            query_n,
            keys_n,
            values,
            mixed,
            log_total,
            second_hat,
            second_factor,
            piece,
            hidden,
            active,
        )
        return (kept, result)

    def backward(weights, kept, grad_out):
        whole_qkv, whole_out, whole_up, whole_down, gains, shifts = weights
        gains = gains.astype(jnp.float32)
        flat_qkv = whole_qkv.reshape(width, 3 * head_cols)
        (
            first_hat,
            first_factor,
            first_full,
            query_hat,
            query_factor,
            keys_hat,
            keys_factor,
            query_n,
            keys_n,
            values,
            mixed_keep,
            log_total,
            second_hat,
            second_factor,
            second_full,
            hidden,
            active,
        ) = kept
        piece = lax.all_gather(grad_out, "tensor", axis=0, tiled=True)
        grad_full = piece
        grad_active = jnp.dot(piece, whole_down, preferred_element_type=jnp.float32)
        grad_down = contract_rows(grad_full, active)
        unused_value, gelu_pull = jax.vjp(
            lambda value: jax.nn.gelu(value, approximate=False), hidden
        )
        grad_hidden = gelu_pull(grad_active)[0].astype(jnp.bfloat16)
        grad_up = contract_rows(second_full, grad_hidden)
        grad_second = lax.psum_scatter(
            contract_cols(grad_hidden, whole_up), "tensor", scatter_dimension=0, tiled=True
        )
        grad_middle = grad_out.astype(jnp.float32) + norm_back(
            grad_second * gains[:, 1], second_hat, second_factor
        )
        grad_branch = grad_middle.astype(jnp.bfloat16)
        piece = lax.all_gather(grad_branch, "tensor", axis=0, tiled=True)
        grad_mixed = jnp.dot(piece, whole_out, preferred_element_type=jnp.float32)
        grad_out_w = contract_rows(piece, mixed_keep)
        grad_mixed = grad_mixed.astype(jnp.bfloat16)
        grad_mixed = grad_mixed.reshape(blocks, block, local_heads, HD)

        def attend_back(carry, item):
            grad_keys_sum, grad_values_sum = carry
            query_block, grad_block, log_block = item
            scores = jnp.einsum(
                "qhd,khd->hqk", query_block, keys_n, preferred_element_type=jnp.float32
            )
            probs = jnp.exp(scores - log_block[..., None])
            grad_probs = jnp.einsum(
                "qhd,khd->hqk", grad_block, values, preferred_element_type=jnp.float32
            )
            delta = jnp.sum(probs * grad_probs, -1, keepdims=True)
            grad_scores = (probs * (grad_probs - delta)).astype(jnp.bfloat16)
            grad_query_block = jnp.einsum(
                "hqk,khd->qhd", grad_scores, keys_n, preferred_element_type=jnp.float32
            )
            grad_keys_sum = grad_keys_sum + jnp.einsum(
                "hqk,qhd->khd", grad_scores, query_block, preferred_element_type=jnp.float32
            )
            grad_values_sum = grad_values_sum + jnp.einsum(
                "hqk,qhd->khd",
                probs.astype(jnp.bfloat16),
                grad_block,
                preferred_element_type=jnp.float32,
            )
            return ((grad_keys_sum, grad_values_sum), grad_query_block)

        empty_heads = jnp.zeros((full_len, local_heads, HD), jnp.float32)
        (grad_keys_n, grad_values), grad_query_n = lax.scan(
            attend_back,
            (empty_heads, empty_heads),
            (query_n.reshape(blocks, block, local_heads, HD), grad_mixed, log_total),
        )
        grad_query_n = grad_query_n.reshape(full_len, local_heads, HD)
        grad_query = norm_back(grad_query_n * gain_query * scale_query, query_hat, query_factor)
        grad_keys = norm_back(grad_keys_n * gain_keys, keys_hat, keys_factor)
        qk_grad = jnp.stack(
            [
                jnp.sum(grad_query_n * query_hat * scale_query, (0, 1)),
                jnp.sum(grad_keys_n * keys_hat, (0, 1)),
            ]
        )
        grad_joined = jnp.stack([grad_query, grad_keys, grad_values], 1).astype(jnp.bfloat16)
        grad_joined = grad_joined.reshape(full_len, 3 * head_cols)
        grad_qkv = contract_rows(first_full, grad_joined).reshape(width, 3, head_cols)
        grad_first = lax.psum_scatter(
            contract_cols(grad_joined, flat_qkv).astype(jnp.bfloat16),
            "tensor",
            scatter_dimension=0,
            tiled=True,
        ).astype(jnp.float32)
        grad_input = grad_middle + norm_back(grad_first * gains[:, 0], first_hat, first_factor)
        gain_grad = jnp.stack(
            [jnp.sum(grad_first * first_hat, 0), jnp.sum(grad_second * second_hat, 0)], 1
        )
        shift_grad = jnp.stack([jnp.sum(grad_first, 0), jnp.sum(grad_second, 0)], 1)
        return (
            (grad_qkv, grad_out_w, grad_up, grad_down, gain_grad, shift_grad, qk_grad),
            grad_input,
        )

    def micro_step(totals, item):
        inputs, grad_out = item
        forward_weights = fetch()
        kept, result = forward(forward_weights, inputs)
        backward_weights = fetch()
        grads, grad_input = backward(backward_weights, kept, grad_out)
        totals = tuple((total + part for total, part in zip(totals, grads)))
        return (totals, (result, grad_input))

    out_cols_count = wo_t.shape[1]
    start_sums = (
        jnp.zeros((width, 3, head_cols), jnp.float32),
        jnp.zeros((width, out_cols_count), jnp.float32),
        jnp.zeros((width, hidden_cols), jnp.float32),
        jnp.zeros((width, hidden_cols), jnp.float32),
        jnp.zeros((width, 2), jnp.float32),
        jnp.zeros((width, 2), jnp.float32),
        jnp.zeros((2, HD), jnp.float32),
    )
    totals, (outputs, grad_tokens) = lax.scan(micro_step, start_sums, (tokens, cotangent))
    out_total = totals[1]
    grad_qkv, grad_out_w, grad_up, grad_down = (
        lax.psum_scatter(
            totals[0].astype(jnp.bfloat16), "fsdp", scatter_dimension=0, tiled=True
        ).astype(jnp.float32),
        lax.psum_scatter(
            out_total.astype(jnp.bfloat16), "fsdp", scatter_dimension=0, tiled=True
        ).astype(jnp.float32),
        lax.psum_scatter(
            totals[2].astype(jnp.bfloat16), "fsdp", scatter_dimension=0, tiled=True
        ).astype(jnp.float32),
        lax.psum_scatter(
            totals[3].astype(jnp.bfloat16), "fsdp", scatter_dimension=0, tiled=True
        ).astype(jnp.float32),
    )
    gain_total, shift_total, qk_total = lax.psum(
        (totals[4], totals[5], totals[6]), ("fsdp", "tensor")
    )
    own_rows = width // lax.axis_size("fsdp")
    offset = lax.axis_index("fsdp") * own_rows
    gain_part = lax.dynamic_slice_in_dim(gain_total, offset, own_rows, 0)
    shift_part = lax.dynamic_slice_in_dim(shift_total, offset, own_rows, 0)
    return (
        outputs,
        grad_tokens,
        grad_qkv,
        grad_out_w,
        grad_up,
        grad_down,
        gain_part,
        shift_part,
        qk_total,
    )


PAIR = 2 * HD
F32, BF16 = jnp.float32, jnp.bfloat16
LIMIT = 60 << 20


def nn(a, b):
    return lax.dot_general(a, b, (((1,), (0,)), ((), ())), preferred_element_type=F32)


def nt(a, b):
    return lax.dot_general(a, b, (((1,), (1,)), ((), ())), preferred_element_type=F32)


def stats(value):
    center = value - jnp.mean(value, -1, keepdims=True)
    factor = lax.rsqrt(jnp.mean(center * center, -1, keepdims=True) + EPSILON)
    return center * factor, factor


def back(grad_hat, normed, factor):
    return factor * (
        grad_hat
        - jnp.mean(grad_hat, -1, keepdims=True)
        - normed * jnp.mean(grad_hat * normed, -1, keepdims=True)
    )


def head_mean_matrix(width):
    row = lax.broadcasted_iota(jnp.int32, (width, width), 0) // HD
    col = lax.broadcasted_iota(jnp.int32, (width, width), 1) // HD
    return jnp.where(row == col, 1.0 / HD, 0.0).astype(BF16)


def head_mean(value, matrix):
    high = value.astype(BF16)
    low = (value - high.astype(F32)).astype(BF16)
    return nn(high, matrix) + nn(low, matrix)


def head_stats(value, matrix):
    center = value - head_mean(value, matrix)
    factor = lax.rsqrt(head_mean(center * center, matrix) + EPSILON)
    return center * factor, factor


def head_back(grad_hat, normed, factor, matrix):
    return factor * (
        grad_hat - head_mean(grad_hat, matrix) - normed * head_mean(grad_hat * normed, matrix)
    )


MESH = pl.DeviceIdType.MESH
ALL = slice(None)


class Place:
    def __init__(self, zs):
        f = lax.axis_index("fsdp")
        self.zs = zs
        self.x = lax.axis_index("tensor")
        self.c = lax.rem(f, 2)
        self.y = lax.rem(lax.div(f, 2), 2)
        self.z = lax.div(f, 4)

    def dev(self, z=None, y=None, c=None, x=None):
        z = self.z if z is None else z
        y = self.y if y is None else y
        c = self.c if c is None else c
        x = self.x if x is None else x
        return {"fsdp": (z * 2 + y) * 2 + c, "tensor": x}

    def along_z(self):
        return [lax.rem(self.z + k, self.zs) for k in range(1, self.zs)]

    def peers(self):
        out = [self.dev(z=z) for z in self.along_z()]
        return out + [self.dev(y=1 - self.y), self.dev(c=1 - self.c), self.dev(x=1 - self.x)]


def meet(place):
    barrier = pltpu.get_barrier_semaphore()
    peers = place.peers()
    for peer in peers:
        pl.semaphore_signal(barrier, inc=1, device_id=peer, device_id_type=MESH)
    pl.semaphore_wait(barrier, len(peers))


def remote(src, dst, send, recv, peer):
    return pltpu.make_async_remote_copy(
        src_ref=src, dst_ref=dst, send_sem=send, recv_sem=recv, device_id=peer, device_id_type=MESH
    )


def start(*copies):
    for copy in copies:
        copy.start()


def wait(*copies):
    for copy in copies:
        copy.wait()


class Gather:
    def __init__(self, place, shard, whole, lo, size, order, send, recv, since=0):
        p = self.p = place
        cols = self.cols = pl.ds(lo, size)
        self.shard = None if shard is None else shard.at[:, cols]
        self.whole = whole
        self.order, self.since = order, since
        self.send, self.recv = send, recv
        if shard is not None:
            self.own = pltpu.make_async_copy(self.shard, self.at({}), self.send.at[2 * p.zs + 7])

    def at(self, index):
        p = self.p
        own = {"x": p.x, "y": p.y, "z": p.z}
        x, y, z = (index.get(d, own[d]) for d in "xyz")
        return self.whole.at[x, z, y, p.c, :, self.cols]

    def others(self, d):
        return self.p.along_z() if d == "z" else [1 - getattr(self.p, d)]

    def copies(self, base, i, pairs):
        base += sum(len(self.others(d)) for d in self.order[:i])
        return [remote(src, dst, self.send.at[base + k], self.recv.at[base + k], peer) for k, (src, dst, peer) in enumerate(pairs)]

    def stage(self, i):
        d = self.order[i]
        held = self.at({e: ALL for e in self.order[:i]})
        src = self.shard if i == 0 and self.shard is not None else held
        return self.copies(0, i, [(src, held, self.p.dev(**{d: to})) for to in self.others(d)])

    def core_parts(self, i):
        done = {e: ALL for e in self.order[:i]}
        d = self.order[i]
        if i == 0:
            refs = [self.at({d: ALL})]
        else:
            refs = [self.at({**done, d: to}) for to in self.others(d)]
        peer = self.p.dev(c=1 - self.p.c)
        return self.copies(self.p.zs + 1, i, [(ref, ref, peer) for ref in refs])

    def start(self, i):
        if i == 0 and self.shard is not None:
            self.own.start()
        if i < 3:
            start(*self.stage(i))
        if i > 0:
            start(*self.core_parts(i - 1))

    def done(self, i):
        if i == 0 and self.shard is not None:
            self.own.wait()
        if i < 3:
            wait(*self.stage(i))
        else:
            self.rest(self.since - 1 if self.since else 0, 3)

    def rest(self, lo, hi):
        for i in range(lo, hi):
            wait(*self.core_parts(i))


def gather_sems(zs):
    return 2 * zs + 8


CHUNKS = 4


class Swap:
    def __init__(self, place, src, dst, sems):
        rows = src.shape[0] // CHUNKS
        part = lambda ref, i: ref.at[pl.ds(i * rows, rows)]
        self.copies = [remote(part(src, i), part(dst, i), sems.at[0, i], sems.at[1, i], place.dev(x=1 - place.x)) for i in range(CHUNKS)]

    def start(self, i):
        self.copies[i].start()

    def done(self, i):
        self.copies[i].wait()


def half_rows(ref, which, rows):
    return ref.at[pl.ds(pl.multiple_of(which * rows, rows), rows)]


class Sum:
    def __init__(self, place, total, got, send, recv):
        self.p, self.total, self.got, self.send, self.recv = place, total, got, send, recv

    def copies(self, i):
        p = self.p
        if i < 3:
            peers = [(p.dev(c=1 - p.c), p.dev(x=1 - p.x), p.dev(y=1 - p.y))[i]]
        else:
            peers = [p.dev(z=z) for z in p.along_z()]
        return [remote(self.total, self.got.at[i + k], self.send.at[i + k], self.recv.at[i + k], peer)
                for k, peer in enumerate(peers)]

    def start(self, i):
        start(*self.copies(i))

    def done(self, i):
        copies = self.copies(i)
        wait(*copies)
        total = self.total[...]
        for k in range(len(copies)):
            total = total + self.got[i + k]
        self.total[...] = total


def add_slabs(count, pair):
    def body(i, _):
        into, from_ = pair(i)
        into[...] = into[...] + from_[...]
        return 0
    lax.fori_loop(0, count, body, 0)


class Scatter:
    def __init__(self, place, order, held, away, landings, send, recv, out=None):
        self.p, self.order, self.held, self.away = place, order, held, away
        self.landings, self.send, self.recv, self.out = landings, send, recv, out

    def size(self, d):
        return self.p.zs if d == "z" else 2

    def others(self, d):
        return self.p.along_z() if d == "z" else [1 - getattr(self.p, d)]

    def part(self, i, value, rest=None):
        at = {e: ALL for e in "xzy"}
        at.update(rest or {})
        at.update({e: getattr(self.p, e) for e in self.order[:i]})
        at[self.order[i]] = value
        return self.held(at["x"], at["z"], at["y"])

    def copies(self, i):
        p = self.p
        if i == 0:
            return [remote(self.away, self.landings[0], self.send.at[0], self.recv.at[0], p.dev(c=1 - p.c))]
        d = self.order[i - 1]
        base = 1 + sum(len(self.others(e)) for e in self.order[:i - 1])
        return [remote(self.part(i - 1, to), self.landings[i].at[k], self.send.at[base + k], self.recv.at[base + k], p.dev(**{d: to}))
                for k, to in enumerate(self.others(d))]

    def start(self, i):
        start(*self.copies(i))

    def done(self, i):
        p = self.p
        wait(*self.copies(i))
        if i == 3:
            value = self.part(2, getattr(p, self.order[2]))[...].astype(F32)
            for k in range(len(self.others(self.order[2]))):
                value = value + self.landings[3][k].astype(F32)
            for ref, lo, size in self.out:
                ref[...] = value[:, lo:lo + size]
            return
        dims = [e for e in "xzy" if e not in self.order[:i]]
        walked = [e for e in dims if e != "z"]

        def body(j, _):
            at, left = {"z": ALL}, j
            for e in reversed(walked):
                at[e] = lax.rem(left, 2)
                left = lax.div(left, 2)
            index = tuple(at[e] for e in dims)
            if i == 0:
                into, froms = self.held(at["x"], at["z"], at["y"]), [self.landings[0].at[index]]
            else:
                d = self.order[i - 1]
                into = self.part(i - 1, getattr(p, d), {e: at[e] for e in dims})
                froms = [self.landings[i].at[(k,) + index] for k in range(len(self.others(d)))]
            value = into[...]
            if len(froms) == 1:
                value = value + froms[0][...]
            else:
                value = value.astype(F32)
                for from_ in froms:
                    value = value + from_[...].astype(F32)
                value = value.astype(BF16)
            into[...] = value
            return 0
        lax.fori_loop(0, 2 ** len(walked), body, 0)

    def state(self, stages):
        return self.part(stages - 2, getattr(self.p, self.order[stages - 2]))


def scatter_sems(zs):
    return zs + 2


def rest_shape(zs, rows, m, gone):
    size = {"x": 2, "z": zs, "y": 2}
    return tuple(size[e] for e in "xzy" if e not in gone) + (rows, m)


def landing(zs, rows, m, order, since=0):
    shapes = [rest_shape(zs, rows, m, "")]
    for i, d in enumerate(order):
        shapes.append((zs - 1 if d == "z" else 1,) + rest_shape(zs, rows, m, order[:i + 1]))
    return [pltpu.VMEM(shape, BF16) for shape in shapes[since:]]


def follow(chains, plan):
    for name, i in plan:
        if i < 0:
            chains[name].start(-1 - i)
        else:
            chains[name].done(i)


def at_steps(step, chains, plans):
    for at, plan in enumerate(plans):
        if plan:
            pl.when(step == at)(functools.partial(follow, chains, plan))


def on(step, hooks):
    for at, hook in hooks.items():
        pl.when(step == at)(hook)


HBM = pl.BlockSpec(memory_space=pl.ANY)
WHOLE_VMEM = pl.BlockSpec(memory_space=pltpu.VMEM)
DMA = pltpu.SemaphoreType.DMA


def params(collective_id):
    return pltpu.CompilerParams(collective_id=collective_id, has_side_effects=True, vmem_limit_bytes=LIMIT)


Q_ORDERS = ('zyx', 'xzy', 'zxy', 'xzy', 'zyx', 'zxy', 'xzy')
O_ORDER = 'zxy'
U_ORDERS = ('xyz', 'zyx', 'zxy', 'xzy')
D_ORDERS = ('xzy', 'xzy', 'yzx', 'yzx')
FEED_SINCE = (3, 1, 0)
FEED_ORDERS = ('zyx', 'xyz', 'yzx', 'xyz')
FEED_DONE = (2, 2)
LATE_ORDERS = ('zyx', 'yxz', 'xyz', 'xyz')
O_BACK_ORDER = 'yzx'
CLOSING = ((0, 0, 256, 'zyx'), (0, 256, 256, 'xyz'), (0, 512, 256, 'yxz'), (1, 0, 256, 'yxz'), (1, 256, 256, 'yxz'), (1, 512, 256, 'zyx'))
ATTENTION_LEAVES = (('U1', 3), ('D1', 3), ('U2', 1), ('D2', 1), ('U3', 0), ('D3', 0))
OPENING_PLANS = (
    ((6, -1), ('T', -1), (0, -1), (2, -1), ('D2', -1), (6, 0), (1, -1), ('D2', 0), (1, 0), (3, -1), (0, 0), (6, -2), (0, -2), (2, 0), (1, -2), ('T', 0), ('T', -2), (3, 0), (2, -2), (0, 1), (6, 1), (6, -3), (3, -2), (2, 1), (0, -3), (2, -3), (1, 1), (4, -1), ('T', 1), ('T', -3), (6, 2), (6, -4), (1, -3), (6, 3),),
    ((3, 1), (5, -1), (4, 0), ('O', -1), (2, 2), (2, -4), (3, -3), (0, 2), (0, -4), ('U0', -1), ('T', 2), ('T', -4), (2, 3), (1, 2), (1, -4), (4, -2), (0, 3), ('U0', 0), ('D0', -1), (5, 0), ('U1', -1), (1, 3), ('D0', 0), (5, -2), ('O', 0), ('D0', -2), (3, 2), (3, -4), ('U0', -2), (4, 1), ('T', 3), (4, -3),),
)
ATTENTION_PLANS = (
    ((3, 3), (5, 1), (5, -3), ('O', -2),),
    (('U0', 1),),
    (('U1', 0), ('U0', -3), ('U1', -2),),
    (),
    (),
    (),
    ((4, 2), (4, -4), ('D1', -1), (5, 2), (5, -4),),
    (('O', 1), ('O', -3), ('C', -1), ('U1', 1), (4, 3), ('D1', 0), ('U1', -3), (5, 3),),
    (('D0', 1), ('D0', -3), ('D1', -2),),
    (),
    (),
    (),
    (('C', 0), ('C', -2),),
    (),
    (),
    (),
    (('O', 2), ('O', -4), ('U1', 2),),
    (('D0', 2), ('D0', -4), ('C', 1), ('C', -3),),
    (('O', 3), ('D1', 1), ('D1', -3), ('U2', -1),),
    (('D0', 3),),
    (('U0', 2), ('U0', -4), ('C', 2), ('C', -4),),
    (),
    (('U2', 0),),
    (('U0', 3),),
)
ATTENTION_END = (('C', 3), ('D1', 2),)
FEED_PLANS = (
    (('U1', -4), ('D1', -4), ('U2', -2), ('D2', -2), ('U3', -1), ('D3', -1),),
    (('D3', 0), ('D3', -2), ('U3', 0), ('U1', 3), ('D1', 3), ('U2', 1), ('U2', -3),),
    (),
    (('D2', 1), ('D2', -3), ('U3', -2),),
    (('u0', -1), ('d0', -1),),
    (('U2', 2), ('U2', -4),),
    (('D3', 1), ('D3', -3),),
    (('u0', 0), ('u0', -2), ('d0', 0), ('D2', 2), ('D2', -4), ('d0', -2), ('U2', 3), ('U3', 1), ('U3', -3),),
    (('u1', -1), ('d1', -1), ('D2', 3),),
    (),
    (('D3', 2), ('D3', -4), ('u1', 0), ('u1', -2), ('d1', 0), ('d1', -2),),
    (('U3', 2), ('U3', -4), ('D3', 3),),
    (('d0', 1), ('U3', 3),),
    (('u0', 1), ('u1', 1),),
    (('d1', 1),),
    (),
)
FEED_END = ()
BACKWARD_PLANS = (
    (('u0', -3), ('d0', -3), ('u1', -3), ('u2', -1), ('d2', -1), ('u3', -1), ('d3', -1), ('R', -1),),
    (),
    (),
    (('u0', 2), ('u0', -4), ('d1', -3), ('R', 0), ('R', -2), ('d0', 2), ('d0', -4),),
    (('u1', 2),),
    (('u0', 3), ('u1', -4), ('u2', 0), ('u2', -2), ('o', -1), ('d2', 0), ('d2', -2), ('u3', 0), ('d3', 0), ('d1', 2), ('d1', -4), ('d0', 3), ('R', 1), ('u3', -2),),
    (('u1', 3), ('d3', -2), ('o', 0), ('o', -2),),
    (),
    (),
    (('d1', 3),),
    (('d2', 1),),
    (('u3', 1), ('d2', -3), ('u3', -3),),
    (('o', 1), ('o', -3), ('d3', 1), ('d3', -3), ('R', -3),),
    (('u2', 1),),
    (('u3', 2), ('u2', -3), ('u3', -4), ('d2', 2), ('d2', -4),),
    (('d3', 2), ('R', 2), ('R', -4),),
    (('u2', 2), ('u2', -4),),
    (),
    (('o', 2), ('d3', -4), ('u2', 3), ('o', -4), ('R', 3),),
    (('u3', 3), ('d2', 3), ('o', 3),),
)
BACKWARD_END = (('d3', 3),)
CLOSING_PLANS = (
    ((0, -1), (1, -1), (2, -1),),
    (),
    (('G', -1),),
    ((3, -1), (0, 0), (0, -2), (4, -1), (1, 0), (1, -2), (5, -1), (2, 0), (2, -2),),
    (('G', 0), ('G', -2),),
)
CLOSING_END = (('S', -1), (3, 0), (3, -2), (4, 0), (5, 0), (5, -2), (2, 1), (4, -2), ('S', 0), (1, 1), ('S', -2), ('S', 1), (2, -3), ('G', 1), ('G', -3), (0, 1), (3, 1), ('S', -3), (4, 1), (0, -3), (2, 2), (2, -4), (3, -3), ('S', 2), ('S', -4), (1, -3), (0, 2), (5, 1), (5, -3), ('G', 2), (0, -4), (3, 2), (3, -4), (4, -3), (1, 2), (2, 3), (1, -4), (0, 3), ('G', -4), (5, 2), ('S', 3), (4, 2), (4, -4), (5, -4), (3, 3), (1, 3), (5, 3), (4, 3), ('G', 3),)


Q_TILE = 256
ATTEND_TILE = 512
ROWS = 256
FF_GROUP = 512


def full(shape):
    return pl.BlockSpec(shape, lambda s: (0,) * len(shape), pipeline_mode=pl.Buffered(1))


def clipped(shape, axis, first, count):
    def at(s):
        i = jnp.clip(s - first, 0, count - 1)
        return (i, 0) if axis == 0 else (0, i)
    return pl.BlockSpec(shape, at)


def tile_of(part, s):
    i = jnp.clip(s - 4 * part, 0, 3)
    column = lax.div(i, 2)
    return lax.rem(i, 2) * 2 + (1 - column if part == 0 else column)


def project_step(step, joined, gains, kept, blocks):
    tile = joined.shape[1]
    qn_s, kn_s, v_s = kept
    qn, kn, v, q_raw, k_raw = blocks
    matrix = head_mean_matrix(tile)

    def cols(part):
        return pl.ds(pl.multiple_of(tile_of(part, step) * tile, tile), tile)

    @pl.when(step < 4)
    def _():
        value = joined.astype(BF16)
        v[...] = value
        v_s[:, cols(0)] = value

    @pl.when((step >= 4) & (step < 8))
    def _():
        hat, _f = head_stats(joined, matrix)
        value = (hat * gains[1:2]).astype(BF16)
        kn[...] = value
        kn_s[:, cols(1)] = value
        k_raw[...] = joined.astype(BF16)

    @pl.when(step >= 8)
    def _():
        hat, _f = head_stats(joined, matrix)
        value = (hat * gains[0:1] * (HD ** -0.5)).astype(BF16)
        qn[...] = value
        qn_s[:, cols(2)] = value
        q_raw[...] = joined.astype(BF16)


def attend_step(query_all, keys, values, mixed_s, cols, mixed, inverse):
    length = keys.shape[0]
    lane = lax.broadcasted_iota(jnp.int32, (1, PAIR), 1) < HD
    zero = jnp.zeros((), BF16)
    values_t = values.astype(F32).T.astype(BF16)
    ones = jnp.ones((16, length), BF16)
    heads = [(jnp.where(mask, keys, zero), jnp.concatenate([values_t[h * HD:(h + 1) * HD], ones], axis=0))
             for h, mask in ((0, lane), (1, ~lane))]
    for i in range(length // ATTEND_TILE):
        at = slice(i * ATTEND_TILE, (i + 1) * ATTEND_TILE)
        query = query_all[at]
        got, inv = [], []
        for keys_h, values_h in heads:
            both = nn(values_h, jnp.exp(nt(keys_h, query)).astype(BF16))
            one_over = 1.0 / both[HD:HD + 1]
            got.append(both[:HD] * one_over)
            inv.append(jnp.broadcast_to(one_over, (HD, ATTEND_TILE)))
        value = jnp.concatenate(got, axis=0).T.astype(BF16)
        mixed[at] = value
        mixed_s[at, cols] = value
        inverse[at] = jnp.concatenate(inv, axis=0).T


PROJECT_STEPS = 12


def first_after(plans, name):
    return max([at for at, plan in enumerate(plans) if (name, 3) in plan], default=0)


def attention_body(
    zs, pairs, qk_gains, norm_gains, norm_shifts, q_in, o_in, u_in, d_in, tokens, cot_in,
    first, qn, kn, v, q_raw, k_raw, mixed, inverse, middle, second, norms, image, cot, whole_q, whole_o, whole_u, whole_d,
    image_v, qn_s, kn_s, v_s, mixed_s, out_w, tiles, q_v, o_v, u_v, d_v, cot_v, side_v, turn, local_sem, send, recv, swap_sem,
):
    step = pl.program_id(0)
    p = Place(zs)
    length = image_v.shape[0]
    half, rows = whole_o.shape[5], whole_o.shape[4]
    tile = half // 2
    head0, row0 = PROJECT_STEPS, PROJECT_STEPS + pairs
    n = FF_GROUP
    mine = pl.ds(pl.multiple_of(p.x * (length // 2), length // 2), length // 2)
    chains = {
        "T": Swap(p, tokens.at[1 - p.x], half_rows(image_v, p.x, length // 2), swap_sem.at[0]),
        "C": Swap(p, cot_in.at[1 - p.x], half_rows(cot, p.x, length // 2), swap_sem.at[1]),
    }
    local = lambda i, src, dst: pltpu.make_async_copy(src, dst, local_sem.at[i])
    own_shards = [local(i, a, b) for i, (a, b) in enumerate(((o_in, o_v), (u_in, u_v), (d_in, d_v)))]
    own_shards += [local(i, q_in.at[k], q_v.at[:, pl.ds(k * half, half)]) for i, k in ((3, 0), (12, 1), (13, 2))]
    own_tokens = local(4, tokens.at[p.x], image_v.at[mine])
    own_cot = [local(5, cot_in.at[p.x], cot_v), local(6, cot_v, cot.at[mine])]
    keep_image = local(7, image_v, image)
    side = local(8, whole_q.at[0, :, :, :, :, pl.ds(3 * half, PAIR)], side_v)
    load_out = local(9, whole_o, out_w)
    starts = (2 * half + tile, 2 * half, half, half + tile, 0, tile)
    for i, lo in enumerate(starts):
        chains[i] = Gather(p, q_v, whole_q, lo, tile, Q_ORDERS[i], send.at[i], recv.at[i])
    chains[6] = Gather(p, q_v, whole_q, 3 * half, PAIR, Q_ORDERS[6], send.at[15], recv.at[15])

    def load_tile(i):
        return local(10 + i % 2, whole_q.at[:, :, :, :, :, pl.ds(starts[i], tile)], tiles.at[i % 2])

    chains["O"] = Gather(p, o_v, whole_o, 0, half, O_ORDER, send.at[6], recv.at[6])
    for j in range(4):
        chains[f"U{j}"] = Gather(p, u_v, whole_u, j * n, n, U_ORDERS[j], send.at[7 + j], recv.at[7 + j])
        chains[f"D{j}"] = Gather(p, d_v, whole_d, j * n, n, D_ORDERS[j], send.at[11 + j], recv.at[11 + j])

    @pl.when(step == 0)
    def _():
        start(*own_shards, own_tokens, own_cot[0])
        turn[...] = jnp.zeros_like(turn)
        turn[0:2, 0:rows] = norm_gains[...].astype(F32)
        turn[2:4, 0:rows] = norm_shifts[...].astype(F32)
        q_v[:, 3 * half:] = turn[...].T[:rows].astype(BF16)
        meet(p)
        wait(*own_shards)
        for name, stages in ATTENTION_LEAVES:
            if stages == 0:
                chains[name].own.start()

        def norm(which):
            def rows_norm(i, _):
                at = pl.ds(pl.multiple_of(which * (length // 2) + i * ROWS, ROWS), ROWS)
                hat, _f = stats(image_v[at].astype(F32))
                first[at] = (hat * norms[0:1] + norms[2:3]).astype(BF16)
                return 0
            lax.fori_loop(0, length // 2 // ROWS, rows_norm, 0)

        follow(chains, OPENING_PLANS[0])
        side.start()
        own_cot[0].wait()
        own_cot[1].start()
        side.wait()
        norms[...] = side_v[...].reshape(-1, PAIR).astype(F32).T[:8]
        own_tokens.wait()
        norm(p.x)
        follow(chains, OPENING_PLANS[1])
        load_tile(0).start()
        keep_image.start()
        norm(1 - p.x)

    at_steps(step, chains, ATTENTION_PLANS)

    on(step, {0: lambda: load_tile(0).wait()})
    for i in range(1, 6):
        on(step, {max(2 * i - 2, first_after(ATTENTION_PLANS, i)): lambda i=i: load_tile(i).start()})
        on(step, {2 * i: lambda i=i: load_tile(i).wait()})
    on(step, {max(1, first_after(ATTENTION_PLANS, "O")): lambda: load_out.start()})
    on(step, {row0: lambda: load_out.wait()})

    @pl.when(step < head0)
    def _():
        gains = qk_gains[...].astype(F32)
        gains = jnp.concatenate([gains] * (tile // HD), axis=1)
        w = tiles[lax.rem(lax.div(step, 2), 2), lax.rem(step, 2)].reshape(-1, tile)
        project_step(step, nn(first[...], w), gains, (qn_s, kn_s, v_s), (qn, kn, v, q_raw, k_raw))

    @pl.when((step >= head0) & (step < row0))
    def _():
        cols = pl.ds(pl.multiple_of((step - head0) * PAIR, PAIR), PAIR)
        attend_step(qn_s[:, cols], kn_s[:, cols], v_s[:, cols], mixed_s, cols, mixed, inverse)

    @pl.when(step >= row0)
    def _():
        at = pl.ds(pl.multiple_of((step - row0) * ROWS, ROWS), ROWS)
        w0, w1 = (out_w[t].reshape(-1, half) for t in range(2))
        value = image_v[at].astype(F32) + nt(mixed_s[at, :half], w0) + nt(mixed_s[at, half:], w1)
        middle[...] = value
        hat, _f = stats(value)
        second[...] = (hat * norms[1:2] + norms[3:4]).astype(BF16)

    @pl.when(step == pl.num_programs(0) - 1)
    def _():
        follow(chains, ATTENTION_END)
        for name, stages in ATTENTION_LEAVES:
            chains[name].rest(0, stages - 1)
            if stages == 0:
                chains[name].own.wait()
        wait(own_cot[1], keep_image)


def attention(qk_gains, norm_gains, norm_shifts, q, o, u, d, tokens, cot, zs):
    rows = o.shape[0]
    length, width = 2 * tokens.shape[1], tokens.shape[2]
    half = o.shape[1]
    pairs = 2 * half // PAIR
    head0, row0 = PROJECT_STEPS, PROJECT_STEPS + pairs
    tile = half // 2
    tiles = lambda part: pl.BlockSpec((length, tile), lambda s: (0, tile_of(part, s)))
    heads = clipped((length, PAIR), 1, head0, pairs)
    by_rows = clipped((ROWS, width), 0, row0, length // ROWS)
    bf = jax.ShapeDtypeStruct((length, 2 * half), BF16)
    square = jax.ShapeDtypeStruct((length, width), BF16)
    f32 = lambda *shape: jax.ShapeDtypeStruct(shape, F32)
    whole = lambda n: jax.ShapeDtypeStruct((2, zs, 2, 2, rows, n), BF16)
    store = pltpu.VMEM((length, 2 * half), BF16)
    wide = lambda n: pltpu.VMEM((rows, n), BF16)
    return pl.pallas_call(
        functools.partial(attention_body, zs, pairs),
        grid=(row0 + length // ROWS,),
        in_specs=[full(qk_gains.shape), full(norm_gains.shape), full(norm_shifts.shape)] + [HBM] * 6,
        out_specs=[full((length, width)), tiles(2), tiles(1), tiles(0), tiles(2), tiles(1), heads, heads, by_rows, by_rows,
                   full((8, width))] + [HBM] * 6,
        out_shape=[square, bf, bf, bf, bf, bf, bf, f32(length, 2 * half), f32(length, width), square, f32(8, width),
                   square, square, whole(3 * half + PAIR), whole(half), whole(u.shape[1]), whole(d.shape[1])],
        scratch_shapes=[pltpu.VMEM((length, width), BF16), store, store, store, store, pltpu.VMEM((2, zs, 2, 2, rows, half), BF16),
                        pltpu.VMEM((2, 2, zs, 2, 2, rows, tile), BF16), wide(3 * half + PAIR), wide(half), wide(u.shape[1]), wide(d.shape[1]),
                        pltpu.VMEM((length // 2, width), BF16), pltpu.VMEM((zs, 2, 2, rows, PAIR), BF16),
                        pltpu.VMEM((PAIR, PAIR), F32), DMA((14,)), DMA((16, gather_sems(zs))), DMA((16, gather_sems(zs))), DMA((2, 2, CHUNKS))],
        compiler_params=params(0),
        name="attention",
    )(qk_gains, norm_gains, norm_shifts, q, o, u, d, tokens, cot)


def gelu_parts(v):
    bell = jnp.exp(v * v * -0.5)
    t = 1.0 / (1.0 + (0.3275911 * 0.7071067811865476) * jnp.abs(v))
    poly = t * (0.127414796 + t * (-0.142248368 + t * (0.7107068705 + t * (-0.7265760135 + t * 0.5307027145))))
    tail = poly * bell
    return jnp.where(v >= 0, 1.0 - tail, tail), bell * 0.3989422804014327


def feed_body(
    zs, second, cot, middle, _u, _d,
    result, grad_second, grad_u, grad_d, state_0, state_1, state_2, state_3, outputs, whole_u, whole_d,
    acc, second_t, cot_t, active, grad_hidden, tiles, g, tile_sem, misc_sem, send, recv, *landings,
):
    step = pl.program_id(0)
    p = Place(zs)
    length = second.shape[0]
    n = FF_GROUP
    state_refs = (state_0, state_1, state_2, state_3)
    chains = {}
    for j in (1, 2, 3):
        for i, (name, w, orders) in enumerate((("U", whole_u, U_ORDERS), ("D", whole_d, D_ORDERS))):
            k = 2 * j - 2 + i
            chains[f"{name}{j}"] = Gather(p, None, w, j * n, n, orders[j], send.at[k], recv.at[k], FEED_SINCE[j - 1])
    at, states = iter(landings), []
    for j in range(2):
        for k in range(2):
            i = 2 * j + k
            held = lambda x, z, y, j=j, k=k: g.at[k, j, x, z, y, p.c]
            s = Scatter(p, FEED_ORDERS[i], held, g.at[k, j, :, :, :, 1 - p.c], [next(at) for _ in range(FEED_DONE[j])], send.at[6 + i], recv.at[6 + i])
            chains[f"{'ud'[k]}{j}"] = s
            states.append(pltpu.make_async_copy(s.state(FEED_DONE[j]), state_refs[i], misc_sem.at[1 + i]))
    init = pltpu.make_async_copy(middle, acc, misc_sem.at[0])
    mine = pl.ds(pl.multiple_of(p.x * (length // 2), length // 2), length // 2)
    own = pltpu.make_async_copy(result.at[mine], outputs.at[p.x], misc_sem.at[9])
    outs = [pltpu.make_async_copy(g.at[k, j], (grad_u, grad_d)[k].at[j - 2], misc_sem.at[5 + 2 * (j - 2) + k])
            for j in (2, 3) for k in range(2)]

    def loads(s):
        j, t = (s // 2, s % 2) if isinstance(s, int) else (lax.div(s, 2), lax.rem(s, 2))
        slot = t
        cols = pl.ds(j * n if isinstance(s, int) else pl.multiple_of(j * n, n), n)
        return [pltpu.make_async_copy(w.at[t, :, :, :, :, cols], tiles.at[k, slot], tile_sem.at[k, slot])
                for k, w in ((0, whole_u), (1, whole_d))]

    @pl.when(step == 0)
    def _():
        meet(p)
        start(*loads(0))
        start(*loads(1))
        init.start()
        follow(chains, FEED_PLANS[0])
        second_t[...] = second[...].T
        cot_t[...] = cot[...].T
        grad_second[...] = jnp.zeros_like(grad_second)

    at_steps(step, chains, ((),) + FEED_PLANS[2::2])
    for s in range(2, 8):
        here = first_after(FEED_PLANS, f"U{s // 2}"), first_after(FEED_PLANS, f"D{s // 2}")
        on(step, {max(s - 1, (max(here) + 1) // 2): lambda s=s: start(*loads(s))})
    on(step, {7: lambda: start(*outs[:2])})
    wait(*loads(step))

    @pl.when(step == 0)
    def _():
        init.wait()
    slot = lax.rem(step, 2)
    w_up = tiles[0, slot].reshape(-1, n)
    w_down = tiles[1, slot].reshape(-1, n)
    for i in range(length // ROWS):
        at = slice(i * ROWS, (i + 1) * ROWS)
        hidden = nn(second[at], w_up)
        grad_active = nn(cot[at], w_down)
        cumulative, density = gelu_parts(hidden)
        a = (hidden * cumulative).astype(BF16)
        b = (grad_active * (cumulative + hidden * density)).astype(BF16)
        active[at] = a
        grad_hidden[at] = b
        acc[at] += nt(a, w_down)
        grad_second[at] += nt(b, w_up)
    at_steps(step, chains, FEED_PLANS[1::2])
    j, t = lax.div(step, 2), lax.rem(step, 2)
    shape = g.shape[3:]
    g[0, j, t] = nn(second_t[...], grad_hidden[...]).astype(BF16).reshape(shape)
    g[1, j, t] = nn(cot_t[...], active[...]).astype(BF16).reshape(shape)

    @pl.when(step == pl.num_programs(0) - 1)
    def _():
        start(*outs[2:])
        result[...] = acc[...].astype(BF16)
        own.start()
        follow(chains, FEED_END)
        start(*states)
        wait(*states)
        wait(*outs)
        own.wait()


def feed(second, cot, middle, whole_u, whole_d, zs):
    length, width = second.shape
    rows, n = whole_u.shape[4], FF_GROUP
    same = lambda a: jax.ShapeDtypeStruct(a.shape, a.dtype)
    tile = (2, zs, 2, 2, rows, n)
    grads = jax.ShapeDtypeStruct((2,) + tile, BF16)
    square = pltpu.VMEM((length, width), BF16)
    strip = pltpu.VMEM((length, n), BF16)
    scratch = [pltpu.VMEM((length, width), F32), square, square, strip, strip, pltpu.VMEM((2, 2) + tile[1:], BF16),
               pltpu.VMEM((2, 4) + tile, BF16), DMA((2, 2)), DMA((10,)), DMA((10, gather_sems(zs))), DMA((10, gather_sems(zs)))]
    for i in range(4):
        scratch += landing(zs, rows, n, FEED_ORDERS[i])[:FEED_DONE[i // 2]]
    return pl.pallas_call(
        functools.partial(feed_body, zs),
        grid=(8,),
        in_specs=[full(second.shape), full(cot.shape), HBM, HBM, HBM],
        out_specs=[full(second.shape), full(second.shape)] + [HBM] * 9,
        out_shape=[same(second), jax.ShapeDtypeStruct((length, width), F32), grads, grads]
        + [jax.ShapeDtypeStruct(rest_shape(zs, rows, n, o[:FEED_DONE[i // 2] - 1]), BF16) for i, o in enumerate(FEED_ORDERS)]
        + [jax.ShapeDtypeStruct((2, length // 2, width), BF16), same(whole_u), same(whole_d)],
        scratch_shapes=scratch,
        input_output_aliases={3: 9, 4: 10},
        compiler_params=params(1),
        name="feed",
    )(second, cot, middle, whole_u, whole_d)


def attend_back_step(between, gains, go, inv, query, keys, values, q_raw, k_raw, mixed, grad_q, grad_k, grad_v, grad_gains):
    length = query.shape[0]
    lanes = lax.broadcasted_iota(jnp.int32, (1, PAIR), 1)
    first = lanes < HD
    zero = jnp.zeros((), BF16)
    go = go.astype(F32)
    product = go * mixed.astype(F32) * inv
    go_inv = go * inv
    go_t = go_inv.T.astype(BF16)
    go_inv = go_inv.astype(BF16)
    query_t = query.astype(F32).T.astype(BF16)
    heads = []
    for h, mask in ((0, first), (1, ~first)):
        delta = -jnp.sum(jnp.where(mask, product, 0.0), -1, keepdims=True)
        high = delta.astype(BF16)
        low = (delta - high.astype(F32)).astype(BF16)
        spare = (1 - h) * HD
        grad_aug = jnp.where(mask, go_inv, jnp.where(lanes == spare, high, jnp.where(lanes == spare + 1, low, zero)))
        values_aug = jnp.where(mask, values, jnp.where((lanes == spare) | (lanes == spare + 1), jnp.ones((), BF16), zero))
        mine = slice(h * HD, (h + 1) * HD)
        heads.append((jnp.where(mask, keys, zero), grad_aug, values_aug, go_t[mine], query_t[mine]))
    dq = []
    dk = [jnp.zeros((HD, length), F32)] * 2
    dv = [jnp.zeros((HD, length), F32)] * 2
    for i in range(length // Q_TILE):
        if 2 * i == length // Q_TILE:
            between()
        at = slice(i * Q_TILE, (i + 1) * Q_TILE)
        parts = []
        for h, (km, ga, va, gt, qt) in enumerate(heads):
            exponent = jnp.exp(nt(query[at], km))
            grad_scores = (exponent * nt(ga[at], va)).astype(BF16)
            dv[h] = dv[h] + nn(gt[:, at], exponent.astype(BF16))
            dk[h] = dk[h] + nn(qt[:, at], grad_scores)
            parts.append(nn(grad_scores, km))
        dq.append(parts[0] + parts[1])
    dq = jnp.concatenate(dq, axis=0)
    dk = jnp.concatenate(dk, axis=0).T
    dv = jnp.concatenate(dv, axis=0).T
    grad_v[...] = dv.astype(BF16)
    matrix = head_mean_matrix(PAIR)
    hat, factor = head_stats(q_raw.astype(F32), matrix)
    scale = HD ** -0.5
    sum_q = jnp.sum(dq * hat, 0, keepdims=True) * scale
    grad_q[...] = head_back(dq * gains[0:1] * scale, hat, factor, matrix).astype(BF16)
    hat, factor = head_stats(k_raw.astype(F32), matrix)
    sum_k = jnp.sum(dk * hat, 0, keepdims=True)
    grad_k[...] = head_back(dk * gains[1:2], hat, factor, matrix).astype(BF16)
    grad_gains[...] += jnp.concatenate([sum_q, sum_k], axis=0)


def backward_body(
    zs, rows_steps, norms, gains, cot, grad_second, middle, mixed_rows, w, qn, kn, v, q_raw, k_raw, mixed, inverse,
    grads_u, grads_d, state_0, state_1, state_2, state_3, result, _outputs,
    grad_middle, grad_q, grad_k, grad_v, grad_gains, sums, shard_u, shard_d, shard_o, outputs,
    grad_mixed, acc, g_o, own_late, load_sem, swap_sem, send, recv, *landings,
):
    step = pl.program_id(0)
    p = Place(zs)
    n = FF_GROUP
    half = w.shape[2]
    at = iter(landings)
    take = lambda count: [next(at) for _ in range(count)]
    chains, loads = {}, []

    def out(k, j):
        return [((shard_u, shard_d)[k].at[:, pl.ds(j * n, n)], 0, n)]

    for i, state in enumerate((state_0, state_1, state_2, state_3)):
        j, k = divmod(i, 2)
        order = FEED_ORDERS[i]
        own = next(at)

        def held(x, z, y, own=own, gone=order[:FEED_DONE[j] - 1]):
            return own.at[tuple(index for e, index in zip("xzy", (x, z, y)) if e not in gone)]
        skip = FEED_DONE[j]
        chains[f"{'ud'[k]}{j}"] = Scatter(p, order, held, None, [None] * skip + take(4 - skip), send.at[i], recv.at[i], out(k, j))
        loads.append(pltpu.make_async_copy(state, own, load_sem.at[i]))
    for i in range(4):
        j, k = divmod(i, 2)
        grad = (grads_u, grads_d)[k].at[j]
        chains[f"{'ud'[k]}{2 + j}"] = Scatter(
            p, LATE_ORDERS[i], lambda x, z, y, i=i: own_late.at[i, x, z, y], grad.at[:, :, :, 1 - p.c], take(4),
            send.at[4 + i], recv.at[4 + i], out(k, 2 + j))
        loads.append(pltpu.make_async_copy(grad.at[:, :, :, p.c], own_late.at[i], load_sem.at[4 + i]))
    chains["o"] = Scatter(p, O_BACK_ORDER, lambda x, z, y: g_o.at[x, z, y, p.c], g_o.at[:, :, :, 1 - p.c], take(4),
                          send.at[8], recv.at[8], [(shard_o, 0, half)])
    half_length = result.shape[0] // 2
    chains["R"] = Swap(p, half_rows(result, 1 - p.x, half_length), outputs.at[p.x], swap_sem)

    @pl.when(step == 0)
    def _():
        start(*loads)
        meet(p)
        wait(*loads)
        follow(chains, BACKWARD_PLANS[0])

    at_steps(step, chains, ((),) + BACKWARD_PLANS[1:rows_steps] + BACKWARD_PLANS[rows_steps::2])

    def between():
        at_steps(step, chains, ((),) * rows_steps + BACKWARD_PLANS[rows_steps + 1::2])

    @pl.when(step == 0)
    def _():
        sums[...] = jnp.zeros_like(sums)
        acc[...] = jnp.zeros_like(acc)
        grad_gains[...] = jnp.zeros_like(grad_gains)

    @pl.when(step < rows_steps)
    def _():
        hat, factor = stats(middle[...])
        gs = grad_second[...]
        gm = cot[...].astype(F32) + back(gs * norms[1:2], hat, factor)
        grad_middle[...] = gm
        branch_grad = gm.astype(BF16)
        branch_t = branch_grad.T
        here = pl.ds(pl.multiple_of(step * ROWS, ROWS), ROWS)
        for t in range(2):
            cols = slice(t * half, (t + 1) * half)
            grad_mixed[here, cols] = nn(branch_grad, w[t]).astype(BF16)
            acc[t] += nn(branch_t, mixed_rows[:, cols])
        sums[0:1] += jnp.sum(gs * hat, 0, keepdims=True)
        sums[1:2] += jnp.sum(gs, 0, keepdims=True)

    @pl.when(step == rows_steps - 1)
    def _():
        g_o[...] = acc[...].astype(BF16).reshape(g_o.shape)

    @pl.when(step >= rows_steps)
    def _():
        cols = pl.ds(pl.multiple_of((step - rows_steps) * PAIR, PAIR), PAIR)
        attend_back_step(between, gains, grad_mixed[:, cols], inverse[...], qn[...], kn[...], v[...], q_raw[...], k_raw[...], mixed[...],
                         grad_q, grad_k, grad_v, grad_gains)

    @pl.when(step == pl.num_programs(0) - 1)
    def _():
        follow(chains, BACKWARD_END)


def backward(norms, gains, cot, grad_second, middle, mixed, w, kept, inverse, grads_u, grads_d, states, result, outputs, zs):
    length, width = middle.shape
    half = w.shape[2]
    rows, n = grads_u.shape[5], FF_GROUP
    row_steps, pairs = length // ROWS, 2 * half // PAIR
    row = clipped((ROWS, width), 0, 0, row_steps)
    head = clipped((length, PAIR), 1, row_steps, pairs)
    heads = jax.ShapeDtypeStruct((length, 2 * half), BF16)
    f32 = lambda *shape: jax.ShapeDtypeStruct(shape, F32)
    scratch = [
        pltpu.VMEM((length, 2 * half), BF16), pltpu.VMEM(w.shape, F32), pltpu.VMEM((2, zs, 2, 2, rows, half), BF16),
        pltpu.VMEM((4, 2, zs, 2, rows, n), BF16), DMA((8,)), DMA((2, CHUNKS)),
        DMA((9, scatter_sems(zs))), DMA((9, scatter_sems(zs))),
    ]
    for i in range(4):
        skip = FEED_DONE[i // 2]
        scratch += [pltpu.VMEM(rest_shape(zs, rows, n, FEED_ORDERS[i][:skip - 1]), BF16)] + landing(zs, rows, n, FEED_ORDERS[i], skip)
    for i in range(4):
        scratch += landing(zs, rows, n, LATE_ORDERS[i])
    scratch += landing(zs, rows, half, O_BACK_ORDER)
    return pl.pallas_call(
        functools.partial(backward_body, zs, row_steps),
        grid=(row_steps + pairs,),
        in_specs=[full(norms.shape), full(gains.shape), row, row, row, row, full(w.shape)] + [head] * 7 + [HBM] * 8,
        out_specs=[row, head, head, head, full((2, PAIR)), full((2, width)), full((rows, 4 * n)), full((rows, 4 * n)),
                   full((rows, half)), HBM],
        out_shape=[f32(length, width), heads, heads, heads, f32(2, PAIR), f32(2, width), f32(rows, 4 * n), f32(rows, 4 * n),
                   f32(rows, half), jax.ShapeDtypeStruct((2, length // 2, width), BF16)],
        scratch_shapes=scratch,
        input_output_aliases={21: 9},
        compiler_params=params(2),
        name="backward",
    )(norms, gains, cot, grad_second, middle, mixed, w, *kept, mixed, inverse, grads_u, grads_d, *states, result, outputs)


PART_GROUP = 256


def pieces(lo, size):
    out = []
    for part in range(3):
        first, last = max(lo, part * PART_GROUP), min(lo + size, (part + 1) * PART_GROUP)
        if first < last:
            out.append((part, first - lo, last - first))
    return out


def closing_body(
    zs, norms, sums_second, sums_qk, image_in, first_in, grad_middle_in, gq_in, gk_in, gv_in, w_in,
    shard_q, total, grad_tokens,
    image, first, grad_middle, grads, w, first_t, acc, grad_image, g, load_sem, swap_sem, got, sum_send, sum_recv, send, recv, *landings,
):
    p = Place(zs)
    meet(p)
    length, width = image.shape
    half = grads.shape[2] // 2
    load_grads = [pltpu.make_async_copy(a, grads.at[i], load_sem.at[i]) for i, a in enumerate((gq_in, gk_in, gv_in))]
    load_first = pltpu.make_async_copy(first_in, first, load_sem.at[3])
    load_w = pltpu.make_async_copy(w_in, w, load_sem.at[4])
    load_image = pltpu.make_async_copy(image_in, image, load_sem.at[5])
    load_middle = pltpu.make_async_copy(grad_middle_in, grad_middle, load_sem.at[6])
    start(load_first, *load_grads, load_w, load_image, load_middle)
    chains = {}
    at = iter(landings)
    for i, (k, lo, m, order) in enumerate(CLOSING):
        cols = pl.ds(lo, m)
        held = lambda x, z, y, k=k, cols=cols: g.at[k, x, z, y, p.c, :, cols]
        chains[i] = Scatter(p, order, held, g.at[k, :, :, :, 1 - p.c, :, cols], [next(at) for _ in range(4)], send.at[i], recv.at[i],
                            [(shard_q.at[part, :, pl.ds(k * PART_GROUP + max(lo - part * PART_GROUP, 0), n)], at0, n)
                             for part, at0, n in pieces(lo, m)])
    half_length = length // 2
    chains["G"] = Swap(p, half_rows(grad_image, 1 - p.x, half_length), grad_tokens.at[p.x], swap_sem)
    chains["S"] = Sum(p, total, got, sum_send, sum_recv)
    own = pltpu.make_async_copy(half_rows(grad_image, p.x, half_length), grad_tokens.at[p.x], load_sem.at[7])

    load_first.wait()
    first_t[...] = first[...].T
    wait(*load_grads)

    def weight_grad(k):
        def one(i, _):
            t, part = lax.div(i, 3), lax.rem(i, 3)
            cols = pl.ds(pl.multiple_of(t * half + k * PART_GROUP, PART_GROUP), PART_GROUP)
            value = nn(first_t[...], grads[part, :, cols]).astype(BF16)
            g[k, t, :, :, :, :, pl.ds(pl.multiple_of(part * PART_GROUP, PART_GROUP), PART_GROUP)] = value.reshape(
                g.shape[2:6] + (PART_GROUP,))
            return 0
        lax.fori_loop(0, 6, one, 0)

    def first_norm_back(which, carry, plan):
        here = pl.ds(pl.multiple_of(which * half_length, half_length), half_length)
        acc[...] = jnp.zeros_like(acc)

        def to_first(i, _):
            t, part = lax.div(i, 3), lax.rem(i, 3)
            cols = pl.ds(pl.multiple_of(t * half, half), half)
            acc[...] += nt(grads[part, here, cols], w[t, :, pl.ds(pl.multiple_of(part * half, half), half)])
            return 0
        lax.fori_loop(0, 6, to_first, 0)
        follow(chains, plan)

        def norm_back(i, carry):
            at = pl.ds(pl.multiple_of(which * half_length + i * ROWS, ROWS), ROWS)
            hat, factor = stats(image[at].astype(F32))
            gf = acc[pl.ds(pl.multiple_of(i * ROWS, ROWS), ROWS)]
            grad_image[at] = (grad_middle[at] + back(gf * norms[0:1], hat, factor)).astype(BF16)
            return carry[0] + jnp.sum(gf * hat, 0, keepdims=True), carry[1] + jnp.sum(gf, 0, keepdims=True)
        return lax.fori_loop(0, half_length // ROWS, norm_back, carry)

    zero = jnp.zeros((1, width), F32)
    weight_grad(0)
    follow(chains, CLOSING_PLANS[0])
    load_w.wait()
    wait(load_image, load_middle)
    sums = first_norm_back(1 - p.x, (zero, zero), CLOSING_PLANS[1])
    follow(chains, CLOSING_PLANS[2])
    weight_grad(1)
    follow(chains, CLOSING_PLANS[3])
    sum_hat, sum_all = first_norm_back(p.x, sums, CLOSING_PLANS[4])
    own.start()
    total[...] = jnp.zeros_like(total)
    total[0:1] = sum_hat
    total[1:2] = sum_all
    total[2:4] = sums_second[...]
    total[4:6, 0:HD] = sums_qk[:, :HD] + sums_qk[:, HD:]
    follow(chains, CLOSING_END)
    own.wait()


def closing(norms, sums_second, sums_qk, image, first, grad_middle, gq, gk, gv, w, zs):
    length, width = image.shape
    rows = width // (4 * zs)
    wide = 3 * PART_GROUP
    square = pltpu.VMEM((length, width), BF16)
    scratch = [
        square, square, pltpu.VMEM((length, width), F32), pltpu.VMEM((3,) + gq.shape, BF16), pltpu.VMEM(w.shape, BF16), square,
        pltpu.VMEM((length // 2, width), F32), square, pltpu.VMEM((2, 2, zs, 2, 2, rows, wide), BF16), DMA((8,)), DMA((2, CHUNKS)),
        pltpu.VMEM((zs + 2, 8, width), F32), DMA((zs + 2,)), DMA((zs + 2,)),
        DMA((len(CLOSING), scatter_sems(zs))), DMA((len(CLOSING), scatter_sems(zs))),
    ]
    for k, lo, m, order in CLOSING:
        scratch += landing(zs, rows, m, order)
    return pl.pallas_call(
        functools.partial(closing_body, zs),
        in_specs=[WHOLE_VMEM] * 3 + [HBM] * 7,
        out_specs=[WHOLE_VMEM, WHOLE_VMEM, HBM],
        out_shape=[jax.ShapeDtypeStruct((3, rows, gq.shape[1] // 2), F32), jax.ShapeDtypeStruct((8, width), F32),
                   jax.ShapeDtypeStruct((2, length // 2, width), BF16)],
        scratch_shapes=scratch,
        compiler_params=params(3),
        name="closing",
    )(norms, sums_second, sums_qk, image, first, grad_middle, gq, gk, gv, w)


def whole_images(tokens, cotangent, w_qkv, wo_t, w_up, w_down_t, norm_gains, norm_shifts, qk_gains):
    zs = lax.axis_size("fsdp") // 4
    rows = w_qkv.shape[0]
    width = tokens.shape[2]
    half = w_qkv.shape[2]
    cols = 3 * half
    first, qn, kn, v, q_raw, k_raw, mixed, inverse, middle, second, norms, image, cot, whole_q, whole_o, whole_u, whole_d = attention(
        qk_gains, norm_gains.T, norm_shifts.T, w_qkv.transpose(1, 0, 2), wo_t, w_up, w_down_t, tokens, cotangent, zs
    )
    result, grad_second, grads_u, grads_d, *states, outputs, whole_u, whole_d = feed(
        second, cot, middle, whole_u, whole_d, zs
    )
    qkv = whole_q.reshape(2, width, cols + 128)
    grad_middle, gq, gk, gv, sums_qk, sums_second, shard_u, shard_d, shard_o, outputs = backward(
        norms, jnp.tile(qk_gains.astype(F32), (1, 2)), cot, grad_second, middle, mixed, whole_o.reshape(2, width, half),
        (qn, kn, v, q_raw, k_raw), inverse, grads_u, grads_d, states, result, outputs, zs
    )
    grad_q, small, grad_tokens = closing(norms, sums_second, sums_qk, image, first, grad_middle, gq, gk, gv, qkv, zs)
    mine = lax.dynamic_slice_in_dim(small, lax.axis_index("fsdp") * rows, rows, 1)
    return (
        outputs,
        grad_tokens.astype(F32),
        grad_q.transpose(1, 0, 2),
        shard_o,
        shard_u,
        shard_d,
        jnp.stack([mine[0], mine[2]], 1),
        jnp.stack([mine[1], mine[3]], 1),
        small[4:6, :HD],
    )


def layer(tokens, *rest):
    if tokens.shape[0] == lax.axis_size("tensor") == 2 and lax.axis_size("fsdp") % 4 == 0:
        return whole_images(tokens, *rest)
    return per_device(tokens, *rest)


def solution(mesh):
    in_specs = (
        P("fsdp", "tensor", None),
        P("fsdp", "tensor", None),
        P("fsdp", None, "tensor"),
        P("fsdp", "tensor"),
        P("fsdp", "tensor"),
        P("fsdp", "tensor"),
        P("fsdp", None),
        P("fsdp", None),
        P(),
    )
    out_specs = (
        P("fsdp", "tensor", None),
        P("fsdp", "tensor", None),
        P("fsdp", None, "tensor"),
        P("fsdp", "tensor"),
        P("fsdp", "tensor"),
        P("fsdp", "tensor"),
        P("fsdp", None),
        P("fsdp", None),
        P(),
    )
    return jax.shard_map(
        layer, mesh=mesh, in_specs=in_specs, out_specs=out_specs, check_vma=False
    )
```
